32 devices in a mesh: group: 2 (over x), fsdp: 8 (over z, y), ctx: 2 (over core).
Axes of the slice: x: 2, y: 2, z: 4, core: 2. Of those that a mesh axis runs over, the one named last changes fastest.
Arguments:
- normed: bfloat16 [16, 512, 8192], P(('group', 'fsdp'), 'ctx'), parts along dimension 0, may hold values from -6 to 6
- queries: bfloat16 [16, 512, 4096], P(('group', 'fsdp'), 'ctx'), parts along dimension 0, may hold values from -103 to 103
- key_weight: bfloat16 [8192, 512], P('fsdp'), may hold values from -0.0625 to 0.0625
- value_weight: bfloat16 [8192, 512], P('fsdp'), may hold values from -0.0625 to 0.0625
- doc_start: int32 [16], P(('group', 'fsdp')), parts along dimension 0, may hold values from 1 to 511
Outputs:
- attention: bfloat16 [16, 512, 4096], P(('group', 'fsdp'), 'ctx'), parts along dimension 0
The draws below stay inside these ranges and needn't reach their ends.
There are 2 independent parts, one for each index of `group`. The reference program is written for one: setup_inputs(seed, part) draws one part's arguments, and reference() takes and returns one part's arrays. A program takes and returns all parts, laid end to end along the dimension named above; an argument that names none is the same for every part. Nothing has to cross between parts.
Inputs may be any that keep to these rules, and one draw needn't show every extreme that they name: Rows before doc_start of a window belong to one document and the other rows to the next.
All inputs are finite; a program needn't handle non-finite values.
Results may differ from the reference program's by a relative error of at most 0.0055.
The reference program's roundings to bfloat16 on the way count: a program that leaves them out, or rounds other values in their place, can miss the bound.
Values may be sent and summed in bfloat16 or wider, within the bound.
A program may use at most 128 MiB of HBM per device.

```python
import jax
import jax.numpy as jnp
from jax import lax

D = 8192
HEAD_DIM = 128
GROUP = 8
KV_HEADS = 4
HEADS = 32
KVW = 512
QW = 4096
LENGTH = 512
WINDOWS = 8


def draw_queries(key, part):
    draw_shape = (WINDOWS, LENGTH, QW)
    values = jnp.clip(jax.random.normal(key, draw_shape, jnp.float32), -6.0, 6.0)
    return values.astype(jnp.bfloat16)


def touch_ends(result, key, low, largest):
    longest = result.shape.index(max(result.shape))
    spots = []
    for shift in (0, 1):
        where = [jax.random.randint(jax.random.fold_in(key, axis), (), 0, length) for axis, length in enumerate(result.shape)]
        where[longest] = (where[longest] + shift) % result.shape[longest]
        spots.append(tuple(where))
    return result.at[spots[0]].set(low).at[spots[1]].set(largest)


def block_scale(stream_key, extent, split, least, high):
    gain = 1.0
    for axis_at, shards_of in split:
        heights = jax.random.uniform(jax.random.fold_in(jax.random.fold_in(stream_key, 6), axis_at), (shards_of,), jnp.float32, least / len(split), high / len(split))
        gain = gain * jnp.repeat(jnp.exp(heights), extent[axis_at] // shards_of).reshape((-1,) + (1,) * (len(extent) - 1 - axis_at))
    return gain


def centred(own_key, dims, scale, limit, pieces=(), kind=jnp.bfloat16):
    array = jax.random.normal(own_key, dims, jnp.float32) * scale
    if len(pieces) > 0:
        array = block_scale(own_key, dims, pieces, -0.22, 0.18) * array
    return jnp.clip(array, min=-limit, max=limit).astype(kind)


def setup_inputs(seed: int = 0, part: int = 0) -> dict:
    seeds = jax.random.split(jax.random.key(seed), 6)
    part_splits = jax.random.split(jax.random.fold_in(seeds[5], part), 6)
    normed = centred(part_splits[0], (WINDOWS, LENGTH, D), 1.0, 6.0, ((0, 8), (1, 2)))
    queries = draw_queries(jax.random.fold_in(jax.random.fold_in(seeds[5], part), 71), part)
    key_weight = centred(seeds[2], (D, KVW), D ** -0.5, 0.0625, ((0, 8),))
    value_weight = centred(seeds[3], (D, KVW), D ** -0.5, 0.0625, ((0, 8),))
    doc_start = touch_ends(jax.random.randint(part_splits[4], (WINDOWS,), 1, LENGTH), jax.random.fold_in(part_splits[4], 1), 1, LENGTH - 1).astype(jnp.int32)
    return {"normed": normed, "queries": queries, "key_weight": key_weight, "value_weight": value_weight, "doc_start": doc_start}


theta_base = 500000.0
masked_score = -1.0e30


def rotate(values, positions):
    head_width = values.shape[-1]
    half_width = head_width // 2
    frequency = theta_base ** (-jnp.arange(half_width, dtype=jnp.float32) * 2.0 / head_width)
    angles = positions.astype(jnp.float32)[:, None] * frequency[None, :]
    cosine = jnp.cos(angles)[:, None, :]
    sine_part = jnp.sin(angles)[:, None, :]
    first_half = values[..., :half_width]
    second_half = values[..., half_width:]
    return jnp.concatenate([first_half * cosine - second_half * sine_part, second_half * cosine + first_half * sine_part], axis=-1)


def reference(normed, queries, key_weight, value_weight, doc_start):
    windows, length, model_width = normed.shape
    flattened = normed.reshape(windows * length, model_width)
    positions = jnp.arange(length, dtype=jnp.int32)
    key_proj = jnp.dot(flattened, key_weight, preferred_element_type=jnp.float32)
    value_proj = jnp.dot(flattened, value_weight, preferred_element_type=jnp.float32)
    key_heads = rotate(key_proj.reshape(windows, length, KV_HEADS, HEAD_DIM), positions).astype(jnp.bfloat16)
    value_heads = value_proj.astype(jnp.bfloat16).reshape(windows, length, KV_HEADS, HEAD_DIM)
    query_heads = rotate(queries.astype(jnp.float32).reshape(windows, length, HEADS, HEAD_DIM), positions)
    query_heads = query_heads.astype(jnp.bfloat16).reshape(windows, length, KV_HEADS, GROUP, HEAD_DIM)

    def one_window(operands):
        query_block, key_block, value_block, doc_bound = operands
        scores = jnp.einsum("rkgd,skd->kgrs", query_block.astype(jnp.float32), key_block.astype(jnp.float32)) * HEAD_DIM ** -0.5
        before_query = positions[None, :] <= positions[:, None]
        same_document = (positions[None, :] >= doc_bound) | (positions[:, None] < doc_bound)
        visible = before_query & same_document
        scores = jnp.where(visible, scores, masked_score)
        row_max = jnp.max(scores, axis=-1, keepdims=True)
        weights = jnp.where(visible, jnp.exp(scores - row_max), 0.0)
        denominator = jnp.sum(weights, axis=-1)
        context = jnp.einsum("kgrs,skd->rkgd", weights.astype(jnp.bfloat16).astype(jnp.float32), value_block.astype(jnp.float32))
        context = context / jnp.transpose(denominator, (2, 0, 1))[..., None]
        return context.astype(jnp.bfloat16).reshape(length, HEADS * HEAD_DIM)

    return lax.map(one_window, (query_heads, key_heads, value_heads, doc_start))
```

```python
import functools

import jax
import jax.numpy as jnp
import numpy as np
from jax import lax
from jax.experimental import pallas as pl
from jax.experimental.pallas import tpu as pltpu
from jax.sharding import PartitionSpec as P

HEAD_DIM = 128
GROUP = 8
THETA = 500000.0
MASKED = -1e30
MESH = pl.DeviceIdType.MESH
PHASES = 2
OUT_GROUPS = 4
PARTS = 8
WAIT = 4
SCHEDULE = (
    ("load", (0,), (), ()),
    ("begin", (), ((0, 0, 0, 0, 0), (2, 0, 0, 0, 0), (0, 0, 0, 0, 1), (2, 0, 0, 0, 1), (0, 0, 0, 0, 2), (2, 0, 0, 0, 2)), ((0, 0, 0, 0, 0), (1, 0, 0, 0, 0), (2, 0, 0, 0, 0), (0, 0, 0, 0, 1), (1, 0, 0, 0, 1), (2, 0, 0, 0, 1), (0, 0, 0, 0, 2), (1, 0, 0, 0, 2), (2, 0, 0, 0, 2))),
    ("load", (1,), (), ()),
    ("clear", (), (), ()),
    ("queries", (), ((0, 0, 0, 0, 3), (0, 0, 0, 0, 4), (4, 0, 0, 1, 0), (3, 0, 0, 1, 0), (4, 0, 1, 0, 0), (2, 0, 1, 0, 0), (3, 0, 1, 0, 0)), ((0, 0, 0, 0, 3), (1, 0, 0, 0, 3), (4, 0, 1, 0, 0), (3, 0, 1, 0, 0), (2, 0, 1, 0, 0), (4, 0, 0, 1, 0), (3, 0, 0, 1, 0), (0, 0, 1, 0, 0), (4, 0, 2, 0, 0), (1, 0, 2, 0, 0), (2, 0, 2, 0, 0), (3, 0, 2, 0, 0))),
    ("rotate", (0, 2), (), ()),
    ("rotate", (2, 2), ((0, 0, 0, 0, 5),), ()),
    ("rotate", (4, 2), ((4, 0, 1, 0, 1), (2, 0, 1, 0, 1), (3, 0, 1, 0, 1), (0, 1, 0, 0, 0)), ((4, 0, 1, 0, 1), (0, 0, 1, 0, 1), (4, 0, 2, 0, 1), (1, 0, 2, 0, 1), (2, 0, 1, 0, 1), (2, 0, 2, 0, 1))),
    ("rotate", (6, 2), ((4, 0, 1, 0, 2), (2, 0, 1, 0, 2)), ((4, 0, 1, 0, 2), (0, 0, 1, 0, 2), (4, 0, 2, 0, 2), (1, 0, 2, 0, 2))),
    ("rotate", (8, 2), ((0, 1, 0, 0, 1), (4, 0, 1, 1, 0), (3, 0, 1, 1, 0), (4, 0, 1, 0, 3), (2, 0, 1, 0, 3)), ((4, 0, 1, 1, 0), (3, 0, 1, 1, 0), (4, 0, 1, 0, 3), (0, 0, 1, 0, 3), (4, 0, 2, 0, 3), (1, 0, 2, 0, 3))),
    ("rotate", (10, 2), ((0, 1, 0, 0, 2),), ((0, 0, 0, 0, 4),)),
    ("rotate", (12, 2), ((4, 0, 2, 0, 0), (3, 0, 2, 0, 0), (2, 0, 2, 0, 0), (4, 0, 1, 1, 1), (3, 0, 1, 1, 1)), ((3, 0, 1, 0, 1), (4, 0, 2, 1, 0), (3, 0, 2, 1, 0), (4, 0, 3, 0, 0), (2, 0, 3, 0, 0), (3, 0, 3, 0, 0), (1, 0, 3, 0, 0))),
    ("rotate", (14, 2), ((0, 1, 0, 0, 3), (4, 0, 2, 0, 1), (2, 0, 2, 0, 1), (3, 0, 2, 0, 1)), ((0, 0, 0, 0, 5), (2, 0, 1, 0, 2), (4, 0, 3, 0, 1), (2, 0, 3, 0, 1), (1, 0, 3, 0, 1))),
    ("normed", (), ((0, 1, 0, 0, 4), (4, 0, 2, 0, 2), (2, 0, 2, 0, 2), (0, 1, 0, 0, 5), (4, 0, 2, 1, 0), (3, 0, 2, 1, 0), (4, 0, 2, 0, 3), (2, 0, 2, 0, 3)), ((4, 0, 1, 0, 4), (0, 0, 1, 0, 4), (2, 0, 2, 0, 2), (3, 0, 2, 0, 1), (4, 0, 3, 0, 2), (1, 0, 3, 0, 2), (4, 0, 1, 0, 5), (0, 0, 1, 0, 5), (2, 0, 3, 0, 2), (4, 0, 1, 1, 1), (3, 0, 1, 1, 1), (4, 0, 3, 1, 0), (3, 0, 3, 1, 0), (4, 0, 3, 0, 3), (1, 0, 3, 0, 3))),
    ("add", (0, 0, 0), (), ()),
    ("add", (1, 0, 0), ((0, 1, 0, 0, 6),), ((0, 1, 0, 0, 0), (1, 0, 0, 0, 4), (2, 0, 1, 0, 3))),
    ("add", (0, 1, 0), ((4, 0, 3, 0, 0), (3, 0, 3, 0, 0), (2, 0, 3, 0, 0), (4, 0, 2, 1, 1), (3, 0, 2, 1, 1), (4, 0, 3, 0, 1), (2, 0, 3, 0, 1), (3, 0, 3, 0, 1), (4, 0, 3, 0, 2), (2, 0, 3, 0, 2), (2, 0, 0, 0, 3), (4, 0, 1, 1, 2), (3, 0, 1, 1, 2), (4, 0, 3, 1, 0), (3, 0, 3, 1, 0), (4, 0, 3, 0, 3), (2, 0, 3, 0, 3), (2, 0, 0, 0, 4), (4, 0, 2, 1, 2), (3, 0, 2, 1, 2), (4, 0, 3, 1, 1), (3, 0, 3, 1, 1), (2, 0, 0, 0, 5), (4, 0, 3, 1, 2), (3, 0, 3, 1, 2), (4, 0, 1, 0, 7), (4, 0, 1, 0, 6), (4, 0, 1, 0, 4), (4, 0, 1, 0, 5)), ((3, 0, 3, 0, 1), (0, 1, 0, 0, 1), (1, 0, 0, 0, 5), (2, 0, 2, 0, 3), (4, 0, 2, 1, 1), (3, 0, 2, 1, 1), (0, 1, 0, 0, 2), (4, 0, 2, 0, 4), (1, 0, 2, 0, 4), (2, 0, 3, 0, 3), (4, 0, 3, 1, 1), (3, 0, 3, 1, 1), (0, 1, 0, 0, 3), (4, 0, 2, 0, 5), (1, 0, 2, 0, 5), (2, 0, 0, 0, 3), (4, 0, 1, 1, 2), (3, 0, 1, 1, 2), (4, 1, 1, 0, 0), (0, 1, 1, 0, 0), (4, 0, 3, 0, 4), (1, 0, 3, 0, 4), (2, 0, 0, 0, 4), (4, 0, 2, 1, 2), (3, 0, 2, 1, 2), (4, 1, 1, 0, 1), (0, 1, 1, 0, 1), (4, 0, 3, 0, 5), (1, 0, 3, 0, 5), (2, 0, 0, 0, 5), (4, 0, 3, 1, 2), (3, 0, 3, 1, 2), (4, 0, 1, 0, 7), (4, 0, 1, 0, 6))),
    ("add", (0, 2, 0), ((2, 0, 0, 0, 6), (4, 0, 1, 1, 3), (3, 0, 1, 1, 3), (2, 1, 0, 0, 0), (4, 0, 2, 1, 3), (3, 0, 2, 1, 3), (4, 0, 2, 0, 7), (4, 0, 2, 0, 6), (4, 0, 2, 0, 4), (4, 0, 2, 0, 5)), ((4, 1, 1, 0, 2), (0, 1, 1, 0, 2), (1, 1, 0, 0, 0), (2, 0, 0, 0, 6), (4, 0, 1, 1, 3), (3, 0, 1, 1, 3), (4, 1, 1, 0, 3), (0, 1, 1, 0, 3), (1, 1, 0, 0, 1), (2, 1, 1, 0, 0), (4, 0, 2, 1, 3), (3, 0, 2, 1, 3), (4, 0, 2, 0, 7), (4, 0, 2, 0, 6))),
    ("add", (0, 3, 0), ((2, 1, 0, 0, 1), (4, 0, 3, 1, 3), (3, 0, 3, 1, 3), (4, 0, 3, 0, 7), (4, 0, 3, 0, 6), (4, 0, 3, 0, 4), (4, 0, 3, 0, 5)), ((0, 1, 0, 0, 4), (1, 1, 0, 0, 2), (4, 1, 2, 0, 0), (2, 1, 2, 0, 0), (4, 0, 3, 1, 3), (3, 0, 3, 1, 3), (0, 1, 0, 0, 5), (1, 1, 0, 0, 3), (4, 1, 3, 0, 0), (2, 1, 3, 0, 0), (3, 1, 1, 0, 0), (4, 0, 3, 0, 7), (4, 0, 3, 0, 6))),
    ("add", (0, 0, 1), ((4, 1, 1, 0, 0), (2, 1, 1, 0, 0), (3, 1, 1, 0, 0), (4, 0, 0, 1, 1), (4, 0, 0, 1, 2), (4, 0, 0, 1, 7), (4, 0, 0, 1, 3), (4, 0, 0, 1, 4), (4, 0, 0, 1, 5), (4, 0, 0, 1, 6)), ((0, 1, 0, 0, 6), (1, 1, 2, 0, 0), (2, 1, 1, 0, 1), (3, 1, 2, 0, 0), (4, 0, 0, 1, 1), (4, 0, 0, 1, 2), (4, 0, 0, 1, 7), (4, 0, 0, 1, 3), (4, 0, 0, 1, 4), (4, 0, 0, 1, 5), (4, 0, 0, 1, 6))),
    ("add", (0, 1, 1), ((4, 0, 1, 1, 7), (4, 0, 1, 1, 6), (4, 0, 1, 1, 5), (4, 0, 1, 1, 4)), ((4, 1, 1, 0, 4), (0, 1, 1, 0, 4), (4, 1, 2, 0, 1), (1, 1, 2, 0, 1), (2, 1, 2, 0, 1), (4, 0, 1, 1, 7), (4, 0, 1, 1, 6), (4, 0, 1, 1, 5), (4, 0, 1, 1, 4))),
    ("add", (0, 2, 1), ((4, 1, 1, 0, 1), (2, 1, 1, 0, 1), (4, 1, 0, 1, 0), (3, 1, 0, 1, 0), (4, 0, 2, 1, 7), (4, 0, 2, 1, 6), (4, 0, 2, 1, 5), (4, 0, 2, 1, 4)), ((3, 1, 3, 0, 0), (4, 1, 1, 0, 5), (0, 1, 1, 0, 5), (4, 1, 2, 0, 2), (1, 1, 2, 0, 2), (4, 1, 3, 0, 1), (2, 1, 3, 0, 1), (4, 0, 2, 1, 7), (4, 0, 2, 1, 6), (4, 0, 2, 1, 5), (4, 0, 2, 1, 4))),
    ("add", (0, 3, 1), ((4, 1, 1, 0, 2), (2, 1, 1, 0, 2), (4, 0, 3, 1, 7), (4, 0, 3, 1, 6), (4, 0, 3, 1, 5), (4, 0, 3, 1, 4)), ((4, 1, 1, 1, 0), (3, 1, 1, 1, 0), (4, 1, 1, 0, 6), (0, 1, 1, 0, 6), (4, 1, 2, 0, 3), (1, 1, 2, 0, 3), (2, 1, 1, 0, 2), (4, 0, 3, 1, 7), (4, 0, 3, 1, 6), (4, 0, 3, 1, 5), (4, 0, 3, 1, 4))),
    ("keys", (), ((4, 1, 1, 1, 0), (3, 1, 1, 1, 0), (4, 1, 1, 0, 3), (2, 1, 1, 0, 3)), ((4, 1, 2, 1, 0), (3, 1, 2, 1, 0))),
    ("weigh", (0, 2), (), ((1, 1, 3, 0, 0), (2, 1, 2, 0, 2))),
    ("weigh", (2, 2), ((4, 1, 2, 0, 0), (3, 1, 2, 0, 0), (2, 1, 2, 0, 0), (4, 1, 1, 1, 1), (3, 1, 1, 1, 1)), ((4, 1, 3, 1, 0), (3, 1, 3, 1, 0), (1, 1, 3, 0, 1), (4, 1, 3, 0, 2), (2, 1, 3, 0, 2))),
    ("weigh", (4, 2), ((4, 1, 2, 0, 1), (2, 1, 2, 0, 1), (4, 1, 1, 1, 2), (3, 1, 1, 1, 2)), ((4, 1, 1, 1, 1), (3, 1, 1, 1, 1))),
    ("weigh", (6, 2), (), ((1, 1, 3, 0, 2), (2, 1, 1, 0, 3), (4, 1, 2, 1, 1), (3, 1, 2, 1, 1))),
    ("weigh", (8, 2), ((4, 1, 2, 0, 2), (2, 1, 2, 0, 2)), ((4, 1, 3, 0, 3), (1, 1, 3, 0, 3), (2, 1, 2, 0, 3))),
    ("weigh", (10, 2), ((4, 1, 2, 1, 0), (3, 1, 2, 1, 0), (4, 1, 2, 0, 3), (2, 1, 2, 0, 3)), ((4, 1, 3, 1, 1), (3, 1, 3, 1, 1))),
    ("weigh", (12, 2), ((4, 1, 3, 0, 0), (3, 1, 3, 0, 0), (2, 1, 3, 0, 0), (4, 1, 2, 1, 1), (3, 1, 2, 1, 1)), ((1, 1, 0, 0, 4), (2, 1, 3, 0, 3), (4, 1, 1, 1, 2), (3, 1, 1, 1, 2))),
    ("weigh", (14, 2), (), ((1, 1, 0, 0, 5), (2, 1, 0, 0, 0))),
    ("add", (1, 1, 0), ((4, 1, 3, 0, 1), (2, 1, 3, 0, 1), (4, 1, 2, 1, 2), (3, 1, 2, 1, 2), (4, 1, 3, 0, 2), (2, 1, 3, 0, 2), (2, 1, 0, 0, 2), (4, 1, 3, 1, 0), (3, 1, 3, 1, 0), (4, 1, 3, 0, 3), (2, 1, 3, 0, 3), (2, 1, 0, 0, 3), (4, 1, 1, 1, 3), (3, 1, 1, 1, 3), (4, 1, 3, 1, 1), (3, 1, 3, 1, 1), (2, 1, 0, 0, 4), (4, 1, 2, 1, 3), (3, 1, 2, 1, 3), (4, 1, 3, 1, 2), (3, 1, 3, 1, 2), (2, 1, 0, 0, 5), (4, 1, 3, 1, 3), (3, 1, 3, 1, 3), (4, 1, 1, 0, 7), (4, 1, 1, 0, 4), (4, 1, 1, 0, 5), (4, 1, 1, 0, 6)), ((4, 1, 2, 1, 2), (3, 1, 2, 1, 2), (1, 1, 0, 0, 6), (2, 1, 0, 0, 1), (4, 1, 3, 1, 2), (3, 1, 3, 1, 2), (4, 1, 2, 0, 4), (1, 1, 2, 0, 4), (2, 1, 0, 0, 2), (4, 1, 2, 0, 5), (1, 1, 2, 0, 5), (2, 1, 0, 0, 3), (4, 1, 1, 1, 3), (3, 1, 1, 1, 3), (4, 1, 2, 0, 6), (1, 1, 2, 0, 6), (2, 1, 0, 0, 4), (4, 1, 2, 1, 3), (3, 1, 2, 1, 3), (4, 1, 0, 1, 0), (3, 1, 0, 1, 0), (4, 1, 3, 0, 4), (1, 1, 3, 0, 4), (2, 1, 0, 0, 5), (4, 1, 3, 1, 3), (3, 1, 3, 1, 3), (4, 1, 1, 0, 7))),
    ("add", (1, 1, 1), ((2, 1, 0, 0, 6), (4, 1, 1, 1, 7), (4, 1, 1, 1, 6), (4, 1, 1, 1, 5), (4, 1, 1, 1, 4)), ((4, 1, 3, 0, 5), (1, 1, 3, 0, 5), (2, 1, 0, 0, 6), (4, 1, 3, 0, 6), (1, 1, 3, 0, 6), (4, 1, 1, 1, 7), (4, 1, 1, 1, 6), (4, 1, 1, 1, 5), (4, 1, 1, 1, 4))),
    ("add", (1, 2, 0), ((4, 1, 2, 0, 7), (4, 1, 2, 0, 4), (4, 1, 2, 0, 5), (4, 1, 2, 0, 6)), ((4, 1, 2, 0, 7),)),
    ("add", (1, 2, 1), ((4, 1, 2, 1, 7), (4, 1, 2, 1, 6), (4, 1, 2, 1, 5), (4, 1, 2, 1, 4)), ((4, 1, 2, 1, 7), (4, 1, 2, 1, 6), (4, 1, 2, 1, 5), (4, 1, 2, 1, 4))),
    ("add", (1, 3, 1), ((4, 1, 3, 1, 7), (4, 1, 3, 1, 6), (4, 1, 3, 1, 5), (4, 1, 3, 1, 4)), ((4, 1, 3, 1, 7), (4, 1, 3, 1, 6), (4, 1, 3, 1, 5), (4, 1, 3, 1, 4))),
    ("add", (1, 0, 1), ((4, 1, 0, 1, 1), (4, 1, 0, 1, 7), (4, 1, 0, 1, 2), (4, 1, 0, 1, 3), (4, 1, 0, 1, 4), (4, 1, 0, 1, 5), (4, 1, 0, 1, 6)), ((4, 1, 0, 1, 1), (4, 1, 0, 1, 2), (4, 1, 0, 1, 7), (4, 1, 0, 1, 3), (4, 1, 0, 1, 4), (4, 1, 0, 1, 5), (4, 1, 0, 1, 6))),
    ("add", (1, 3, 0), ((4, 1, 3, 0, 7), (4, 1, 3, 0, 4), (4, 1, 3, 0, 5), (4, 1, 3, 0, 6)), ((4, 1, 3, 0, 7),)),
    ("", (), (), ()),
)


def paired(groups, shards):
    return groups == 2 and shards == 8


def rotary_tables(length):
    half = HEAD_DIM // 2
    exponent = -np.arange(half, dtype=np.float32) * np.float32(2.0) / np.float32(HEAD_DIM)
    frequency = np.power(np.float32(THETA), exponent, dtype=np.float32)
    angles = np.arange(length, dtype=np.float32)[:, None] * frequency[None, :]
    cosine, sine = np.cos(angles).astype(np.float32), np.sin(angles).astype(np.float32)
    return np.concatenate([cosine, cosine], 1), np.concatenate([-sine, sine], 1)


def kernel(
    groups, shards, doc_ref, normed_ref, queries_ref, key_ref, value_ref, cos_hbm, sin_hbm, out_ref,
    wbuf, xbuf, qbuf, obuf, pbuf, inverse, acc, kbuf, vbuf, bias, cos_ref, sin_ref,
    load_sem, recv_sem, send_sem, pair_send, pair_recv, out_sem, out_send, out_recv,
):
    twins = paired(groups, shards)
    ny = 2 if twins else 1
    nz = shards // ny
    parts = PARTS if twins else 1
    g, f, c = lax.axis_index("group"), lax.axis_index("fsdp"), lax.axis_index("ctx")
    z, y = f // ny, f % ny
    own_rows, depth = normed_ref.shape[1], key_ref.shape[0]
    length = 2 * own_rows
    piece_rows = depth // parts
    half_cols = queries_ref.shape[2] // 2
    pair = (g, f, 1 - c)
    up, down = (g, f + ny, c), (g, f - ny, c)
    if twins:
        y_dev, x_dev = (g, z * 2 + 1 - y, c), (1 - g, f, c)

    def shard(zs, ys):
        return zs * ny + ys

    def part(j):
        return g * (parts - 1) + j * (1 - 2 * g) if twins else 0

    def piece(h, s, q):
        return wbuf.at[h, s, pl.ds(pl.multiple_of(q * piece_rows, piece_rows), piece_rows), :]

    def copy(h, s, q, send_sem, device):
        ref = piece(h, s, q)
        return pltpu.make_async_remote_copy(
            src_ref=ref, dst_ref=ref, send_sem=send_sem, recv_sem=recv_sem.at[h, s, q],
            device_id=device, device_id_type=MESH,
        )

    middle = (z + 1) // 2 % 2
    inward = 1 - 2 * (z // 2)

    def place(k, o):
        zs = z if k == 0 else z + inward * (k - middle * (2 if k == 1 else 1))
        return shard(zs, 1 - y if o else y)

    def wait_piece(h, s, j):
        q = part(j)
        copy(h, s, q, recv_sem.at[h, s, q], pair).wait_recv()

    def send(index, link, h, k, o, j):
        device = (
            (g, f + inward * ny, c) if link == 0 else (g, f - inward * ny, c) if link == 1 else y_dev if link == 2 else x_dev
        )
        return copy(h, place(k, o), part(j), send_sem.at[index], device)

    def z_copy(h, zs, way):
        return copy(h, zs, 0, send_sem.at[(h * nz + zs) * 2 + way], up if way == 0 else down)

    head_cols = pl.ds(pl.multiple_of(c * 2 * HEAD_DIM, 2 * HEAD_DIM), 2 * HEAD_DIM)
    weight_loads = [
        pltpu.make_async_copy(ref.at[:, head_cols], wbuf.at[h, f], load_sem.at[h])
        for h, ref in enumerate((key_ref, value_ref))
    ]
    own = pl.ds(pl.multiple_of(c * own_rows, own_rows), own_rows)
    other = pl.ds(pl.multiple_of((1 - c) * own_rows, own_rows), own_rows)
    my_cols = pl.ds(pl.multiple_of(c * half_cols, half_cols), half_cols)
    other_cols = pl.ds(pl.multiple_of((1 - c) * half_cols, half_cols), half_cols)
    other_loads = [
        pltpu.make_async_copy(normed_ref.at[0], xbuf.at[own, :], load_sem.at[2]),
        pltpu.make_async_copy(queries_ref.at[0, :, my_cols], qbuf.at[own, :], load_sem.at[3]),
        pltpu.make_async_copy(cos_hbm, cos_ref, load_sem.at[4]),
        pltpu.make_async_copy(sin_hbm, sin_ref, load_sem.at[5]),
    ]
    for load in weight_loads:
        load.start()

    barrier = pltpu.get_barrier_semaphore()
    pl.semaphore_signal(barrier, inc=1, device_id=pair, device_id_type=MESH)
    if twins:
        pl.semaphore_signal(barrier, inc=1, device_id=y_dev, device_id_type=MESH)
        pl.semaphore_signal(barrier, inc=1, device_id=x_dev, device_id_type=MESH)

    @pl.when(z < nz - 1)
    def _():
        pl.semaphore_signal(barrier, inc=1, device_id=up, device_id_type=MESH)

    @pl.when(z > 0)
    def _():
        pl.semaphore_signal(barrier, inc=1, device_id=down, device_id_type=MESH)

    line_peers = jnp.where(z > 0, 1, 0) + jnp.where(z < nz - 1, 1, 0)
    pl.semaphore_wait(barrier, (3 if twins else 1) + line_peers)

    def send_own(h):
        weight_loads[h].wait()

        @pl.when(z < nz - 1)
        def _():
            z_copy(h, z, 0).start()

        @pl.when(z > 0)
        def _():
            z_copy(h, z, 1).start()

    def each_way(d, action):
        @pl.when(z - d >= 0)
        def _():
            action(z - d, 0)

        @pl.when(z + d < nz)
        def _():
            action(z + d, 1)

    def passes_on(way):
        return z < nz - 1 if way == 0 else z > 0

    def forward_z(h, d):
        def one(zs, way):
            wait_piece(h, zs, 0)

            @pl.when(passes_on(way))
            def _():
                z_copy(h, zs, way).start()

        each_way(d, one)

    def drain_sends(h, d):
        def one(zs, way):
            @pl.when(passes_on(way))
            def _():
                z_copy(h, zs, way).wait_send()

        each_way(d, one)

    def drain_own(h):
        @pl.when(z < nz - 1)
        def _():
            z_copy(h, z, 0).wait_send()

        @pl.when(z > 0)
        def _():
            z_copy(h, z, 1).wait_send()

    def add_shard(h, s):
        columns = pl.ds(pl.multiple_of(s * depth, depth), depth)

        def tile(t, carry):
            rows = pl.ds(pl.multiple_of(t * 256, 256), 256)
            acc[h, rows, :] += jnp.dot(xbuf[rows, columns], wbuf[h, s], preferred_element_type=jnp.float32)
            return carry

        lax.fori_loop(0, length // 256, tile, 0)

    def add_same(h, d):
        each_way(d, lambda zs, way: add_shard(h, zs))

    def rotated(u, rows):
        return (u * cos_ref[rows, :] + pltpu.roll(u, HEAD_DIM // 2, 1) * sin_ref[rows, :]).astype(jnp.bfloat16)

    def wait_queries():
        for load in other_loads[1:]:
            load.wait()
        query_copy.wait_recv()

    def rotate_queries(first, count):
        def head(i, carry):
            cols = pl.ds(pl.multiple_of(i * HEAD_DIM, HEAD_DIM), HEAD_DIM)

            def tile(t, carry):
                rows = pl.ds(pl.multiple_of(t * 128, 128), 128)
                qbuf[rows, cols] = rotated(qbuf[rows, cols].astype(jnp.float32), rows)
                return carry

            return lax.fori_loop(0, length // 128, tile, carry)

        lax.fori_loop(first, first + count, head, 0)

    def make_bias():
        first = doc_ref[0]
        row = lax.broadcasted_iota(jnp.int32, (length, length), 0)
        col = lax.broadcasted_iota(jnp.int32, (length, length), 1)
        visible = (col <= row) & ((col >= first) | (row < first))
        bias[...] = jnp.where(visible, 0.0, MASKED)

    def finish_keys():
        def tile(t, carry):
            rows = pl.ds(pl.multiple_of(t * 128, 128), 128)
            for h in range(2):
                kbuf[h, rows, :] = rotated(acc[0, rows, h * HEAD_DIM:(h + 1) * HEAD_DIM], rows)
            return carry

        lax.fori_loop(0, length // 128, tile, 0)

    factor = HEAD_DIM ** -0.5 * 1.4426950408889634

    def weigh(first, count):
        h = first // GROUP

        def head(i, carry):
            cols = pl.ds(pl.multiple_of(i * HEAD_DIM, HEAD_DIM), HEAD_DIM)
            for block in range(2):
                rows = slice(block * own_rows, (block + 1) * own_rows)
                keys = (block + 1) * own_rows
                scores = lax.dot_general(
                    qbuf[rows, cols], kbuf[h, :keys, :], (((1,), (1,)), ((), ())),
                    preferred_element_type=jnp.float32,
                ) * factor + bias[rows, :keys]
                probs = jnp.exp2(scores - jnp.max(scores, axis=1, keepdims=True))
                total = jnp.sum(probs, axis=1, keepdims=True)
                pbuf[i, rows, :keys] = probs.astype(jnp.bfloat16)
                inverse[i, rows, :] = jnp.broadcast_to(1.0 / total, (own_rows, HEAD_DIM))
            return carry

        lax.fori_loop(first, first + count, head, 0)

    def mix(first, count):
        h = first // GROUP

        def head(i, carry):
            cols = pl.ds(pl.multiple_of(i * HEAD_DIM, HEAD_DIM), HEAD_DIM)
            for block in range(2):
                rows = slice(block * own_rows, (block + 1) * own_rows)
                keys = (block + 1) * own_rows
                mixed = jnp.dot(
                    pbuf[i, rows, :keys], vbuf[:keys, h * HEAD_DIM:(h + 1) * HEAD_DIM],
                    preferred_element_type=jnp.float32,
                )
                obuf[rows, cols] = (mixed * inverse[i, rows, :]).astype(jnp.bfloat16)
            return carry

        lax.fori_loop(first, first + count, head, 0)

    def out_copies(h):
        width = half_cols // OUT_GROUPS
        source = pl.ds(h * width, width)
        target = out_ref.at[0, :, pl.ds(pl.multiple_of(c * half_cols + h * width, width), width)]
        return (
            pltpu.make_async_copy(obuf.at[own, source], target, out_sem.at[h]),
            pltpu.make_async_remote_copy(
                src_ref=obuf.at[other, source], dst_ref=target, send_sem=out_send.at[h],
                recv_sem=out_recv.at[h], device_id=pair, device_id_type=MESH,
            ),
        )

    def send_out(h):
        for one in out_copies(h):
            one.start()

    query_copy = pltpu.make_async_remote_copy(
        src_ref=queries_ref.at[0, :, other_cols], dst_ref=qbuf.at[own, :], send_sem=pair_send.at[0],
        recv_sem=pair_recv.at[0], device_id=pair, device_id_type=MESH,
    )
    normed_copy = pltpu.make_async_remote_copy(
        src_ref=normed_ref.at[0], dst_ref=xbuf.at[own, :], send_sem=pair_send.at[1],
        recv_sem=pair_recv.at[1], device_id=pair, device_id_type=MESH,
    )

    def begin():
        for load in other_loads:
            load.start()
        query_copy.start()
        normed_copy.start()

    def clear():
        acc[...] = jnp.zeros_like(acc)
        make_bias()

    def wait_normed():
        other_loads[0].wait()
        normed_copy.wait_recv()

    if twins:
        steps = {
            "load": lambda h: weight_loads[h].wait(),
            "begin": begin,
            "clear": clear,
            "queries": wait_queries,
            "rotate": rotate_queries,
            "normed": wait_normed,
            "add": lambda h, k, o: add_shard(h, place(k, o)),
            "keys": finish_keys,
            "weigh": weigh,
        }
        sent = [0, 0]
        held = [set(), set()]
        for name, operands, *moves in SCHEDULE:
            for role in range(2):
                @pl.when(middle == role)
                def _(role=role):
                    for link, *which in moves[role]:
                        h, k, o, j = which
                        if (k or o) and tuple(which) not in held[role]:
                            held[role].add(tuple(which))
                            wait_piece(h, place(k, o), j)
                        if link < WAIT:
                            send(sent[role], link, h, k, o, j).start()
                            sent[role] += 1
            if name:
                steps[name](*operands)
    else:
        send_own(0)
        begin()
        clear()
        wait_queries()
        rotate_queries(0, half_cols // HEAD_DIM)
        send_own(1)
        wait_normed()
        for h in range(PHASES):
            add_shard(h, f)

            def step(d, carry, h=h):
                forward_z(h, d)
                add_same(h, d)
                return carry

            lax.fori_loop(1, nz, step, 0)
            if h == 0:
                finish_keys()
                weigh(0, 8)
                weigh(8, 8)
    vbuf[...] = acc[1].astype(jnp.bfloat16)
    heads = 2 * GROUP // OUT_GROUPS
    for group in range(OUT_GROUPS):
        mix(group * heads, heads)
        send_out(group)

    if twins:
        for role in range(2):
            @pl.when(middle == role)
            def _(role=role):
                moves = [move for step in SCHEDULE for move in step[2 + role] if move[0] < WAIT]
                for index, move in enumerate(moves):
                    send(index, *move).wait_send()
    else:
        for h in range(PHASES):
            drain_own(h)

            def drain(d, carry, h=h):
                drain_sends(h, d)
                return carry

            lax.fori_loop(1, nz, drain, 0)
    query_copy.wait_send()
    normed_copy.wait_send()
    for group in range(OUT_GROUPS):
        local, remote = out_copies(group)
        local.wait()
        remote.wait()


def body(groups, shards, normed, queries, key_weight, value_weight, doc_start):
    _, rows, width = normed.shape
    depth = key_weight.shape[0]
    query_cols = queries.shape[2]
    length = 2 * rows
    twins = paired(groups, shards)
    parts = PARTS if twins else 1
    sends = max(sum(move[0] < WAIT for step in SCHEDULE for move in step[role]) for role in (2, 3))
    cosine, sine = rotary_tables(length)
    dma = pltpu.SemaphoreType.DMA
    hbm = pl.BlockSpec(memory_space=pl.ANY)
    return pl.pallas_call(
        functools.partial(kernel, groups, shards),
        out_shape=jax.ShapeDtypeStruct((1, rows, query_cols), jnp.bfloat16),
        in_specs=[pl.BlockSpec(memory_space=pltpu.SMEM)] + [hbm] * 6,
        out_specs=hbm,
        scratch_shapes=[
            pltpu.VMEM((PHASES, shards, depth, 2 * HEAD_DIM), jnp.bfloat16),
            pltpu.VMEM((length, width), jnp.bfloat16),
            pltpu.VMEM((length, query_cols // 2), jnp.bfloat16),
            pltpu.VMEM((length, query_cols // 2), jnp.bfloat16),
            pltpu.VMEM((2 * GROUP, length, length), jnp.bfloat16),
            pltpu.VMEM((2 * GROUP, length, HEAD_DIM), jnp.float32),
            pltpu.VMEM((PHASES, length, 2 * HEAD_DIM), jnp.float32),
            pltpu.VMEM((2, length, HEAD_DIM), jnp.bfloat16),
            pltpu.VMEM((length, 2 * HEAD_DIM), jnp.bfloat16),
            pltpu.VMEM((length, length), jnp.float32),
            pltpu.VMEM((length, HEAD_DIM), jnp.float32),
            pltpu.VMEM((length, HEAD_DIM), jnp.float32),
            dma((6,)),
            dma((PHASES, shards, parts)),
            dma((sends if twins else PHASES * shards * 2,)),
            dma((2,)),
            dma((2,)),
            dma((OUT_GROUPS,)),
            dma((OUT_GROUPS,)),
            dma((OUT_GROUPS,)),
        ],
        compiler_params=pltpu.CompilerParams(
            collective_id=0, has_side_effects=True, vmem_limit_bytes=56 * 1024 * 1024
        ),
    )(doc_start, normed, queries, key_weight, value_weight, jnp.asarray(cosine), jnp.asarray(sine))


def solution(mesh):
    placed = (
        P(("group", "fsdp"), "ctx", None),
        P(("group", "fsdp"), "ctx", None),
        P("fsdp", None),
        P("fsdp", None),
        P(("group", "fsdp")),
    )
    return jax.shard_map(
        functools.partial(body, mesh.shape["group"], mesh.shape["fsdp"]),
        mesh=mesh,
        in_specs=placed,
        out_specs=P(("group", "fsdp"), "ctx", None),
        check_vma=False,
    )
```

```python
import functools

import jax
import jax.numpy as jnp
import numpy as np
from jax import lax
from jax.experimental import pallas as pl
from jax.experimental.pallas import tpu as pltpu
from jax.sharding import PartitionSpec as P

HEAD_DIM = 128
GROUP = 8
THETA = 500000.0
MASKED = -1e30
MESH = pl.DeviceIdType.MESH
PHASES = 2
OUT_GROUPS = 4
PARTS = 8
WAIT = 4
CHUNKS = 4
ROWS, SHARES = 2, 3
SHARE_TYPE = jnp.bfloat16
SCHEDULE = (
    ("load", (0,), (), ()),
    ("begin", (), ((0, 0, 0, 0, 0), (2, 0, 0, 0, 0), (0, 0, 0, 0, 1), (2, 0, 0, 0, 1), (0, 0, 0, 0, 2), (2, 0, 0, 0, 2)), ((0, 0, 0, 0, 0), (1, 0, 0, 0, 0), (0, 0, 0, 0, 1), (1, 0, 0, 0, 1), (0, 0, 0, 0, 2), (1, 0, 0, 0, 2))),
    ("load", (1,), (), ()),
    ("clear", (), (), ((2, 1, 0, 0, 0), (2, 1, 0, 0, 1), (2, 1, 0, 0, 2))),
    ("queries", (), ((0, 0, 0, 0, 3), (0, 0, 0, 0, 4), (4, 0, 0, 1, 0), (3, 0, 0, 1, 0), (4, 0, 1, 0, 0), (2, 0, 1, 0, 0), (3, 0, 1, 0, 0)), ((0, 0, 0, 0, 3), (1, 0, 0, 0, 3), (4, 1, 0, 1, 0), (3, 1, 0, 1, 0), (4, 0, 1, 0, 0), (2, 0, 1, 0, 0), (0, 0, 1, 0, 0), (4, 0, 2, 0, 0), (1, 0, 2, 0, 0), (2, 0, 2, 0, 0))),
    ("rotate", (0, 2), (), ()),
    ("rotate", (2, 2), ((0, 0, 0, 0, 5),), ()),
    ("rotate", (4, 2), ((4, 0, 1, 0, 1), (2, 0, 1, 0, 1), (3, 0, 1, 0, 1), (0, 0, 0, 0, 6)), ((4, 1, 0, 1, 1), (3, 1, 0, 1, 1), (4, 0, 1, 0, 1), (0, 0, 1, 0, 1), (4, 0, 2, 0, 1), (1, 0, 2, 0, 1), (2, 0, 1, 0, 1), (2, 0, 2, 0, 1))),
    ("rotate", (6, 2), ((4, 0, 1, 0, 2), (2, 0, 1, 0, 2)), ((4, 1, 0, 1, 2), (3, 1, 0, 1, 2), (4, 0, 1, 0, 2), (0, 0, 1, 0, 2), (4, 0, 2, 0, 2), (1, 0, 2, 0, 2))),
    ("rotate", (8, 2), ((0, 0, 0, 0, 7), (4, 0, 1, 1, 0), (3, 0, 1, 1, 0), (4, 0, 1, 0, 3), (2, 0, 1, 0, 3)), ((4, 0, 1, 1, 0), (3, 0, 1, 1, 0), (4, 0, 1, 0, 3), (0, 0, 1, 0, 3), (4, 0, 2, 0, 3), (1, 0, 2, 0, 3))),
    ("rotate", (10, 2), ((0, 1, 0, 0, 0),), ((0, 0, 0, 0, 4),)),
    ("rotate", (12, 2), ((4, 0, 2, 0, 0), (3, 0, 2, 0, 0), (2, 0, 2, 0, 0), (4, 0, 1, 1, 1), (3, 0, 1, 1, 1)), ((4, 0, 2, 1, 0), (3, 0, 2, 1, 0), (4, 0, 3, 0, 0), (2, 0, 3, 0, 0), (1, 0, 3, 0, 0))),
    ("rotate", (14, 2), ((0, 1, 0, 0, 1), (4, 0, 2, 0, 1), (2, 0, 2, 0, 1), (3, 0, 2, 0, 1)), ((0, 0, 0, 0, 5), (2, 0, 1, 0, 2), (4, 0, 1, 1, 1), (3, 0, 1, 1, 1), (4, 0, 3, 0, 1), (2, 0, 3, 0, 1), (1, 0, 3, 0, 1))),
    ("normed", (), ((0, 1, 0, 0, 2), (4, 0, 2, 0, 2), (2, 0, 2, 0, 2), (0, 1, 0, 0, 3), (4, 0, 2, 1, 0), (3, 0, 2, 1, 0), (4, 0, 2, 0, 3), (2, 0, 2, 0, 3)), ((0, 0, 0, 0, 6), (2, 0, 2, 0, 2), (4, 0, 2, 1, 1), (3, 0, 2, 1, 1), (4, 0, 3, 0, 2), (1, 0, 3, 0, 2), (0, 0, 0, 0, 7), (2, 0, 3, 0, 2), (4, 0, 3, 1, 0), (3, 0, 3, 1, 0), (4, 0, 3, 0, 3), (1, 0, 3, 0, 3))),
    ("add", (0, 0, 0), (), ()),
    ("add", (1, 0, 0), ((0, 1, 0, 0, 4),), ((4, 0, 1, 0, 4), (0, 0, 1, 0, 4), (1, 0, 0, 0, 4), (2, 0, 1, 0, 3))),
    ("add", (0, 1, 0), ((4, 0, 3, 0, 0), (3, 0, 3, 0, 0), (2, 0, 3, 0, 0), (4, 0, 2, 1, 1), (3, 0, 2, 1, 1), (0, 1, 0, 0, 5), (4, 0, 3, 0, 1), (2, 0, 3, 0, 1), (3, 0, 3, 0, 1), (0, 2, 0, 0, 0), (4, 0, 3, 0, 2), (2, 0, 3, 0, 2), (2, 0, 0, 0, 3), (4, 0, 1, 1, 2), (3, 0, 1, 1, 2), (4, 0, 3, 1, 0), (3, 0, 3, 1, 0), (4, 0, 3, 0, 3), (2, 0, 3, 0, 3), (2, 0, 0, 0, 4), (4, 0, 2, 1, 2), (3, 0, 2, 1, 2), (4, 0, 3, 1, 1), (3, 0, 3, 1, 1), (2, 0, 0, 0, 5), (4, 0, 3, 1, 2), (3, 0, 3, 1, 2), (4, 0, 1, 0, 7), (4, 0, 1, 0, 6), (4, 0, 1, 0, 4), (4, 0, 1, 0, 5)), ((4, 0, 3, 1, 1), (3, 0, 3, 1, 1), (4, 0, 1, 0, 5), (0, 0, 1, 0, 5), (1, 0, 0, 0, 5), (2, 0, 2, 0, 3), (4, 0, 1, 1, 2), (3, 0, 1, 1, 2), (4, 0, 1, 0, 6), (0, 0, 1, 0, 6), (4, 0, 2, 0, 4), (1, 0, 2, 0, 4), (2, 0, 3, 0, 3), (4, 0, 2, 1, 2), (3, 0, 2, 1, 2), (4, 0, 1, 0, 7), (0, 0, 1, 0, 7), (4, 0, 2, 0, 5), (1, 0, 2, 0, 5), (2, 1, 0, 0, 3), (4, 0, 3, 1, 2), (3, 0, 3, 1, 2), (0, 1, 0, 0, 0), (2, 1, 0, 0, 4), (4, 0, 1, 1, 3), (3, 0, 1, 1, 3), (4, 0, 3, 0, 4), (1, 0, 3, 0, 4), (0, 1, 0, 0, 1), (2, 0, 0, 0, 0), (4, 0, 2, 1, 3), (3, 0, 2, 1, 3), (4, 0, 3, 0, 5), (1, 0, 3, 0, 5))),
    ("add", (0, 2, 0), ((2, 0, 0, 0, 6), (0, 2, 0, 0, 1), (4, 0, 1, 1, 3), (3, 0, 1, 1, 3), (2, 1, 0, 0, 0), (4, 0, 2, 1, 3), (3, 0, 2, 1, 3), (4, 0, 2, 0, 7), (4, 0, 2, 0, 6), (4, 0, 2, 0, 4), (4, 0, 2, 0, 5)), ((0, 1, 0, 0, 2), (2, 0, 0, 0, 1), (4, 0, 3, 1, 3), (3, 0, 3, 1, 3), (0, 1, 0, 0, 3), (2, 0, 0, 0, 2), (4, 0, 2, 0, 6), (4, 0, 2, 0, 7))),
    ("add", (0, 3, 0), ((2, 1, 0, 0, 1), (4, 0, 3, 1, 3), (3, 0, 3, 1, 3), (2, 1, 0, 0, 2), (4, 0, 3, 0, 7), (4, 0, 3, 0, 6), (4, 0, 3, 0, 4), (4, 0, 3, 0, 5)), ((4, 1, 1, 0, 0), (0, 1, 1, 0, 0), (2, 0, 0, 0, 3), (4, 1, 2, 0, 0), (1, 1, 2, 0, 0), (4, 1, 1, 0, 1), (0, 1, 1, 0, 1), (2, 0, 0, 0, 4), (4, 1, 2, 0, 1), (1, 1, 2, 0, 1), (4, 0, 0, 1, 0), (3, 0, 0, 1, 0), (4, 0, 3, 0, 6), (4, 0, 3, 0, 7))),
    ("add", (0, 1, 1), ((0, 2, 0, 0, 2), (4, 1, 2, 0, 0), (3, 1, 2, 0, 0), (2, 1, 2, 0, 0), (4, 0, 1, 1, 7), (4, 0, 1, 1, 6), (4, 0, 1, 1, 5), (4, 0, 1, 1, 4)), ((4, 2, 1, 0, 0), (4, 1, 1, 0, 2), (0, 1, 1, 0, 2), (2, 1, 1, 0, 0), (4, 1, 2, 0, 2), (1, 1, 2, 0, 2), (4, 0, 0, 1, 1), (3, 0, 0, 1, 1), (4, 1, 1, 0, 3), (0, 1, 1, 0, 3), (2, 1, 2, 0, 0), (4, 0, 1, 1, 7), (4, 0, 1, 1, 6), (4, 0, 1, 1, 5), (4, 0, 1, 1, 4))),
    ("add", (0, 2, 1), ((4, 1, 0, 1, 0), (3, 1, 0, 1, 0), (4, 1, 2, 0, 1), (2, 1, 2, 0, 1), (3, 1, 2, 0, 1), (4, 0, 2, 1, 7), (4, 0, 2, 1, 6), (4, 0, 2, 1, 5), (4, 0, 2, 1, 4)), ((4, 1, 2, 0, 3), (1, 1, 2, 0, 3), (4, 0, 0, 1, 2), (3, 0, 0, 1, 2), (0, 1, 0, 0, 4), (4, 0, 2, 1, 7), (4, 0, 2, 1, 6), (4, 0, 2, 1, 5), (4, 0, 2, 1, 4))),
    ("add", (0, 3, 1), ((4, 1, 2, 0, 2), (2, 1, 2, 0, 2), (4, 0, 3, 1, 7), (4, 0, 3, 1, 6), (4, 0, 3, 1, 5), (4, 0, 3, 1, 4)), ((4, 1, 3, 0, 0), (1, 1, 3, 0, 0), (2, 1, 3, 0, 0), (0, 1, 0, 0, 5), (2, 1, 1, 0, 1), (4, 0, 3, 1, 7), (4, 0, 3, 1, 6), (4, 0, 3, 1, 5), (4, 0, 3, 1, 4))),
    ("add", (0, 0, 1), ((0, 2, 0, 0, 3), (4, 1, 2, 0, 3), (2, 1, 2, 0, 3), (4, 0, 0, 1, 1), (4, 0, 0, 1, 2), (4, 0, 0, 1, 7), (4, 0, 0, 1, 3), (4, 0, 0, 1, 4), (4, 0, 0, 1, 5), (4, 0, 0, 1, 6)), ((4, 1, 3, 0, 1), (1, 1, 3, 0, 1), (4, 2, 1, 0, 1), (0, 1, 0, 0, 6), (2, 1, 2, 0, 1), (4, 0, 0, 1, 7), (4, 0, 0, 1, 3), (4, 0, 0, 1, 6), (4, 0, 0, 1, 4), (4, 0, 0, 1, 5))),
    ("keys", (), ((4, 1, 2, 1, 0), (3, 1, 2, 1, 0)), ((4, 1, 0, 1, 7), (4, 1, 0, 1, 6), (4, 1, 0, 1, 5), (4, 1, 0, 1, 3), (4, 1, 0, 1, 4), (1, 3, 0, 0, 0), (4, 1, 3, 0, 2), (1, 1, 3, 0, 2), (4, 1, 1, 1, 0), (3, 1, 1, 1, 0))),
    ("weigh", (0, 2), ((4, 1, 3, 0, 0), (3, 1, 3, 0, 0), (2, 1, 3, 0, 0)), ((0, 1, 0, 0, 7), (2, 1, 3, 0, 1))),
    ("weigh", (2, 2), ((4, 1, 2, 1, 1), (3, 1, 2, 1, 1), (4, 1, 3, 0, 1), (2, 1, 3, 0, 1), (3, 1, 3, 0, 1)), ((4, 1, 3, 0, 3), (1, 1, 3, 0, 3), (4, 1, 2, 1, 0), (3, 1, 2, 1, 0), (1, 3, 0, 0, 1), (4, 1, 1, 0, 4), (0, 1, 1, 0, 4), (2, 1, 1, 0, 2))),
    ("weigh", (4, 2), (), ((4, 1, 3, 1, 0), (3, 1, 3, 1, 0), (4, 1, 2, 0, 4), (1, 1, 2, 0, 4))),
    ("weigh", (6, 2), ((4, 1, 3, 0, 2), (2, 1, 3, 0, 2)), ((4, 1, 1, 0, 5), (0, 1, 1, 0, 5), (2, 1, 2, 0, 2))),
    ("weigh", (8, 2), ((0, 1, 0, 0, 6), (2, 1, 0, 0, 3), (4, 1, 3, 0, 3), (2, 1, 3, 0, 3)), ((4, 1, 1, 1, 1), (3, 1, 1, 1, 1), (4, 1, 2, 0, 5), (1, 1, 2, 0, 5), (4, 2, 1, 0, 2), (2, 1, 3, 0, 2))),
    ("weigh", (10, 2), ((4, 1, 2, 1, 2), (3, 1, 2, 1, 2), (4, 1, 3, 1, 0), (3, 1, 3, 1, 0)), ((4, 1, 2, 1, 1), (3, 1, 2, 1, 1))),
    ("weigh", (12, 2), ((0, 1, 0, 0, 7), (2, 1, 0, 0, 4), (4, 1, 3, 1, 1), (3, 1, 3, 1, 1)), ((2, 1, 1, 0, 3), (4, 1, 3, 1, 1), (3, 1, 3, 1, 1))),
    ("weigh", (14, 2), ((2, 1, 0, 0, 5),), ((1, 3, 0, 0, 2), (2, 1, 2, 0, 3))),
    ("add", (1, 2, 0), ((4, 1, 2, 1, 3), (3, 1, 2, 1, 3), (4, 1, 3, 1, 2), (3, 1, 3, 1, 2), (2, 1, 0, 0, 6), (4, 1, 3, 1, 3), (3, 1, 3, 1, 3), (4, 1, 2, 0, 7), (4, 1, 2, 0, 6), (4, 1, 2, 0, 4), (4, 1, 2, 0, 5)), ((4, 1, 1, 1, 2), (3, 1, 1, 1, 2), (4, 1, 3, 0, 4), (1, 1, 3, 0, 4), (2, 1, 3, 0, 3), (4, 2, 1, 0, 3), (4, 1, 2, 1, 2), (3, 1, 2, 1, 2), (4, 1, 3, 0, 5), (1, 1, 3, 0, 5), (4, 1, 2, 0, 6), (4, 1, 2, 0, 7))),
    ("add", (1, 1, 0), (), ((4, 1, 1, 0, 6), (0, 1, 1, 0, 6), (4, 1, 3, 1, 2), (3, 1, 3, 1, 2), (4, 1, 1, 0, 7), (0, 1, 1, 0, 7))),
    ("add", (1, 0, 1), ((4, 1, 0, 1, 1), (4, 1, 0, 1, 2), (4, 1, 0, 1, 7), (4, 1, 0, 1, 3), (4, 1, 0, 1, 4), (4, 1, 0, 1, 5), (4, 1, 0, 1, 6)), ((4, 1, 1, 1, 3), (3, 1, 1, 1, 3), (1, 3, 0, 0, 3), (4, 1, 2, 1, 3), (3, 1, 2, 1, 3), (4, 1, 3, 1, 3), (3, 1, 3, 1, 3))),
    ("add", (1, 3, 0), ((4, 1, 3, 0, 7), (4, 1, 3, 0, 6), (4, 1, 3, 0, 4), (4, 1, 3, 0, 5)), ((4, 1, 3, 0, 6), (4, 1, 3, 0, 7))),
    ("add", (1, 1, 1), (), ((4, 1, 1, 1, 7), (4, 1, 1, 1, 6), (4, 1, 1, 1, 5), (4, 1, 1, 1, 4))),
    ("add", (1, 2, 1), ((4, 1, 2, 1, 7), (4, 1, 2, 1, 6), (4, 1, 2, 1, 5), (4, 1, 2, 1, 4)), ((4, 1, 2, 1, 7), (4, 1, 2, 1, 6), (4, 1, 2, 1, 5), (4, 1, 2, 1, 4))),
    ("add", (1, 3, 1), ((4, 1, 3, 1, 7), (4, 1, 3, 1, 6), (4, 1, 3, 1, 5), (4, 1, 3, 1, 4)), ((4, 1, 3, 1, 7), (4, 1, 3, 1, 6), (4, 1, 3, 1, 5), (4, 1, 3, 1, 4))),
    ("", (), ((4, 3, 1, 0, 0), (4, 3, 1, 0, 1), (4, 3, 1, 0, 2), (4, 3, 1, 0, 3)), ()),
    ("", (), (), ()),
)


def paired(groups, shards):
    return groups == 2 and shards == 8


def rotary_tables(length):
    half = HEAD_DIM // 2
    exponent = -np.arange(half, dtype=np.float32) * np.float32(2.0) / np.float32(HEAD_DIM)
    frequency = np.power(np.float32(THETA), exponent, dtype=np.float32)
    angles = np.arange(length, dtype=np.float32)[:, None] * frequency[None, :]
    cosine, sine = np.cos(angles).astype(np.float32), np.sin(angles).astype(np.float32)
    return np.concatenate([cosine, cosine], 1), np.concatenate([-sine, sine], 1)


def kernel(
    groups, shards, doc_ref, normed_ref, queries_ref, key_ref, value_ref, cos_hbm, sin_hbm, out_ref,
    wbuf, xbuf, qbuf, obuf, pbuf, inverse, acc, kbuf, vbuf, bias, cos_ref, sin_ref,
    guest, share_out, share_in, load_sem, recv_sem, send_sem, guest_sem, share_sem, pair_send, pair_recv, out_sem, out_send, out_recv,
):
    twins = paired(groups, shards)
    ny = 2 if twins else 1
    nz = shards // ny
    parts = PARTS if twins else 1
    g, f, c = lax.axis_index("group"), lax.axis_index("fsdp"), lax.axis_index("ctx")
    z, y = f // ny, f % ny
    own_rows, depth = normed_ref.shape[1], key_ref.shape[0]
    length = 2 * own_rows
    piece_rows = depth // parts
    half_cols = queries_ref.shape[2] // 2
    pair = (g, f, 1 - c)
    up, down = (g, f + ny, c), (g, f - ny, c)
    if twins:
        y_dev, x_dev = (g, z * 2 + 1 - y, c), (1 - g, f, c)

    def shard(zs, ys):
        return zs * ny + ys

    def part(j):
        return g * (parts - 1) + j * (1 - 2 * g) if twins else 0

    def piece(h, s, q):
        return wbuf.at[h, s, pl.ds(pl.multiple_of(q * piece_rows, piece_rows), piece_rows), :]

    def copy(h, s, q, send_sem, device):
        ref = piece(h, s, q)
        return pltpu.make_async_remote_copy(
            src_ref=ref, dst_ref=ref, send_sem=send_sem, recv_sem=recv_sem.at[h, s, q],
            device_id=device, device_id_type=MESH,
        )

    middle = (z + 1) // 2 % 2
    inward = 1 - 2 * (z // 2)

    def place(k, o):
        zs = z if k == 0 else z + inward * (k - middle * (2 if k == 1 else 1))
        return shard(zs, 1 - y if o else y)

    def wait_piece(h, s, j):
        q = part(j)
        copy(h, s, q, recv_sem.at[h, s, q], pair).wait_recv()

    chunk = own_rows // CHUNKS

    def remote(source, target, send_sem, recv_sem, device):
        return pltpu.make_async_remote_copy(
            src_ref=source, dst_ref=target, send_sem=send_sem, recv_sem=recv_sem, device_id=device, device_id_type=MESH,
        )

    def send(index, link, h, k, o, j):
        near, far = (g, f + inward * ny, c), (g, f - inward * ny, c)
        device = near if link == 0 else far if link == 1 else y_dev if link == 2 else x_dev
        done = send_sem.at[index]
        if h == ROWS:
            start = pl.multiple_of((z + inward) * ny * depth, ny * depth)
            source = normed_ref.at[0, pl.ds(j * chunk, chunk), pl.ds(start, ny * depth)]
            return remote(source, guest.at[c, j], done, guest_sem.at[0, j], device)
        if h == SHARES:
            return remote(share_out.at[j], share_in.at[j], done, share_sem.at[j], device)
        return copy(h, place(k, o), part(j), done, device)

    def pass_guest(j):
        ref = guest.at[c, j]
        return remote(ref, ref, guest_sem.at[1, j], guest_sem.at[2, j], pair)

    def arrive(h, k, o, j):
        if h == ROWS:
            remote(guest.at[c, j], guest.at[c, j], guest_sem.at[1, j], guest_sem.at[0, j], pair).wait_recv()
            pass_guest(j).start()
        elif h == SHARES:
            remote(share_in.at[j], share_in.at[j], share_sem.at[j], share_sem.at[j], pair).wait_recv()
        else:
            wait_piece(h, place(k, o), j)

    def make_share(j):
        pass_guest(j).wait_recv()
        for side in range(2):
            total = jnp.zeros((chunk, 2 * HEAD_DIM), jnp.float32)
            for ys in range(ny):
                total += jnp.dot(
                    guest[side, j, :, ys * depth:(ys + 1) * depth], wbuf[1, shard(z, ys)],
                    preferred_element_type=jnp.float32,
                )
            share_out[j, side] = total.astype(SHARE_TYPE)

    def finish_values():
        vbuf[...] = acc[1].astype(jnp.bfloat16)

        if twins:
            @pl.when(middle == 0)
            def _():
                for j in range(CHUNKS):
                    for side in range(2):
                        rows = slice(side * own_rows + j * chunk, side * own_rows + (j + 1) * chunk)
                        vbuf[rows, :] = (acc[1, rows, :] + share_in[j, side].astype(jnp.float32)).astype(jnp.bfloat16)

    def z_copy(h, zs, way):
        return copy(h, zs, 0, send_sem.at[(h * nz + zs) * 2 + way], up if way == 0 else down)

    head_cols = pl.ds(pl.multiple_of(c * 2 * HEAD_DIM, 2 * HEAD_DIM), 2 * HEAD_DIM)
    weight_loads = [
        pltpu.make_async_copy(ref.at[:, head_cols], wbuf.at[h, f], load_sem.at[h])
        for h, ref in enumerate((key_ref, value_ref))
    ]
    own = pl.ds(pl.multiple_of(c * own_rows, own_rows), own_rows)
    other = pl.ds(pl.multiple_of((1 - c) * own_rows, own_rows), own_rows)
    my_cols = pl.ds(pl.multiple_of(c * half_cols, half_cols), half_cols)
    other_cols = pl.ds(pl.multiple_of((1 - c) * half_cols, half_cols), half_cols)
    other_loads = [
        pltpu.make_async_copy(normed_ref.at[0], xbuf.at[own, :], load_sem.at[2]),
        pltpu.make_async_copy(queries_ref.at[0, :, my_cols], qbuf.at[own, :], load_sem.at[3]),
        pltpu.make_async_copy(cos_hbm, cos_ref, load_sem.at[4]),
        pltpu.make_async_copy(sin_hbm, sin_ref, load_sem.at[5]),
    ]
    for load in weight_loads:
        load.start()

    barrier = pltpu.get_barrier_semaphore()
    pl.semaphore_signal(barrier, inc=1, device_id=pair, device_id_type=MESH)
    if twins:
        pl.semaphore_signal(barrier, inc=1, device_id=y_dev, device_id_type=MESH)
        pl.semaphore_signal(barrier, inc=1, device_id=x_dev, device_id_type=MESH)

    @pl.when(z < nz - 1)
    def _():
        pl.semaphore_signal(barrier, inc=1, device_id=up, device_id_type=MESH)

    @pl.when(z > 0)
    def _():
        pl.semaphore_signal(barrier, inc=1, device_id=down, device_id_type=MESH)

    line_peers = jnp.where(z > 0, 1, 0) + jnp.where(z < nz - 1, 1, 0)
    pl.semaphore_wait(barrier, (3 if twins else 1) + line_peers)

    def send_own(h):
        weight_loads[h].wait()

        @pl.when(z < nz - 1)
        def _():
            z_copy(h, z, 0).start()

        @pl.when(z > 0)
        def _():
            z_copy(h, z, 1).start()

    def each_way(d, action):
        @pl.when(z - d >= 0)
        def _():
            action(z - d, 0)

        @pl.when(z + d < nz)
        def _():
            action(z + d, 1)

    def passes_on(way):
        return z < nz - 1 if way == 0 else z > 0

    def forward_z(h, d):
        def one(zs, way):
            wait_piece(h, zs, 0)

            @pl.when(passes_on(way))
            def _():
                z_copy(h, zs, way).start()

        each_way(d, one)

    def drain_sends(h, d):
        def one(zs, way):
            @pl.when(passes_on(way))
            def _():
                z_copy(h, zs, way).wait_send()

        each_way(d, one)

    def drain_own(h):
        @pl.when(z < nz - 1)
        def _():
            z_copy(h, z, 0).wait_send()

        @pl.when(z > 0)
        def _():
            z_copy(h, z, 1).wait_send()

    def add_shard(h, s):
        columns = pl.ds(pl.multiple_of(s * depth, depth), depth)

        def tile(t, carry):
            rows = pl.ds(pl.multiple_of(t * 256, 256), 256)
            acc[h, rows, :] += jnp.dot(xbuf[rows, columns], wbuf[h, s], preferred_element_type=jnp.float32)
            return carry

        lax.fori_loop(0, length // 256, tile, 0)

    def add_same(h, d):
        each_way(d, lambda zs, way: add_shard(h, zs))

    def rotated(u, rows):
        return (u * cos_ref[rows, :] + pltpu.roll(u, HEAD_DIM // 2, 1) * sin_ref[rows, :]).astype(jnp.bfloat16)

    def wait_queries():
        for load in other_loads[1:]:
            load.wait()
        query_copy.wait_recv()

    def rotate_queries(first, count):
        def head(i, carry):
            cols = pl.ds(pl.multiple_of(i * HEAD_DIM, HEAD_DIM), HEAD_DIM)

            def tile(t, carry):
                rows = pl.ds(pl.multiple_of(t * 128, 128), 128)
                qbuf[rows, cols] = rotated(qbuf[rows, cols].astype(jnp.float32), rows)
                return carry

            return lax.fori_loop(0, length // 128, tile, carry)

        lax.fori_loop(first, first + count, head, 0)

    def make_bias():
        first = doc_ref[0]
        row = lax.broadcasted_iota(jnp.int32, (length, length), 0)
        col = lax.broadcasted_iota(jnp.int32, (length, length), 1)
        visible = (col <= row) & ((col >= first) | (row < first))
        bias[...] = jnp.where(visible, 0.0, MASKED)

    def finish_keys():
        def tile(t, carry):
            rows = pl.ds(pl.multiple_of(t * 128, 128), 128)
            for h in range(2):
                kbuf[h, rows, :] = rotated(acc[0, rows, h * HEAD_DIM:(h + 1) * HEAD_DIM], rows)
            return carry

        lax.fori_loop(0, length // 128, tile, 0)

    factor = HEAD_DIM ** -0.5 * 1.4426950408889634

    def weigh(first, count):
        h = first // GROUP

        def head(i, carry):
            cols = pl.ds(pl.multiple_of(i * HEAD_DIM, HEAD_DIM), HEAD_DIM)
            for block in range(2):
                rows = slice(block * own_rows, (block + 1) * own_rows)
                keys = (block + 1) * own_rows
                scores = lax.dot_general(
                    qbuf[rows, cols], kbuf[h, :keys, :], (((1,), (1,)), ((), ())),
                    preferred_element_type=jnp.float32,
                ) * factor + bias[rows, :keys]
                probs = jnp.exp2(scores - jnp.max(scores, axis=1, keepdims=True))
                total = jnp.sum(probs, axis=1, keepdims=True)
                pbuf[i, rows, :keys] = probs.astype(jnp.bfloat16)
                inverse[i, rows, :] = jnp.broadcast_to(1.0 / total, (own_rows, HEAD_DIM))
            return carry

        lax.fori_loop(first, first + count, head, 0)

    def mix(first, count):
        h = first // GROUP

        def head(i, carry):
            cols = pl.ds(pl.multiple_of(i * HEAD_DIM, HEAD_DIM), HEAD_DIM)
            for block in range(2):
                rows = slice(block * own_rows, (block + 1) * own_rows)
                keys = (block + 1) * own_rows
                mixed = jnp.dot(
                    pbuf[i, rows, :keys], vbuf[:keys, h * HEAD_DIM:(h + 1) * HEAD_DIM],
                    preferred_element_type=jnp.float32,
                )
                obuf[rows, cols] = (mixed * inverse[i, rows, :]).astype(jnp.bfloat16)
            return carry

        lax.fori_loop(first, first + count, head, 0, unroll=count)

    def out_copies(h):
        width = half_cols // OUT_GROUPS
        source = pl.ds(h * width, width)
        target = out_ref.at[0, :, pl.ds(pl.multiple_of(c * half_cols + h * width, width), width)]
        return (
            pltpu.make_async_copy(obuf.at[own, source], target, out_sem.at[h]),
            pltpu.make_async_remote_copy(
                src_ref=obuf.at[other, source], dst_ref=target, send_sem=out_send.at[h],
                recv_sem=out_recv.at[h], device_id=pair, device_id_type=MESH,
            ),
        )

    def send_out(h):
        for one in out_copies(h):
            one.start()

    query_copy = pltpu.make_async_remote_copy(
        src_ref=queries_ref.at[0, :, other_cols], dst_ref=qbuf.at[own, :], send_sem=pair_send.at[0],
        recv_sem=pair_recv.at[0], device_id=pair, device_id_type=MESH,
    )
    normed_copy = pltpu.make_async_remote_copy(
        src_ref=normed_ref.at[0], dst_ref=xbuf.at[own, :], send_sem=pair_send.at[1],
        recv_sem=pair_recv.at[1], device_id=pair, device_id_type=MESH,
    )

    def begin():
        for load in other_loads:
            load.start()
        query_copy.start()
        normed_copy.start()

    def clear():
        acc[...] = jnp.zeros_like(acc)
        make_bias()

    def wait_normed():
        other_loads[0].wait()
        normed_copy.wait_recv()

    def add_place(h, k, o):
        if h == 1 and k == 1:
            pl.when(middle == 1)(lambda: add_shard(h, place(k, o)))
        else:
            add_shard(h, place(k, o))

    if twins:
        steps = {
            "load": lambda h: weight_loads[h].wait(),
            "begin": begin,
            "clear": clear,
            "queries": wait_queries,
            "rotate": rotate_queries,
            "normed": wait_normed,
            "add": add_place,
            "keys": finish_keys,
            "weigh": weigh,
        }
        sent = [0, 0]
        held = [set(), set()]
        for name, operands, *moves in SCHEDULE:
            for role in range(2):
                @pl.when(middle == role)
                def _(role=role):
                    for link, *which in moves[role]:
                        h, k, o, j = which
                        if (k or o) and tuple(which) not in held[role]:
                            held[role].add(tuple(which))
                            arrive(h, k, o, j)
                        if link < WAIT:
                            if h == SHARES:
                                make_share(j)
                            send(sent[role], link, h, k, o, j).start()
                            sent[role] += 1
            if name:
                steps[name](*operands)
    else:
        send_own(0)
        begin()
        clear()
        wait_queries()
        rotate_queries(0, half_cols // HEAD_DIM)
        send_own(1)
        wait_normed()
        for h in range(PHASES):
            add_shard(h, f)

            def step(d, carry, h=h):
                forward_z(h, d)
                add_same(h, d)
                return carry

            lax.fori_loop(1, nz, step, 0)
            if h == 0:
                finish_keys()
                weigh(0, 8)
                weigh(8, 8)
    finish_values()
    heads = 2 * GROUP // OUT_GROUPS
    for group in range(OUT_GROUPS):
        mix(group * heads, heads)
        send_out(group)

    if twins:
        for role in range(2):
            @pl.when(middle == role)
            def _(role=role):
                moves = [move for step in SCHEDULE for move in step[2 + role] if move[0] < WAIT]
                for index, move in enumerate(moves):
                    send(index, *move).wait_send()
                if role == 1:
                    for j in range(CHUNKS):
                        pass_guest(j).wait_send()
    else:
        for h in range(PHASES):
            drain_own(h)

            def drain(d, carry, h=h):
                drain_sends(h, d)
                return carry

            lax.fori_loop(1, nz, drain, 0)
    query_copy.wait_send()
    normed_copy.wait_send()
    for group in range(OUT_GROUPS):
        local, remote = out_copies(group)
        local.wait()
        remote.wait()


def body(groups, shards, normed, queries, key_weight, value_weight, doc_start):
    _, rows, width = normed.shape
    depth = key_weight.shape[0]
    query_cols = queries.shape[2]
    length = 2 * rows
    twins = paired(groups, shards)
    parts = PARTS if twins else 1
    sends = max(sum(move[0] < WAIT for step in SCHEDULE for move in step[role]) for role in (2, 3))
    cosine, sine = rotary_tables(length)
    dma = pltpu.SemaphoreType.DMA
    hbm = pl.BlockSpec(memory_space=pl.ANY)
    return pl.pallas_call(
        functools.partial(kernel, groups, shards),
        out_shape=jax.ShapeDtypeStruct((1, rows, query_cols), jnp.bfloat16),
        in_specs=[pl.BlockSpec(memory_space=pltpu.SMEM)] + [hbm] * 6,
        out_specs=hbm,
        scratch_shapes=[
            pltpu.VMEM((PHASES, shards, depth, 2 * HEAD_DIM), jnp.bfloat16),
            pltpu.VMEM((length, width), jnp.bfloat16),
            pltpu.VMEM((length, query_cols // 2), jnp.bfloat16),
            pltpu.VMEM((length, query_cols // 2), jnp.bfloat16),
            pltpu.VMEM((2 * GROUP, length, length), jnp.bfloat16),
            pltpu.VMEM((2 * GROUP, length, HEAD_DIM), jnp.float32),
            pltpu.VMEM((PHASES, length, 2 * HEAD_DIM), jnp.float32),
            pltpu.VMEM((2, length, HEAD_DIM), jnp.bfloat16),
            pltpu.VMEM((length, 2 * HEAD_DIM), jnp.bfloat16),
            pltpu.VMEM((length, length), jnp.float32),
            pltpu.VMEM((length, HEAD_DIM), jnp.float32),
            pltpu.VMEM((length, HEAD_DIM), jnp.float32),
            pltpu.VMEM((2, CHUNKS, rows // CHUNKS, 2 * depth if twins else HEAD_DIM), jnp.bfloat16),
            pltpu.VMEM((CHUNKS, 2, rows // CHUNKS, 2 * HEAD_DIM), SHARE_TYPE),
            pltpu.VMEM((CHUNKS, 2, rows // CHUNKS, 2 * HEAD_DIM), SHARE_TYPE),
            dma((6,)),
            dma((PHASES, shards, parts)),
            dma((sends if twins else PHASES * shards * 2,)),
            dma((3, CHUNKS)),
            dma((CHUNKS,)),
            dma((2,)),
            dma((2,)),
            dma((OUT_GROUPS,)),
            dma((OUT_GROUPS,)),
            dma((OUT_GROUPS,)),
        ],
        compiler_params=pltpu.CompilerParams(
            collective_id=0, has_side_effects=True, vmem_limit_bytes=56 * 1024 * 1024
        ),
    )(doc_start, normed, queries, key_weight, value_weight, jnp.asarray(cosine), jnp.asarray(sine))


def solution(mesh):
    placed = (
        P(("group", "fsdp"), "ctx", None),
        P(("group", "fsdp"), "ctx", None),
        P("fsdp", None),
        P("fsdp", None),
        P(("group", "fsdp")),
    )
    return jax.shard_map(
        functools.partial(body, mesh.shape["group"], mesh.shape["fsdp"]),
        mesh=mesh,
        in_specs=placed,
        out_specs=P(("group", "fsdp"), "ctx", None),
        check_vma=False,
    )
```

```python
import functools

import jax
import jax.numpy as jnp
import numpy as np
from jax import lax
from jax.experimental import pallas as pl
from jax.experimental.pallas import tpu as pltpu
from jax.sharding import PartitionSpec as P

HEAD_DIM = 128
GROUP = 8
THETA = 500000.0
MASKED = -1e30
MESH = pl.DeviceIdType.MESH
PHASES = 2
OUT_GROUPS = 4
PARTS = 8
WAIT = 4
CHUNKS = 4
ROWS, SHARES = 2, 3
SHARE_TYPE = jnp.bfloat16
SCHEDULE = (
    ("load", (0,), (), ()),
    ("begin", (), ((0, 0, 0, 0, 0), (2, 0, 0, 0, 0), (2, 0, 0, 0, 1), (0, 0, 0, 0, 3), (0, 0, 0, 0, 1)), ((0, 0, 0, 0, 0), (1, 0, 0, 0, 0), (2, 0, 0, 0, 0), (0, 0, 0, 0, 1), (1, 0, 0, 0, 1), (2, 0, 0, 0, 1), (2, 0, 0, 0, 2), (0, 0, 0, 0, 3), (1, 0, 0, 0, 3), (4, 0, 1, 0, 0), (0, 0, 1, 0, 0), (4, 0, 2, 0, 0), (3, 0, 2, 0, 0), (2, 0, 1, 0, 0), (3, 0, 1, 0, 0), (1, 0, 2, 0, 0), (0, 0, 0, 0, 4))),
    ("load", (1,), (), ()),
    ("clear", (), ((2, 1, 0, 0, 2), (0, 0, 0, 0, 2)), ((4, 0, 1, 0, 3), (2, 0, 1, 0, 3), (4, 0, 2, 0, 1), (1, 0, 2, 0, 1))),
    ("queries", (), ((2, 1, 0, 0, 0), (0, 1, 0, 0, 3), (4, 0, 1, 0, 0), (3, 0, 1, 0, 0), (4, 0, 0, 1, 0), (3, 0, 0, 1, 0), (4, 0, 1, 0, 1), (3, 0, 1, 0, 1), (0, 1, 0, 0, 4), (2, 0, 1, 0, 0), (0, 1, 0, 0, 1), (0, 1, 0, 0, 0), (2, 0, 1, 0, 1), (0, 0, 0, 0, 5)), ((4, 0, 0, 1, 1), (3, 0, 0, 1, 1), (1, 0, 0, 0, 4), (0, 0, 0, 0, 5), (4, 0, 1, 0, 1), (0, 0, 1, 0, 1))),
    ("rotate", (0, 2), ((0, 0, 0, 0, 4), (4, 1, 0, 1, 2), (3, 1, 0, 1, 2)), ((2, 0, 1, 0, 1), (4, 0, 3, 0, 0), (1, 0, 3, 0, 0), (4, 0, 2, 0, 3), (1, 0, 2, 0, 3), (2, 0, 2, 0, 1), (4, 0, 0, 1, 2), (3, 0, 0, 1, 2), (4, 0, 0, 1, 0), (3, 0, 0, 1, 0))),
    ("rotate", (2, 2), ((4, 1, 0, 1, 0), (3, 1, 0, 1, 0), (4, 0, 1, 0, 3), (2, 0, 1, 0, 3), (2, 0, 0, 0, 3), (4, 0, 1, 1, 0), (3, 0, 1, 1, 0), (4, 0, 2, 0, 0), (2, 0, 2, 0, 0), (0, 1, 0, 0, 5), (4, 0, 3, 0, 0), (3, 0, 3, 0, 0), (2, 0, 3, 0, 0), (3, 0, 2, 0, 0), (4, 0, 2, 0, 1), (2, 0, 2, 0, 1), (0, 1, 0, 0, 2), (2, 0, 0, 0, 2), (0, 1, 0, 0, 7), (4, 0, 0, 1, 1), (3, 0, 0, 1, 1), (2, 1, 0, 0, 1), (4, 0, 1, 0, 2), (2, 0, 1, 0, 2), (4, 0, 3, 0, 1), (3, 0, 3, 0, 1), (4, 0, 1, 1, 1), (3, 0, 1, 1, 1), (4, 0, 2, 0, 3), (2, 0, 2, 0, 3), (0, 0, 0, 0, 6), (4, 0, 3, 1, 0), (3, 0, 3, 1, 0)), ((2, 0, 2, 0, 0), (0, 0, 0, 0, 2), (2, 0, 3, 0, 0), (0, 0, 1, 0, 3), (1, 0, 0, 0, 2), (4, 0, 1, 1, 0), (3, 0, 1, 1, 0), (4, 0, 1, 1, 3), (3, 0, 1, 1, 3), (4, 0, 1, 0, 2), (2, 0, 1, 0, 2), (4, 0, 3, 0, 1), (1, 0, 3, 0, 1), (0, 1, 0, 0, 0), (4, 0, 2, 0, 2), (1, 0, 2, 0, 2), (2, 0, 2, 0, 2), (0, 0, 1, 0, 2), (4, 0, 2, 1, 1), (3, 0, 2, 1, 1), (4, 0, 2, 0, 4), (1, 0, 2, 0, 4), (0, 1, 0, 0, 2), (1, 0, 0, 0, 5), (4, 0, 3, 0, 3), (1, 0, 3, 0, 3), (4, 1, 1, 0, 3), (0, 1, 1, 0, 3), (2, 0, 0, 0, 3), (2, 0, 2, 0, 3), (3, 0, 3, 0, 0), (2, 0, 3, 0, 3), (4, 0, 1, 1, 1), (3, 0, 1, 1, 1), (4, 0, 2, 1, 0), (3, 0, 2, 1, 0), (4, 0, 1, 0, 4), (0, 0, 1, 0, 4))),
    ("rotate", (4, 2), (), ()),
    ("rotate", (6, 2), (), ()),
    ("rotate", (8, 2), (), ()),
    ("rotate", (10, 2), (), ()),
    ("rotate", (12, 2), ((4, 0, 2, 0, 2), (2, 0, 2, 0, 2), (0, 2, 0, 0, 0), (4, 0, 2, 1, 1), (3, 0, 2, 1, 1), (4, 0, 2, 1, 0), (3, 0, 2, 1, 0), (0, 1, 0, 0, 6), (0, 2, 0, 0, 1), (4, 0, 3, 0, 3), (2, 0, 3, 0, 3)), ((4, 1, 1, 0, 1), (0, 1, 1, 0, 1), (2, 0, 3, 0, 1), (0, 1, 0, 0, 1), (4, 0, 2, 0, 5), (1, 0, 2, 0, 5), (4, 1, 2, 0, 0), (1, 1, 2, 0, 0), (4, 0, 3, 1, 0), (3, 0, 3, 1, 0), (4, 0, 3, 0, 2), (1, 0, 3, 0, 2))),
    ("rotate", (14, 2), ((0, 2, 0, 0, 2), (2, 1, 0, 0, 3), (2, 0, 3, 0, 1), (4, 0, 1, 1, 2), (3, 0, 1, 1, 2), (4, 0, 1, 1, 3), (3, 0, 1, 1, 3), (4, 0, 2, 1, 2), (3, 0, 2, 1, 2), (2, 0, 0, 0, 4)), ((2, 0, 3, 0, 2), (2, 1, 0, 0, 1), (4, 1, 1, 0, 0), (0, 1, 1, 0, 0), (4, 0, 2, 1, 2), (3, 0, 2, 1, 2), (4, 0, 1, 1, 2), (3, 0, 1, 1, 2), (0, 0, 0, 0, 6), (4, 0, 2, 1, 3), (3, 0, 2, 1, 3), (2, 1, 0, 0, 3), (4, 0, 1, 0, 5), (0, 0, 1, 0, 5), (0, 1, 0, 0, 3), (2, 1, 1, 0, 3), (4, 1, 2, 0, 2), (1, 1, 2, 0, 2), (4, 0, 1, 0, 6), (0, 0, 1, 0, 6), (4, 1, 3, 0, 3), (2, 1, 3, 0, 3))),
    ("normed", (), (), ()),
    ("add", (0, 0, 0), (), ()),
    ("add", (1, 0, 0), (), ()),
    ("add", (0, 1, 1), ((4, 0, 2, 1, 3), (3, 0, 2, 1, 3), (0, 2, 0, 0, 3), (4, 0, 3, 0, 2), (2, 0, 3, 0, 2), (2, 0, 0, 0, 5), (4, 0, 3, 1, 3), (3, 0, 3, 1, 3), (4, 0, 3, 1, 1), (3, 0, 3, 1, 1), (2, 1, 0, 0, 4), (4, 1, 2, 0, 0), (2, 1, 2, 0, 0), (4, 0, 1, 1, 7), (4, 0, 1, 1, 6), (4, 0, 1, 1, 5), (4, 0, 1, 1, 4)), ((4, 0, 3, 1, 1), (3, 0, 3, 1, 1), (2, 1, 1, 0, 1), (4, 1, 3, 0, 1), (1, 1, 3, 0, 1), (4, 1, 1, 0, 5), (0, 1, 1, 0, 5), (4, 0, 0, 1, 3), (3, 0, 0, 1, 3), (4, 1, 1, 0, 2), (2, 1, 1, 0, 2), (4, 0, 3, 0, 4), (1, 0, 3, 0, 4), (4, 1, 3, 0, 0), (1, 1, 3, 0, 0), (0, 1, 1, 0, 2), (4, 0, 3, 1, 2), (3, 0, 3, 1, 2), (4, 1, 1, 0, 4), (0, 1, 1, 0, 4), (2, 1, 1, 0, 0), (4, 0, 1, 1, 7), (4, 0, 1, 1, 6), (4, 0, 1, 1, 5), (4, 0, 1, 1, 4))),
    ("add", (0, 1, 0), ((4, 0, 1, 0, 4), (4, 0, 1, 0, 7), (4, 0, 1, 0, 6), (4, 0, 1, 0, 5)), ((4, 0, 1, 0, 7),)),
    ("add", (0, 2, 1), ((4, 0, 2, 1, 7), (4, 0, 2, 1, 6), (4, 0, 2, 1, 5), (4, 0, 2, 1, 4)), ((4, 0, 2, 1, 7), (4, 0, 2, 1, 6), (4, 0, 2, 1, 5), (4, 0, 2, 1, 4))),
    ("add", (0, 0, 1), ((4, 0, 3, 1, 2), (3, 0, 3, 1, 2), (4, 1, 2, 0, 2), (2, 1, 2, 0, 2), (3, 1, 2, 0, 0), (4, 1, 0, 1, 1), (3, 1, 0, 1, 1), (4, 1, 3, 0, 0), (3, 1, 3, 0, 0), (4, 0, 0, 1, 2), (4, 0, 0, 1, 7), (4, 0, 0, 1, 6), (4, 0, 0, 1, 3), (4, 0, 0, 1, 4), (4, 0, 0, 1, 5)), ((4, 0, 3, 1, 3), (3, 0, 3, 1, 3), (2, 1, 0, 0, 0), (2, 1, 0, 0, 2), (0, 1, 0, 0, 4), (4, 1, 0, 1, 1), (3, 1, 0, 1, 1), (4, 0, 2, 0, 6), (1, 0, 2, 0, 6), (4, 1, 0, 1, 3), (3, 1, 0, 1, 3), (2, 1, 3, 0, 0), (2, 1, 2, 0, 2), (4, 0, 3, 0, 5), (1, 0, 3, 0, 5), (2, 1, 2, 0, 0), (4, 1, 1, 0, 6), (0, 1, 1, 0, 6), (4, 1, 2, 0, 1), (1, 1, 2, 0, 1), (4, 1, 1, 1, 3), (3, 1, 1, 1, 3), (2, 1, 2, 0, 1), (4, 2, 1, 0, 0), (1, 1, 3, 0, 3), (4, 0, 0, 1, 7), (4, 0, 0, 1, 6), (4, 0, 0, 1, 5), (4, 0, 0, 1, 4))),
    ("add", (0, 2, 0), ((4, 0, 2, 0, 4), (4, 0, 2, 0, 7), (4, 0, 2, 0, 5), (4, 0, 2, 0, 6)), ((4, 0, 2, 0, 7),)),
    ("add", (0, 3, 0), ((4, 0, 3, 0, 4), (4, 0, 3, 0, 7), (4, 0, 3, 0, 6), (4, 0, 3, 0, 5)), ((4, 0, 3, 0, 6), (4, 0, 3, 0, 7))),
    ("add", (0, 3, 1), ((4, 0, 3, 1, 7), (4, 0, 3, 1, 6), (4, 0, 3, 1, 5), (4, 0, 3, 1, 4)), ((4, 0, 3, 1, 7), (4, 0, 3, 1, 6), (4, 0, 3, 1, 5), (4, 0, 3, 1, 4))),
    ("keys", (), (), ()),
    ("weigh", (0, 2), ((4, 1, 2, 0, 1), (3, 1, 2, 0, 1), (2, 1, 2, 0, 1), (4, 1, 2, 1, 0), (3, 1, 2, 1, 0), (4, 1, 2, 1, 2), (3, 1, 2, 1, 2), (4, 1, 3, 0, 1), (2, 1, 3, 0, 1), (2, 1, 3, 0, 0)), ((2, 1, 3, 0, 1), (4, 1, 1, 0, 7), (0, 1, 1, 0, 7), (4, 2, 1, 0, 1), (4, 1, 1, 1, 2), (3, 1, 1, 1, 2), (4, 1, 3, 0, 2), (1, 1, 3, 0, 2), (0, 1, 0, 0, 5), (4, 1, 3, 0, 5), (1, 1, 3, 0, 5), (2, 1, 3, 0, 5), (4, 1, 1, 1, 1), (3, 1, 1, 1, 1))),
    ("weigh", (2, 2), (), ()),
    ("weigh", (4, 2), ((4, 1, 3, 0, 3), (2, 1, 3, 0, 3), (4, 1, 3, 0, 2), (2, 1, 3, 0, 2), (3, 1, 2, 0, 2)), ((4, 1, 2, 0, 3), (1, 1, 2, 0, 3), (4, 1, 0, 1, 0), (3, 1, 0, 1, 0), (4, 1, 2, 0, 4), (1, 1, 2, 0, 4), (4, 1, 0, 1, 2), (3, 1, 0, 1, 2), (0, 1, 0, 0, 6))),
    ("weigh", (6, 2), (), ()),
    ("weigh", (8, 2), (), ()),
    ("weigh", (10, 2), ((4, 1, 2, 1, 1), (3, 1, 2, 1, 1), (4, 1, 2, 0, 3), (2, 1, 2, 0, 3)), ((4, 1, 3, 1, 0), (3, 1, 3, 1, 0), (4, 1, 1, 1, 0), (3, 1, 1, 1, 0), (4, 2, 1, 0, 2), (4, 1, 3, 0, 6), (1, 1, 3, 0, 6), (4, 1, 3, 0, 4), (1, 1, 3, 0, 4), (4, 1, 2, 1, 2), (3, 1, 2, 1, 2), (2, 1, 2, 0, 3))),
    ("weigh", (12, 2), (), ()),
    ("weigh", (14, 2), ((4, 1, 3, 1, 0), (3, 1, 3, 1, 0), (4, 1, 3, 1, 1), (3, 1, 3, 1, 1)), ((0, 1, 0, 0, 7), (2, 1, 2, 0, 4), (2, 1, 3, 0, 4), (4, 1, 2, 1, 0), (3, 1, 2, 1, 0), (4, 1, 0, 1, 7), (4, 1, 0, 1, 6), (4, 1, 0, 1, 5), (4, 1, 0, 1, 4), (1, 3, 0, 0, 0))),
    ("add", (1, 1, 1), ((4, 1, 2, 0, 4), (2, 1, 2, 0, 4), (4, 1, 3, 0, 4), (2, 1, 3, 0, 4), (4, 1, 3, 1, 2), (3, 1, 3, 1, 2)), ((4, 2, 1, 0, 3), (1, 3, 0, 0, 1), (4, 1, 2, 1, 1), (3, 1, 2, 1, 1), (1, 3, 0, 0, 2), (4, 1, 1, 1, 7), (4, 1, 1, 1, 6), (4, 1, 1, 1, 5), (4, 1, 1, 1, 4))),
    ("add", (1, 2, 0), ((4, 1, 2, 0, 7), (4, 1, 2, 0, 6), (4, 1, 2, 0, 5)), ((4, 1, 3, 1, 1), (3, 1, 3, 1, 1), (2, 1, 3, 0, 2), (1, 3, 0, 0, 3), (4, 1, 2, 0, 5), (4, 1, 2, 0, 6), (4, 1, 2, 0, 7))),
    ("add", (1, 1, 0), (), ()),
    ("add", (1, 0, 1), ((4, 1, 0, 1, 3), (4, 1, 0, 1, 7), (4, 1, 0, 1, 6), (4, 1, 0, 1, 5), (4, 1, 0, 1, 4)), ()),
    ("add", (1, 2, 1), ((4, 1, 2, 1, 3), (4, 1, 2, 1, 7), (4, 1, 2, 1, 6), (4, 1, 2, 1, 5), (4, 1, 2, 1, 4)), ((4, 1, 2, 1, 3), (4, 1, 2, 1, 4), (4, 1, 2, 1, 7), (4, 1, 2, 1, 6), (4, 1, 2, 1, 5))),
    ("add", (1, 3, 0), ((4, 1, 3, 0, 7), (4, 1, 3, 0, 5), (4, 1, 3, 0, 6)), ((4, 1, 3, 0, 7),)),
    ("add", (1, 3, 1), ((4, 1, 3, 1, 3), (4, 1, 3, 1, 7), (4, 1, 3, 1, 6), (4, 1, 3, 1, 4), (4, 1, 3, 1, 5)), ((4, 1, 3, 1, 2), (4, 1, 3, 1, 3), (4, 1, 3, 1, 7), (4, 1, 3, 1, 4), (4, 1, 3, 1, 6), (4, 1, 3, 1, 5))),
    ("", (), ((4, 3, 1, 0, 0), (4, 3, 1, 0, 1), (4, 3, 1, 0, 2), (4, 3, 1, 0, 3)), ()),
    ("", (), (), ()),
)


def paired(groups, shards):
    return groups == 2 and shards == 8


def rotary_tables(length):
    half = HEAD_DIM // 2
    exponent = -np.arange(half, dtype=np.float32) * np.float32(2.0) / np.float32(HEAD_DIM)
    frequency = np.power(np.float32(THETA), exponent, dtype=np.float32)
    angles = np.arange(length, dtype=np.float32)[:, None] * frequency[None, :]
    cosine, sine = np.cos(angles).astype(np.float32), np.sin(angles).astype(np.float32)
    return np.concatenate([cosine, cosine], 1), np.concatenate([-sine, sine], 1)


def kernel(
    groups, shards, doc_ref, normed_ref, queries_ref, key_ref, value_ref, cos_hbm, sin_hbm, out_ref,
    wbuf, xbuf, qbuf, obuf, pbuf, inverse, acc, kbuf, vbuf, bias, cos_ref, sin_ref,
    guest, share_out, share_in, load_sem, recv_sem, send_sem, guest_sem, share_sem, pair_send, pair_recv, out_sem, out_send, out_recv,
):
    twins = paired(groups, shards)
    ny = 2 if twins else 1
    nz = shards // ny
    parts = PARTS if twins else 1
    g, f, c = lax.axis_index("group"), lax.axis_index("fsdp"), lax.axis_index("ctx")
    z, y = f // ny, f % ny
    own_rows, depth = normed_ref.shape[1], key_ref.shape[0]
    length = 2 * own_rows
    piece_rows = depth // parts
    half_cols = queries_ref.shape[2] // 2
    pair = (g, f, 1 - c)
    up, down = (g, f + ny, c), (g, f - ny, c)
    if twins:
        y_dev, x_dev = (g, z * 2 + 1 - y, c), (1 - g, f, c)

    def shard(zs, ys):
        return zs * ny + ys

    def part(j):
        return g * (parts - 1) + j * (1 - 2 * g) if twins else 0

    def piece(h, s, q):
        return wbuf.at[h, s, pl.ds(pl.multiple_of(q * piece_rows, piece_rows), piece_rows), :]

    def copy(h, s, q, send_sem, device):
        ref = piece(h, s, q)
        return pltpu.make_async_remote_copy(
            src_ref=ref, dst_ref=ref, send_sem=send_sem, recv_sem=recv_sem.at[h, s, q],
            device_id=device, device_id_type=MESH,
        )

    middle = (z + 1) // 2 % 2
    inward = 1 - 2 * (z // 2)

    def place(k, o):
        zs = z if k == 0 else z + inward * (k - middle * (2 if k == 1 else 1))
        return shard(zs, 1 - y if o else y)

    def wait_piece(h, s, j):
        q = part(j)
        copy(h, s, q, recv_sem.at[h, s, q], pair).wait_recv()

    chunk = own_rows // CHUNKS

    def remote(source, target, send_sem, recv_sem, device):
        return pltpu.make_async_remote_copy(
            src_ref=source, dst_ref=target, send_sem=send_sem, recv_sem=recv_sem, device_id=device, device_id_type=MESH,
        )

    def send(index, link, h, k, o, j):
        near, far = (g, f + inward * ny, c), (g, f - inward * ny, c)
        device = near if link == 0 else far if link == 1 else y_dev if link == 2 else x_dev
        done = send_sem.at[index]
        if h == ROWS:
            start = pl.multiple_of((z + inward) * ny * depth, ny * depth)
            source = normed_ref.at[0, pl.ds(j * chunk, chunk), pl.ds(start, ny * depth)]
            return remote(source, guest.at[c, j], done, guest_sem.at[0, j], device)
        if h == SHARES:
            return remote(share_out.at[j], share_in.at[j], done, share_sem.at[j], device)
        return copy(h, place(k, o), part(j), done, device)

    def pass_guest(j):
        ref = guest.at[c, j]
        return remote(ref, ref, guest_sem.at[1, j], guest_sem.at[2, j], pair)

    def arrive(h, k, o, j):
        if h == ROWS:
            remote(guest.at[c, j], guest.at[c, j], guest_sem.at[1, j], guest_sem.at[0, j], pair).wait_recv()
            pass_guest(j).start()
        elif h == SHARES:
            remote(share_in.at[j], share_in.at[j], share_sem.at[j], share_sem.at[j], pair).wait_recv()
        else:
            wait_piece(h, place(k, o), j)

    def make_share(j):
        pass_guest(j).wait_recv()
        for side in range(2):
            total = jnp.zeros((chunk, 2 * HEAD_DIM), jnp.float32)
            for ys in range(ny):
                total += jnp.dot(
                    guest[side, j, :, ys * depth:(ys + 1) * depth], wbuf[1, shard(z, ys)],
                    preferred_element_type=jnp.float32,
                )
            share_out[j, side] = total.astype(SHARE_TYPE)

    def finish_values():
        vbuf[...] = acc[1].astype(jnp.bfloat16)

        if twins:
            @pl.when(middle == 0)
            def _():
                for j in range(CHUNKS):
                    for side in range(2):
                        rows = slice(side * own_rows + j * chunk, side * own_rows + (j + 1) * chunk)
                        vbuf[rows, :] = (acc[1, rows, :] + share_in[j, side].astype(jnp.float32)).astype(jnp.bfloat16)

    def z_copy(h, zs, way):
        return copy(h, zs, 0, send_sem.at[(h * nz + zs) * 2 + way], up if way == 0 else down)

    head_cols = pl.ds(pl.multiple_of(c * 2 * HEAD_DIM, 2 * HEAD_DIM), 2 * HEAD_DIM)
    weight_loads = [
        pltpu.make_async_copy(ref.at[:, head_cols], wbuf.at[h, f], load_sem.at[h])
        for h, ref in enumerate((key_ref, value_ref))
    ]
    own = pl.ds(pl.multiple_of(c * own_rows, own_rows), own_rows)
    other = pl.ds(pl.multiple_of((1 - c) * own_rows, own_rows), own_rows)
    my_cols = pl.ds(pl.multiple_of(c * half_cols, half_cols), half_cols)
    other_cols = pl.ds(pl.multiple_of((1 - c) * half_cols, half_cols), half_cols)
    other_loads = [
        pltpu.make_async_copy(normed_ref.at[0], xbuf.at[own, :], load_sem.at[2]),
        pltpu.make_async_copy(queries_ref.at[0, :, my_cols], qbuf.at[own, :], load_sem.at[3]),
        pltpu.make_async_copy(cos_hbm, cos_ref, load_sem.at[4]),
        pltpu.make_async_copy(sin_hbm, sin_ref, load_sem.at[5]),
    ]
    for load in weight_loads:
        load.start()

    barrier = pltpu.get_barrier_semaphore()
    pl.semaphore_signal(barrier, inc=1, device_id=pair, device_id_type=MESH)
    if twins:
        pl.semaphore_signal(barrier, inc=1, device_id=y_dev, device_id_type=MESH)
        pl.semaphore_signal(barrier, inc=1, device_id=x_dev, device_id_type=MESH)

    @pl.when(z < nz - 1)
    def _():
        pl.semaphore_signal(barrier, inc=1, device_id=up, device_id_type=MESH)

    @pl.when(z > 0)
    def _():
        pl.semaphore_signal(barrier, inc=1, device_id=down, device_id_type=MESH)

    line_peers = jnp.where(z > 0, 1, 0) + jnp.where(z < nz - 1, 1, 0)
    pl.semaphore_wait(barrier, (3 if twins else 1) + line_peers)

    def send_own(h):
        weight_loads[h].wait()

        @pl.when(z < nz - 1)
        def _():
            z_copy(h, z, 0).start()

        @pl.when(z > 0)
        def _():
            z_copy(h, z, 1).start()

    def each_way(d, action):
        @pl.when(z - d >= 0)
        def _():
            action(z - d, 0)

        @pl.when(z + d < nz)
        def _():
            action(z + d, 1)

    def passes_on(way):
        return z < nz - 1 if way == 0 else z > 0

    def forward_z(h, d):
        def one(zs, way):
            wait_piece(h, zs, 0)

            @pl.when(passes_on(way))
            def _():
                z_copy(h, zs, way).start()

        each_way(d, one)

    def drain_sends(h, d):
        def one(zs, way):
            @pl.when(passes_on(way))
            def _():
                z_copy(h, zs, way).wait_send()

        each_way(d, one)

    def drain_own(h):
        @pl.when(z < nz - 1)
        def _():
            z_copy(h, z, 0).wait_send()

        @pl.when(z > 0)
        def _():
            z_copy(h, z, 1).wait_send()

    def add_shard(h, s):
        columns = pl.ds(pl.multiple_of(s * depth, depth), depth)

        def tile(t, carry):
            rows = pl.ds(pl.multiple_of(t * 256, 256), 256)
            acc[h, rows, :] += jnp.dot(xbuf[rows, columns], wbuf[h, s], preferred_element_type=jnp.float32)
            return carry

        lax.fori_loop(0, length // 256, tile, 0)

    def add_same(h, d):
        each_way(d, lambda zs, way: add_shard(h, zs))

    def rotated(u, rows):
        return (u * cos_ref[rows, :] + pltpu.roll(u, HEAD_DIM // 2, 1) * sin_ref[rows, :]).astype(jnp.bfloat16)

    def wait_queries():
        for load in other_loads[1:]:
            load.wait()
        query_copy.wait_recv()

    def rotate_queries(first, count):
        def head(i, carry):
            cols = pl.ds(pl.multiple_of(i * HEAD_DIM, HEAD_DIM), HEAD_DIM)

            def tile(t, carry):
                rows = pl.ds(pl.multiple_of(t * 128, 128), 128)
                qbuf[rows, cols] = rotated(qbuf[rows, cols].astype(jnp.float32), rows)
                return carry

            return lax.fori_loop(0, length // 128, tile, carry)

        lax.fori_loop(first, first + count, head, 0)

    def make_bias():
        first = doc_ref[0]
        row = lax.broadcasted_iota(jnp.int32, (length, length), 0)
        col = lax.broadcasted_iota(jnp.int32, (length, length), 1)
        visible = (col <= row) & ((col >= first) | (row < first))
        bias[...] = jnp.where(visible, 0.0, MASKED)

    def finish_keys():
        def tile(t, carry):
            rows = pl.ds(pl.multiple_of(t * 128, 128), 128)
            for h in range(2):
                kbuf[h, rows, :] = rotated(acc[0, rows, h * HEAD_DIM:(h + 1) * HEAD_DIM], rows)
            return carry

        lax.fori_loop(0, length // 128, tile, 0)

    factor = HEAD_DIM ** -0.5 * 1.4426950408889634

    def weigh(first, count):
        h = first // GROUP

        def head(i, carry):
            cols = pl.ds(pl.multiple_of(i * HEAD_DIM, HEAD_DIM), HEAD_DIM)
            for block in range(2):
                rows = slice(block * own_rows, (block + 1) * own_rows)
                keys = (block + 1) * own_rows
                scores = lax.dot_general(
                    qbuf[rows, cols], kbuf[h, :keys, :], (((1,), (1,)), ((), ())),
                    preferred_element_type=jnp.float32,
                ) * factor + bias[rows, :keys]
                probs = jnp.exp2(scores - jnp.max(scores, axis=1, keepdims=True))
                total = jnp.sum(probs, axis=1, keepdims=True)
                pbuf[i, rows, :keys] = probs.astype(jnp.bfloat16)
                inverse[i, rows, :] = jnp.broadcast_to(1.0 / total, (own_rows, HEAD_DIM))
            return carry

        lax.fori_loop(first, first + count, head, 0)

    def mix(first, count):
        h = first // GROUP

        def head(i, carry):
            cols = pl.ds(pl.multiple_of(i * HEAD_DIM, HEAD_DIM), HEAD_DIM)
            for block in range(2):
                rows = slice(block * own_rows, (block + 1) * own_rows)
                keys = (block + 1) * own_rows
                mixed = jnp.dot(
                    pbuf[i, rows, :keys], vbuf[:keys, h * HEAD_DIM:(h + 1) * HEAD_DIM],
                    preferred_element_type=jnp.float32,
                )
                obuf[rows, cols] = (mixed * inverse[i, rows, :]).astype(jnp.bfloat16)
            return carry

        lax.fori_loop(first, first + count, head, 0, unroll=count)

    def out_copies(h):
        width = half_cols // OUT_GROUPS
        source = pl.ds(h * width, width)
        target = out_ref.at[0, :, pl.ds(pl.multiple_of(c * half_cols + h * width, width), width)]
        return (
            pltpu.make_async_copy(obuf.at[own, source], target, out_sem.at[h]),
            pltpu.make_async_remote_copy(
                src_ref=obuf.at[other, source], dst_ref=target, send_sem=out_send.at[h],
                recv_sem=out_recv.at[h], device_id=pair, device_id_type=MESH,
            ),
        )

    def send_out(h):
        for one in out_copies(h):
            one.start()

    query_copy = pltpu.make_async_remote_copy(
        src_ref=queries_ref.at[0, :, other_cols], dst_ref=qbuf.at[own, :], send_sem=pair_send.at[0],
        recv_sem=pair_recv.at[0], device_id=pair, device_id_type=MESH,
    )
    normed_copy = pltpu.make_async_remote_copy(
        src_ref=normed_ref.at[0], dst_ref=xbuf.at[own, :], send_sem=pair_send.at[1],
        recv_sem=pair_recv.at[1], device_id=pair, device_id_type=MESH,
    )

    def begin():
        for load in other_loads:
            load.start()
        query_copy.start()
        normed_copy.start()

    def clear():
        acc[...] = jnp.zeros_like(acc)
        make_bias()

    def wait_normed():
        other_loads[0].wait()
        normed_copy.wait_recv()

    def add_place(h, k, o):
        if h == 1 and k == 1:
            pl.when(middle == 1)(lambda: add_shard(h, place(k, o)))
        else:
            add_shard(h, place(k, o))

    if twins:
        steps = {
            "load": lambda h: weight_loads[h].wait(),
            "begin": begin,
            "clear": clear,
            "queries": wait_queries,
            "rotate": rotate_queries,
            "normed": wait_normed,
            "add": add_place,
            "keys": finish_keys,
            "weigh": weigh,
        }
        sent = [0, 0]
        held = [set(), set()]
        for name, operands, *moves in SCHEDULE:
            for role in range(2):
                @pl.when(middle == role)
                def _(role=role):
                    for link, *which in moves[role]:
                        h, k, o, j = which
                        if (k or o) and tuple(which) not in held[role]:
                            held[role].add(tuple(which))
                            arrive(h, k, o, j)
                        if link < WAIT:
                            if h == SHARES:
                                make_share(j)
                            send(sent[role], link, h, k, o, j).start()
                            sent[role] += 1
            if name:
                steps[name](*operands)
    else:
        send_own(0)
        begin()
        clear()
        wait_queries()
        rotate_queries(0, half_cols // HEAD_DIM)
        send_own(1)
        wait_normed()
        for h in range(PHASES):
            add_shard(h, f)

            def step(d, carry, h=h):
                forward_z(h, d)
                add_same(h, d)
                return carry

            lax.fori_loop(1, nz, step, 0)
            if h == 0:
                finish_keys()
                weigh(0, 8)
                weigh(8, 8)
    finish_values()
    heads = 2 * GROUP // OUT_GROUPS
    for group in range(OUT_GROUPS):
        mix(group * heads, heads)
        send_out(group)

    if twins:
        for role in range(2):
            @pl.when(middle == role)
            def _(role=role):
                moves = [move for step in SCHEDULE for move in step[2 + role] if move[0] < WAIT]
                for index, move in enumerate(moves):
                    send(index, *move).wait_send()
                if role == 1:
                    for j in range(CHUNKS):
                        pass_guest(j).wait_send()
    else:
        for h in range(PHASES):
            drain_own(h)

            def drain(d, carry, h=h):
                drain_sends(h, d)
                return carry

            lax.fori_loop(1, nz, drain, 0)
    query_copy.wait_send()
    normed_copy.wait_send()
    for group in range(OUT_GROUPS):
        local, remote = out_copies(group)
        local.wait()
        remote.wait()


def body(groups, shards, normed, queries, key_weight, value_weight, doc_start):
    _, rows, width = normed.shape
    depth = key_weight.shape[0]
    query_cols = queries.shape[2]
    length = 2 * rows
    twins = paired(groups, shards)
    parts = PARTS if twins else 1
    sends = max(sum(move[0] < WAIT for step in SCHEDULE for move in step[role]) for role in (2, 3))
    cosine, sine = rotary_tables(length)
    dma = pltpu.SemaphoreType.DMA
    hbm = pl.BlockSpec(memory_space=pl.ANY)
    return pl.pallas_call(
        functools.partial(kernel, groups, shards),
        out_shape=jax.ShapeDtypeStruct((1, rows, query_cols), jnp.bfloat16),
        in_specs=[pl.BlockSpec(memory_space=pltpu.SMEM)] + [hbm] * 6,
        out_specs=hbm,
        scratch_shapes=[
            pltpu.VMEM((PHASES, shards, depth, 2 * HEAD_DIM), jnp.bfloat16),
            pltpu.VMEM((length, width), jnp.bfloat16),
            pltpu.VMEM((length, query_cols // 2), jnp.bfloat16),
            pltpu.VMEM((length, query_cols // 2), jnp.bfloat16),
            pltpu.VMEM((2 * GROUP, length, length), jnp.bfloat16),
            pltpu.VMEM((2 * GROUP, length, HEAD_DIM), jnp.float32),
            pltpu.VMEM((PHASES, length, 2 * HEAD_DIM), jnp.float32),
            pltpu.VMEM((2, length, HEAD_DIM), jnp.bfloat16),
            pltpu.VMEM((length, 2 * HEAD_DIM), jnp.bfloat16),
            pltpu.VMEM((length, length), jnp.float32),
            pltpu.VMEM((length, HEAD_DIM), jnp.float32),
            pltpu.VMEM((length, HEAD_DIM), jnp.float32),
            pltpu.VMEM((2, CHUNKS, rows // CHUNKS, 2 * depth if twins else HEAD_DIM), jnp.bfloat16),
            pltpu.VMEM((CHUNKS, 2, rows // CHUNKS, 2 * HEAD_DIM), SHARE_TYPE),
            pltpu.VMEM((CHUNKS, 2, rows // CHUNKS, 2 * HEAD_DIM), SHARE_TYPE),
            dma((6,)),
            dma((PHASES, shards, parts)),
            dma((sends if twins else PHASES * shards * 2,)),
            dma((3, CHUNKS)),
            dma((CHUNKS,)),
            dma((2,)),
            dma((2,)),
            dma((OUT_GROUPS,)),
            dma((OUT_GROUPS,)),
            dma((OUT_GROUPS,)),
        ],
        compiler_params=pltpu.CompilerParams(
            collective_id=0, has_side_effects=True, vmem_limit_bytes=56 * 1024 * 1024
        ),
    )(doc_start, normed, queries, key_weight, value_weight, jnp.asarray(cosine), jnp.asarray(sine))


def solution(mesh):
    placed = (
        P(("group", "fsdp"), "ctx", None),
        P(("group", "fsdp"), "ctx", None),
        P("fsdp", None),
        P("fsdp", None),
        P(("group", "fsdp")),
    )
    return jax.shard_map(
        functools.partial(body, mesh.shape["group"], mesh.shape["fsdp"]),
        mesh=mesh,
        in_specs=placed,
        out_specs=P(("group", "fsdp"), "ctx", None),
        check_vma=False,
    )
```

```python
import functools

import jax
import jax.numpy as jnp
import numpy as np
from jax import lax
from jax.experimental import pallas as pl
from jax.experimental.pallas import tpu as pltpu
from jax.sharding import PartitionSpec as P

HEAD_DIM = 128
GROUP = 8
THETA = 500000.0
MASKED = -1e30
MESH = pl.DeviceIdType.MESH
PHASES = 2
OUT_GROUPS = 4
PARTS = 8
WAIT = 4
DOUBLE = 8
CHUNKS = 4
ROWS, SHARES = 2, 3
SHARE_TYPE = jnp.bfloat16
SCHEDULE = (
    ("load", (0,), (), ()),
    ("begin", (), ((0, 0, 0, 0, 0), (10, 0, 0, 0, 0), (0, 0, 0, 0, 3)), ((8, 0, 0, 0, 0), (1, 0, 0, 0, 0), (10, 0, 0, 0, 0), (1, 0, 0, 0, 1), (10, 0, 0, 0, 2), (8, 0, 0, 0, 3), (9, 0, 0, 0, 3), (4, 0, 1, 0, 0), (3, 0, 1, 0, 0))),
    ("load", (1,), (), ()),
    ("clear", (), ((10, 1, 0, 0, 0), (2, 1, 0, 0, 2), (2, 0, 0, 0, 5), (8, 0, 0, 0, 1), (0, 1, 0, 0, 3)), ()),
    ("queries", (), ((8, 0, 0, 0, 4), (4, 0, 1, 0, 0), (3, 0, 1, 0, 0), (4, 0, 1, 0, 1), (3, 0, 1, 0, 1), (12, 0, 0, 1, 0), (11, 0, 0, 1, 0), (0, 1, 0, 0, 2), (10, 0, 1, 0, 0), (4, 1, 0, 1, 2), (3, 1, 0, 1, 2), (12, 1, 0, 1, 0), (3, 1, 0, 1, 0), (8, 1, 0, 0, 0), (12, 0, 2, 0, 0), (10, 0, 2, 0, 0)), ((0, 0, 1, 0, 0), (4, 0, 1, 0, 3), (2, 0, 1, 0, 3), (12, 0, 2, 0, 0), (9, 0, 2, 0, 0), (2, 0, 1, 0, 0), (0, 0, 0, 0, 5), (12, 0, 0, 1, 0), (11, 0, 0, 1, 0), (12, 0, 1, 0, 1), (0, 0, 1, 0, 1), (1, 0, 0, 0, 2))),
    ("rotate", (0, 2), ((3, 0, 2, 0, 0), (2, 0, 0, 0, 4), (4, 0, 1, 0, 2), (12, 0, 1, 0, 3), (10, 0, 1, 0, 2), (12, 0, 1, 1, 0), (11, 0, 1, 1, 0), (0, 0, 0, 0, 6), (8, 1, 0, 0, 4)), ((0, 0, 0, 0, 2), (10, 0, 1, 0, 1), (10, 0, 2, 0, 0), (12, 0, 0, 1, 2), (11, 0, 0, 1, 2), (4, 0, 3, 0, 0), (1, 0, 3, 0, 0), (4, 0, 1, 1, 3), (3, 0, 1, 1, 3), (8, 0, 1, 0, 2), (12, 0, 2, 0, 3), (1, 0, 2, 0, 3))),
    ("rotate", (2, 2), ((4, 0, 3, 0, 0), (4, 0, 3, 0, 1), (11, 0, 3, 0, 0), (0, 2, 0, 0, 0), (8, 1, 0, 0, 6), (12, 0, 2, 1, 0), (11, 0, 2, 1, 0), (10, 0, 3, 0, 0), (12, 0, 1, 1, 2), (11, 0, 1, 1, 2), (4, 0, 2, 0, 2), (4, 0, 2, 0, 3), (10, 0, 2, 0, 2), (0, 2, 0, 0, 2), (12, 0, 3, 0, 2), (10, 0, 3, 0, 2), (12, 0, 3, 1, 0), (11, 0, 3, 1, 0)), ((3, 0, 2, 0, 0), (4, 0, 3, 0, 1), (1, 0, 3, 0, 1), (4, 0, 2, 0, 2), (10, 0, 2, 0, 2), (12, 0, 1, 1, 1), (11, 0, 1, 1, 1), (8, 1, 0, 0, 0), (3, 0, 3, 0, 0), (1, 0, 2, 0, 2), (4, 0, 2, 0, 5), (9, 0, 2, 0, 4), (12, 0, 1, 0, 4), (8, 0, 1, 0, 4), (10, 0, 3, 0, 0), (12, 1, 1, 0, 0), (0, 1, 1, 0, 0), (0, 1, 0, 0, 2), (12, 0, 3, 0, 2), (10, 0, 3, 0, 2), (0, 0, 0, 0, 6), (4, 0, 1, 1, 0), (3, 0, 1, 1, 0), (12, 0, 2, 1, 0), (11, 0, 2, 1, 0), (9, 0, 3, 0, 2), (1, 0, 0, 0, 5), (2, 1, 1, 0, 1), (12, 0, 2, 1, 2), (11, 0, 2, 1, 2))),
    ("rotate", (4, 2), (), ()),
    ("rotate", (6, 2), (), ()),
    ("rotate", (8, 2), (), ()),
    ("rotate", (10, 2), (), ()),
    ("rotate", (12, 2), (), ()),
    ("rotate", (14, 2), ((12, 0, 2, 1, 2), (11, 0, 2, 1, 2), (0, 2, 0, 0, 1), (2, 0, 0, 0, 3), (4, 1, 2, 0, 0), (2, 1, 2, 0, 0), (2, 0, 0, 0, 2), (12, 0, 3, 1, 2), (11, 0, 3, 1, 2), (10, 1, 0, 0, 3), (3, 1, 0, 1, 1), (0, 2, 0, 0, 3)), ((4, 1, 1, 0, 2), (8, 1, 1, 0, 1), (12, 1, 2, 0, 0), (1, 1, 2, 0, 0), (10, 1, 0, 0, 0), (10, 1, 0, 0, 2), (12, 0, 3, 0, 4), (9, 0, 3, 0, 4), (4, 0, 1, 0, 6), (0, 0, 1, 0, 6), (12, 0, 3, 1, 0), (11, 0, 3, 1, 0), (4, 1, 2, 0, 2), (1, 1, 2, 0, 2), (8, 1, 0, 0, 3), (2, 1, 2, 0, 0), (4, 1, 1, 0, 3), (10, 1, 1, 0, 2), (12, 0, 3, 1, 2), (11, 0, 3, 1, 2), (12, 1, 1, 0, 4), (8, 1, 1, 0, 3), (4, 0, 2, 0, 6), (1, 0, 2, 0, 6), (1, 1, 2, 0, 1), (0, 1, 0, 0, 7), (4, 1, 3, 0, 0), (1, 1, 3, 0, 0))),
    ("normed", (), (), ()),
    ("add", (0, 0, 0), (), ()),
    ("add", (1, 0, 0), (), ()),
    ("add", (0, 1, 1), ((12, 0, 1, 1, 6), (12, 0, 1, 1, 4)), ((4, 0, 1, 1, 7), (12, 0, 1, 1, 5), (4, 0, 1, 1, 4))),
    ("add", (0, 1, 0), ((4, 0, 1, 0, 7), (4, 0, 1, 0, 6), (4, 0, 1, 0, 5)), ((4, 0, 1, 0, 7),)),
    ("add", (0, 2, 1), ((12, 0, 2, 1, 6), (12, 0, 2, 1, 4)), ((12, 0, 2, 1, 6), (12, 0, 2, 1, 4))),
    ("add", (0, 0, 1), ((4, 1, 2, 0, 1), (4, 1, 2, 0, 2), (11, 1, 2, 0, 1), (3, 1, 2, 0, 0), (10, 1, 2, 0, 1), (4, 0, 0, 1, 2), (12, 0, 0, 1, 6), (4, 0, 0, 1, 3), (4, 0, 0, 1, 4), (4, 0, 0, 1, 5)), ((2, 1, 1, 0, 0), (12, 1, 3, 0, 1), (9, 1, 3, 0, 1), (12, 1, 0, 1, 0), (11, 1, 0, 1, 0), (12, 1, 1, 0, 6), (8, 1, 1, 0, 5), (10, 1, 2, 0, 1), (12, 0, 0, 1, 6), (12, 0, 0, 1, 4))),
    ("add", (0, 2, 0), ((12, 0, 2, 0, 4), (4, 0, 2, 0, 7), (4, 0, 2, 0, 6)), ((2, 1, 3, 0, 1), (12, 1, 0, 1, 2), (11, 1, 0, 1, 2), (2, 1, 3, 0, 0), (4, 0, 2, 0, 7))),
    ("add", (0, 3, 0), ((12, 0, 3, 0, 4), (12, 0, 3, 0, 6)), ((4, 0, 3, 0, 6), (4, 0, 3, 0, 7))),
    ("add", (0, 3, 1), ((12, 0, 3, 1, 6), (12, 0, 3, 1, 4)), ((12, 0, 3, 1, 6), (12, 0, 3, 1, 4))),
    ("keys", (), (), ()),
    ("weigh", (0, 2), (), ()),
    ("weigh", (2, 2), ((4, 1, 3, 0, 0), (12, 1, 3, 0, 1), (10, 1, 3, 0, 0), (2, 1, 3, 0, 2), (4, 1, 2, 1, 0), (3, 1, 2, 1, 0)), ((12, 1, 3, 0, 3), (9, 1, 3, 0, 3), (12, 1, 2, 0, 3), (9, 1, 2, 0, 3), (12, 1, 1, 1, 2), (11, 1, 1, 1, 2))),
    ("weigh", (4, 2), ((12, 1, 2, 1, 1), (11, 1, 2, 1, 1), (3, 1, 3, 0, 0)), ((4, 1, 1, 1, 0), (4, 1, 1, 1, 1), (11, 1, 1, 1, 0), (4, 2, 1, 0, 0), (10, 1, 3, 0, 2))),
    ("weigh", (6, 2), (), ()),
    ("weigh", (8, 2), (), ()),
    ("weigh", (10, 2), ((12, 1, 3, 0, 3), (2, 1, 3, 0, 3), (12, 1, 3, 1, 0), (11, 1, 3, 1, 0), (12, 1, 2, 0, 3), (10, 1, 2, 0, 3)), ((0, 1, 0, 0, 6), (4, 2, 1, 0, 1), (4, 2, 1, 0, 2), (10, 1, 2, 0, 3), (12, 1, 3, 0, 5), (9, 1, 3, 0, 5), (12, 1, 0, 1, 6), (12, 1, 0, 1, 4), (1, 3, 0, 0, 0), (4, 1, 2, 1, 0), (12, 1, 2, 1, 1), (11, 1, 2, 1, 0), (0, 1, 0, 0, 5), (1, 3, 0, 0, 1), (10, 1, 3, 0, 4))),
    ("weigh", (12, 2), (), ()),
    ("weigh", (14, 2), ((2, 1, 3, 0, 4), (4, 1, 3, 1, 2), (3, 1, 3, 1, 2)), ((3, 1, 2, 1, 2), (4, 1, 3, 1, 0), (4, 1, 3, 1, 1), (11, 1, 3, 1, 0), (1, 3, 0, 0, 2), (4, 2, 1, 0, 3), (0, 1, 1, 0, 7))),
    ("add", (1, 1, 1), (), ((12, 1, 1, 1, 6), (12, 1, 1, 1, 4))),
    ("add", (1, 2, 0), ((4, 1, 2, 0, 7), (12, 1, 2, 0, 5)), ((1, 3, 0, 0, 3), (4, 1, 2, 0, 5), (4, 1, 2, 0, 6), (4, 1, 2, 0, 7))),
    ("add", (1, 1, 0), (), ()),
    ("add", (1, 0, 1), ((12, 1, 0, 1, 3), (4, 1, 0, 1, 7), (4, 1, 0, 1, 6), (4, 1, 0, 1, 5)), ()),
    ("add", (1, 2, 1), ((12, 1, 2, 1, 3), (4, 1, 2, 1, 7), (12, 1, 2, 1, 5)), ((12, 1, 2, 1, 3), (12, 1, 2, 1, 6), (4, 1, 2, 1, 5))),
    ("add", (1, 3, 0), ((4, 1, 3, 0, 7), (12, 1, 3, 0, 5)), ((4, 1, 3, 0, 7),)),
    ("add", (1, 3, 1), ((4, 1, 3, 1, 3), (12, 1, 3, 1, 6), (4, 1, 3, 1, 4), (4, 1, 3, 1, 5)), ((12, 1, 3, 1, 2), (12, 1, 3, 1, 6), (12, 1, 3, 1, 4))),
    ("", (), ((4, 3, 1, 0, 0), (4, 3, 1, 0, 1), (4, 3, 1, 0, 2), (4, 3, 1, 0, 3)), ()),
    ("", (), (), ()),
)


def paired(groups, shards):
    return groups == 2 and shards == 8


def rotary_tables(length):
    half = HEAD_DIM // 2
    exponent = -np.arange(half, dtype=np.float32) * np.float32(2.0) / np.float32(HEAD_DIM)
    frequency = np.power(np.float32(THETA), exponent, dtype=np.float32)
    angles = np.arange(length, dtype=np.float32)[:, None] * frequency[None, :]
    cosine, sine = np.cos(angles).astype(np.float32), np.sin(angles).astype(np.float32)
    return np.concatenate([cosine, cosine], 1), np.concatenate([-sine, sine], 1)


def kernel(
    groups, shards, doc_ref, normed_ref, queries_ref, key_ref, value_ref, cos_hbm, sin_hbm, out_ref,
    wbuf, xbuf, qbuf, obuf, pbuf, inverse, acc, kbuf, vbuf, bias, cos_ref, sin_ref,
    guest, share_out, share_in, load_sem, recv_sem, send_sem, guest_sem, share_sem, pair_send, pair_recv, out_sem, out_send, out_recv,
):
    twins = paired(groups, shards)
    ny = 2 if twins else 1
    nz = shards // ny
    parts = PARTS if twins else 1
    g, f, c = lax.axis_index("group"), lax.axis_index("fsdp"), lax.axis_index("ctx")
    z, y = f // ny, f % ny
    own_rows, depth = normed_ref.shape[1], key_ref.shape[0]
    length = 2 * own_rows
    piece_rows = depth // parts
    half_cols = queries_ref.shape[2] // 2
    pair = (g, f, 1 - c)
    up, down = (g, f + ny, c), (g, f - ny, c)
    if twins:
        y_dev, x_dev = (g, z * 2 + 1 - y, c), (1 - g, f, c)

    def shard(zs, ys):
        return zs * ny + ys

    def part(j, count=1):
        return g * (parts - count) + j * (1 - 2 * g) if twins else 0

    def copy(h, s, q, send_sem, device, count=1):
        ref = wbuf.at[h, s, pl.ds(pl.multiple_of(q * piece_rows, piece_rows), count * piece_rows), :]
        return pltpu.make_async_remote_copy(
            src_ref=ref, dst_ref=ref, send_sem=send_sem, recv_sem=recv_sem.at[h, s, q],
            device_id=device, device_id_type=MESH,
        )

    middle = (z + 1) // 2 % 2
    inward = 1 - 2 * (z // 2)

    def place(k, o):
        zs = z if k == 0 else z + inward * (k - middle * (2 if k == 1 else 1))
        return shard(zs, 1 - y if o else y)

    def wait_piece(h, s, j, count=1):
        q = part(j, count)
        copy(h, s, q, recv_sem.at[h, s, q], pair, count).wait_recv()

    chunk = own_rows // CHUNKS

    def remote(source, target, send_sem, recv_sem, device):
        return pltpu.make_async_remote_copy(
            src_ref=source, dst_ref=target, send_sem=send_sem, recv_sem=recv_sem, device_id=device, device_id_type=MESH,
        )

    def send(index, move):
        code, h, k, o, j = move
        link, count = code % DOUBLE, code // DOUBLE + 1
        near, far = (g, f + inward * ny, c), (g, f - inward * ny, c)
        device = near if link == 0 else far if link == 1 else y_dev if link == 2 else x_dev
        done = send_sem.at[index]
        if h == ROWS:
            start = pl.multiple_of((z + inward) * ny * depth, ny * depth)
            source = normed_ref.at[0, pl.ds(j * chunk, chunk), pl.ds(start, ny * depth)]
            return remote(source, guest.at[c, j], done, guest_sem.at[0, j], device)
        if h == SHARES:
            return remote(share_out.at[j], share_in.at[j], done, share_sem.at[j], device)
        return copy(h, place(k, o), part(j, count), done, device, count)

    def pass_guest(j):
        ref = guest.at[c, j]
        return remote(ref, ref, guest_sem.at[1, j], guest_sem.at[2, j], pair)

    def arrive(h, k, o, j, count):
        if h == ROWS:
            remote(guest.at[c, j], guest.at[c, j], guest_sem.at[1, j], guest_sem.at[0, j], pair).wait_recv()
            pass_guest(j).start()
        elif h == SHARES:
            remote(share_in.at[j], share_in.at[j], share_sem.at[j], share_sem.at[j], pair).wait_recv()
        else:
            wait_piece(h, place(k, o), j, count)

    def make_share(j):
        pass_guest(j).wait_recv()
        for side in range(2):
            total = jnp.zeros((chunk, 2 * HEAD_DIM), jnp.float32)
            for ys in range(ny):
                total += jnp.dot(
                    guest[side, j, :, ys * depth:(ys + 1) * depth], wbuf[1, shard(z, ys)],
                    preferred_element_type=jnp.float32,
                )
            share_out[j, side] = total.astype(SHARE_TYPE)

    def finish_values():
        vbuf[...] = acc[1].astype(jnp.bfloat16)

        if twins:
            @pl.when(middle == 0)
            def _():
                for j in range(CHUNKS):
                    for side in range(2):
                        rows = slice(side * own_rows + j * chunk, side * own_rows + (j + 1) * chunk)
                        vbuf[rows, :] = (acc[1, rows, :] + share_in[j, side].astype(jnp.float32)).astype(jnp.bfloat16)

    def z_copy(h, zs, way):
        return copy(h, zs, 0, send_sem.at[(h * nz + zs) * 2 + way], up if way == 0 else down)

    head_cols = pl.ds(pl.multiple_of(c * 2 * HEAD_DIM, 2 * HEAD_DIM), 2 * HEAD_DIM)
    weight_loads = [
        pltpu.make_async_copy(ref.at[:, head_cols], wbuf.at[h, f], load_sem.at[h])
        for h, ref in enumerate((key_ref, value_ref))
    ]
    own = pl.ds(pl.multiple_of(c * own_rows, own_rows), own_rows)
    other = pl.ds(pl.multiple_of((1 - c) * own_rows, own_rows), own_rows)
    my_cols = pl.ds(pl.multiple_of(c * half_cols, half_cols), half_cols)
    other_cols = pl.ds(pl.multiple_of((1 - c) * half_cols, half_cols), half_cols)
    other_loads = [
        pltpu.make_async_copy(normed_ref.at[0], xbuf.at[own, :], load_sem.at[2]),
        pltpu.make_async_copy(queries_ref.at[0, :, my_cols], qbuf.at[own, :], load_sem.at[3]),
        pltpu.make_async_copy(cos_hbm, cos_ref, load_sem.at[4]),
        pltpu.make_async_copy(sin_hbm, sin_ref, load_sem.at[5]),
    ]
    for load in weight_loads:
        load.start()

    barrier = pltpu.get_barrier_semaphore()
    pl.semaphore_signal(barrier, inc=1, device_id=pair, device_id_type=MESH)
    if twins:
        pl.semaphore_signal(barrier, inc=1, device_id=y_dev, device_id_type=MESH)
        pl.semaphore_signal(barrier, inc=1, device_id=x_dev, device_id_type=MESH)

    @pl.when(z < nz - 1)
    def _():
        pl.semaphore_signal(barrier, inc=1, device_id=up, device_id_type=MESH)

    @pl.when(z > 0)
    def _():
        pl.semaphore_signal(barrier, inc=1, device_id=down, device_id_type=MESH)

    line_peers = jnp.where(z > 0, 1, 0) + jnp.where(z < nz - 1, 1, 0)
    pl.semaphore_wait(barrier, (3 if twins else 1) + line_peers)

    def send_own(h):
        weight_loads[h].wait()

        @pl.when(z < nz - 1)
        def _():
            z_copy(h, z, 0).start()

        @pl.when(z > 0)
        def _():
            z_copy(h, z, 1).start()

    def each_way(d, action):
        @pl.when(z - d >= 0)
        def _():
            action(z - d, 0)

        @pl.when(z + d < nz)
        def _():
            action(z + d, 1)

    def passes_on(way):
        return z < nz - 1 if way == 0 else z > 0

    def forward_z(h, d):
        def one(zs, way):
            wait_piece(h, zs, 0)

            @pl.when(passes_on(way))
            def _():
                z_copy(h, zs, way).start()

        each_way(d, one)

    def drain_sends(h, d):
        def one(zs, way):
            @pl.when(passes_on(way))
            def _():
                z_copy(h, zs, way).wait_send()

        each_way(d, one)

    def drain_own(h):
        @pl.when(z < nz - 1)
        def _():
            z_copy(h, z, 0).wait_send()

        @pl.when(z > 0)
        def _():
            z_copy(h, z, 1).wait_send()

    def add_shard(h, s):
        columns = pl.ds(pl.multiple_of(s * depth, depth), depth)

        def tile(t, carry):
            rows = pl.ds(pl.multiple_of(t * 256, 256), 256)
            acc[h, rows, :] += jnp.dot(xbuf[rows, columns], wbuf[h, s], preferred_element_type=jnp.float32)
            return carry

        lax.fori_loop(0, length // 256, tile, 0)

    def add_same(h, d):
        each_way(d, lambda zs, way: add_shard(h, zs))

    def rotated(u, rows):
        return (u * cos_ref[rows, :] + pltpu.roll(u, HEAD_DIM // 2, 1) * sin_ref[rows, :]).astype(jnp.bfloat16)

    def wait_queries():
        for load in other_loads[1:]:
            load.wait()
        query_copy.wait_recv()

    def rotate_queries(first, count):
        def head(i, carry):
            cols = pl.ds(pl.multiple_of(i * HEAD_DIM, HEAD_DIM), HEAD_DIM)

            def tile(t, carry):
                rows = pl.ds(pl.multiple_of(t * 128, 128), 128)
                qbuf[rows, cols] = rotated(qbuf[rows, cols].astype(jnp.float32), rows)
                return carry

            return lax.fori_loop(0, length // 128, tile, carry)

        lax.fori_loop(first, first + count, head, 0)

    def make_bias():
        first = doc_ref[0]
        row = lax.broadcasted_iota(jnp.int32, (length, length), 0)
        col = lax.broadcasted_iota(jnp.int32, (length, length), 1)
        visible = (col <= row) & ((col >= first) | (row < first))
        bias[...] = jnp.where(visible, 0.0, MASKED)

    def finish_keys():
        def tile(t, carry):
            rows = pl.ds(pl.multiple_of(t * 128, 128), 128)
            for h in range(2):
                kbuf[h, rows, :] = rotated(acc[0, rows, h * HEAD_DIM:(h + 1) * HEAD_DIM], rows)
            return carry

        lax.fori_loop(0, length // 128, tile, 0)

    factor = HEAD_DIM ** -0.5 * 1.4426950408889634

    def weigh(first, count):
        h = first // GROUP

        def head(i, carry):
            cols = pl.ds(pl.multiple_of(i * HEAD_DIM, HEAD_DIM), HEAD_DIM)
            for block in range(2):
                rows = slice(block * own_rows, (block + 1) * own_rows)
                keys = (block + 1) * own_rows
                scores = lax.dot_general(
                    qbuf[rows, cols], kbuf[h, :keys, :], (((1,), (1,)), ((), ())),
                    preferred_element_type=jnp.float32,
                ) * factor + bias[rows, :keys]
                probs = jnp.exp2(scores - jnp.max(scores, axis=1, keepdims=True))
                total = jnp.sum(probs, axis=1, keepdims=True)
                pbuf[i, rows, :keys] = probs.astype(jnp.bfloat16)
                inverse[i, rows, :] = jnp.broadcast_to(1.0 / total, (own_rows, HEAD_DIM))
            return carry

        lax.fori_loop(first, first + count, head, 0)

    def mix(first, count):
        h = first // GROUP

        def head(i, carry):
            cols = pl.ds(pl.multiple_of(i * HEAD_DIM, HEAD_DIM), HEAD_DIM)
            for block in range(2):
                rows = slice(block * own_rows, (block + 1) * own_rows)
                keys = (block + 1) * own_rows
                mixed = jnp.dot(
                    pbuf[i, rows, :keys], vbuf[:keys, h * HEAD_DIM:(h + 1) * HEAD_DIM],
                    preferred_element_type=jnp.float32,
                )
                obuf[rows, cols] = (mixed * inverse[i, rows, :]).astype(jnp.bfloat16)
            return carry

        lax.fori_loop(first, first + count, head, 0, unroll=count)

    def out_copies(h):
        width = half_cols // OUT_GROUPS
        source = pl.ds(h * width, width)
        target = out_ref.at[0, :, pl.ds(pl.multiple_of(c * half_cols + h * width, width), width)]
        return (
            pltpu.make_async_copy(obuf.at[own, source], target, out_sem.at[h]),
            pltpu.make_async_remote_copy(
                src_ref=obuf.at[other, source], dst_ref=target, send_sem=out_send.at[h],
                recv_sem=out_recv.at[h], device_id=pair, device_id_type=MESH,
            ),
        )

    def send_out(h):
        for one in out_copies(h):
            one.start()

    query_copy = pltpu.make_async_remote_copy(
        src_ref=queries_ref.at[0, :, other_cols], dst_ref=qbuf.at[own, :], send_sem=pair_send.at[0],
        recv_sem=pair_recv.at[0], device_id=pair, device_id_type=MESH,
    )
    normed_copy = pltpu.make_async_remote_copy(
        src_ref=normed_ref.at[0], dst_ref=xbuf.at[own, :], send_sem=pair_send.at[1],
        recv_sem=pair_recv.at[1], device_id=pair, device_id_type=MESH,
    )

    def begin():
        for load in other_loads:
            load.start()
        query_copy.start()
        normed_copy.start()

    def clear():
        acc[...] = jnp.zeros_like(acc)
        make_bias()

    def wait_normed():
        other_loads[0].wait()
        normed_copy.wait_recv()

    def add_place(h, k, o):
        if h == 1 and k == 1:
            pl.when(middle == 1)(lambda: add_shard(h, place(k, o)))
        else:
            add_shard(h, place(k, o))

    if twins:
        steps = {
            "load": lambda h: weight_loads[h].wait(),
            "begin": begin,
            "clear": clear,
            "queries": wait_queries,
            "rotate": rotate_queries,
            "normed": wait_normed,
            "add": add_place,
            "keys": finish_keys,
            "weigh": weigh,
        }
        sent = [0, 0]
        for name, operands, *moves in SCHEDULE:
            for role in range(2):
                @pl.when(middle == role)
                def _(role=role):
                    for move in moves[role]:
                        code, h, k, o, j = move
                        if code % DOUBLE == WAIT:
                            arrive(h, k, o, j, code // DOUBLE + 1)
                        else:
                            if h == SHARES:
                                make_share(j)
                            send(sent[role], move).start()
                            sent[role] += 1
            if name:
                steps[name](*operands)
    else:
        send_own(0)
        begin()
        clear()
        wait_queries()
        rotate_queries(0, half_cols // HEAD_DIM)
        send_own(1)
        wait_normed()
        for h in range(PHASES):
            add_shard(h, f)

            def step(d, carry, h=h):
                forward_z(h, d)
                add_same(h, d)
                return carry

            lax.fori_loop(1, nz, step, 0)
            if h == 0:
                finish_keys()
                weigh(0, 8)
                weigh(8, 8)
    finish_values()
    heads = 2 * GROUP // OUT_GROUPS
    for group in range(OUT_GROUPS):
        mix(group * heads, heads)
        send_out(group)

    if twins:
        for role in range(2):
            @pl.when(middle == role)
            def _(role=role):
                moves = [move for step in SCHEDULE for move in step[2 + role] if move[0] % DOUBLE < WAIT]
                for index, move in enumerate(moves):
                    send(index, move).wait_send()
                if role == 1:
                    for j in range(CHUNKS):
                        pass_guest(j).wait_send()
    else:
        for h in range(PHASES):
            drain_own(h)

            def drain(d, carry, h=h):
                drain_sends(h, d)
                return carry

            lax.fori_loop(1, nz, drain, 0)
    query_copy.wait_send()
    normed_copy.wait_send()
    for group in range(OUT_GROUPS):
        local, remote = out_copies(group)
        local.wait()
        remote.wait()


def body(groups, shards, normed, queries, key_weight, value_weight, doc_start):
    _, rows, width = normed.shape
    depth = key_weight.shape[0]
    query_cols = queries.shape[2]
    length = 2 * rows
    twins = paired(groups, shards)
    parts = PARTS if twins else 1
    sends = max(sum(move[0] % DOUBLE < WAIT for step in SCHEDULE for move in step[role]) for role in (2, 3))
    cosine, sine = rotary_tables(length)
    dma = pltpu.SemaphoreType.DMA
    hbm = pl.BlockSpec(memory_space=pl.ANY)
    return pl.pallas_call(
        functools.partial(kernel, groups, shards),
        out_shape=jax.ShapeDtypeStruct((1, rows, query_cols), jnp.bfloat16),
        in_specs=[pl.BlockSpec(memory_space=pltpu.SMEM)] + [hbm] * 6,
        out_specs=hbm,
        scratch_shapes=[
            pltpu.VMEM((PHASES, shards, depth, 2 * HEAD_DIM), jnp.bfloat16),
            pltpu.VMEM((length, width), jnp.bfloat16),
            pltpu.VMEM((length, query_cols // 2), jnp.bfloat16),
            pltpu.VMEM((length, query_cols // 2), jnp.bfloat16),
            pltpu.VMEM((2 * GROUP, length, length), jnp.bfloat16),
            pltpu.VMEM((2 * GROUP, length, HEAD_DIM), jnp.float32),
            pltpu.VMEM((PHASES, length, 2 * HEAD_DIM), jnp.float32),
            pltpu.VMEM((2, length, HEAD_DIM), jnp.bfloat16),
            pltpu.VMEM((length, 2 * HEAD_DIM), jnp.bfloat16),
            pltpu.VMEM((length, length), jnp.float32),
            pltpu.VMEM((length, HEAD_DIM), jnp.float32),
            pltpu.VMEM((length, HEAD_DIM), jnp.float32),
            pltpu.VMEM((2, CHUNKS, rows // CHUNKS, 2 * depth if twins else HEAD_DIM), jnp.bfloat16),
            pltpu.VMEM((CHUNKS, 2, rows // CHUNKS, 2 * HEAD_DIM), SHARE_TYPE),
            pltpu.VMEM((CHUNKS, 2, rows // CHUNKS, 2 * HEAD_DIM), SHARE_TYPE),
            dma((6,)),
            dma((PHASES, shards, parts)),
            dma((sends if twins else PHASES * shards * 2,)),
            dma((3, CHUNKS)),
            dma((CHUNKS,)),
            dma((2,)),
            dma((2,)),
            dma((OUT_GROUPS,)),
            dma((OUT_GROUPS,)),
            dma((OUT_GROUPS,)),
        ],
        compiler_params=pltpu.CompilerParams(
            collective_id=0, has_side_effects=True, vmem_limit_bytes=56 * 1024 * 1024
        ),
    )(doc_start, normed, queries, key_weight, value_weight, jnp.asarray(cosine), jnp.asarray(sine))


def solution(mesh):
    placed = (
        P(("group", "fsdp"), "ctx", None),
        P(("group", "fsdp"), "ctx", None),
        P("fsdp", None),
        P("fsdp", None),
        P(("group", "fsdp")),
    )
    return jax.shard_map(
        functools.partial(body, mesh.shape["group"], mesh.shape["fsdp"]),
        mesh=mesh,
        in_specs=placed,
        out_specs=P(("group", "fsdp"), "ctx", None),
        check_vma=False,
    )
```

```python
import functools

import jax
import jax.numpy as jnp
import numpy as np
from jax import lax
from jax.experimental import pallas as pl
from jax.experimental.pallas import tpu as pltpu
from jax.sharding import PartitionSpec as P

HEAD_DIM = 128
GROUP = 8
THETA = 500000.0
MASKED = -1e30
MESH = pl.DeviceIdType.MESH
PHASES = 2
OUT_GROUPS = 4
PARTS = 8
WAIT = 4
DOUBLE = 8
CHUNKS = 4
ROWS, SHARES = 2, 3
SHARE_TYPE = jnp.bfloat16
SCHEDULE = (
    ("load", (0,), (), ()),
    ("begin", (), ((0, 0, 0, 0, 0), (10, 0, 0, 0, 0), (0, 0, 0, 0, 1), (8, 0, 0, 0, 2), (0, 0, 0, 0, 4)), ((8, 0, 0, 0, 0), (1, 0, 0, 0, 0), (10, 0, 0, 0, 0), (1, 0, 0, 0, 1), (2, 0, 0, 0, 2), (8, 0, 0, 0, 3), (9, 0, 0, 0, 3))),
    ("load", (1,), (), ()),
    ("clear", (), ((0, 1, 0, 0, 0), (10, 1, 0, 0, 0)), ()),
    ("queries", (), ((8, 0, 0, 0, 5), (0, 1, 0, 0, 4), (8, 1, 0, 0, 1), (4, 0, 1, 0, 0), (3, 0, 1, 0, 0), (2, 1, 0, 0, 2), (8, 1, 0, 0, 5), (12, 0, 0, 1, 0), (11, 0, 0, 1, 0), (4, 0, 1, 0, 1), (10, 0, 1, 0, 0), (3, 0, 1, 0, 1), (12, 0, 1, 0, 3), (2, 0, 1, 0, 3), (0, 1, 0, 0, 3), (12, 1, 0, 1, 0), (3, 1, 0, 1, 0), (4, 1, 0, 1, 2), (3, 1, 0, 1, 2), (12, 0, 2, 0, 0), (3, 0, 2, 0, 0), (10, 0, 2, 0, 0), (0, 1, 0, 0, 7), (12, 0, 1, 1, 0), (11, 0, 1, 1, 0), (4, 0, 1, 0, 2), (2, 0, 1, 0, 2), (10, 1, 0, 0, 3), (0, 2, 0, 0, 2), (12, 0, 3, 0, 0), (11, 0, 3, 0, 0), (12, 0, 2, 1, 0), (11, 0, 2, 1, 0), (0, 2, 0, 0, 0)), ((2, 0, 0, 0, 3), (4, 0, 1, 0, 0), (3, 0, 1, 0, 0), (4, 0, 1, 0, 1), (8, 0, 1, 0, 0), (0, 0, 0, 0, 2), (12, 0, 2, 0, 0), (3, 0, 2, 0, 0), (9, 0, 2, 0, 0), (10, 0, 2, 0, 0), (12, 0, 0, 1, 0), (11, 0, 0, 1, 0), (1, 0, 0, 0, 2), (4, 0, 0, 1, 2), (4, 0, 0, 1, 3), (11, 0, 0, 1, 2), (12, 0, 1, 0, 2), (8, 0, 1, 0, 2), (2, 0, 1, 0, 3), (10, 0, 1, 0, 1), (2, 0, 1, 0, 0), (12, 0, 2, 0, 3), (1, 0, 2, 0, 3), (12, 0, 2, 1, 0), (11, 0, 2, 1, 0), (12, 0, 3, 0, 0), (3, 0, 3, 0, 0), (8, 0, 0, 0, 5), (9, 0, 3, 0, 0), (4, 0, 2, 0, 2), (10, 0, 2, 0, 2), (1, 0, 2, 0, 4), (8, 1, 0, 0, 0), (4, 1, 1, 0, 0), (0, 1, 1, 0, 0), (12, 0, 3, 0, 2), (10, 0, 3, 0, 2), (10, 0, 3, 0, 0), (10, 1, 0, 0, 0), (0, 1, 0, 0, 2), (12, 0, 1, 1, 1), (4, 0, 1, 1, 3), (11, 0, 1, 1, 2), (1, 0, 2, 0, 2), (4, 0, 1, 0, 4), (12, 0, 1, 0, 5), (8, 0, 1, 0, 4), (9, 0, 3, 0, 2))),
    ("rotate", (0, 2), (), ()),
    ("rotate", (2, 2), ((2, 0, 3, 0, 1), (4, 0, 1, 1, 2), (4, 0, 1, 1, 3), (11, 0, 1, 1, 2), (2, 0, 3, 0, 0), (4, 0, 2, 0, 2), (4, 0, 2, 0, 3), (10, 0, 2, 0, 2), (0, 2, 0, 0, 1)), ((12, 0, 2, 1, 2), (11, 0, 2, 1, 2), (1, 0, 0, 0, 5))),
    ("rotate", (4, 2), (), ((10, 1, 0, 0, 2), (12, 1, 1, 0, 1), (8, 1, 1, 0, 1), (12, 1, 2, 0, 0), (1, 1, 2, 0, 0))),
    ("rotate", (6, 2), (), ()),
    ("rotate", (8, 2), ((0, 2, 0, 0, 3), (12, 0, 3, 0, 2), (10, 0, 3, 0, 2), (10, 0, 0, 0, 4), (4, 0, 3, 1, 0), (4, 0, 3, 1, 1), (11, 0, 3, 1, 0)), ((4, 0, 1, 1, 0), (11, 0, 1, 1, 0), (12, 0, 3, 1, 2), (11, 0, 3, 1, 2), (4, 1, 3, 0, 0), (1, 1, 3, 0, 0), (4, 1, 2, 0, 2), (9, 1, 2, 0, 1), (12, 0, 2, 0, 5), (9, 0, 2, 0, 5))),
    ("rotate", (10, 2), (), ()),
    ("rotate", (12, 2), (), ()),
    ("rotate", (14, 2), ((12, 0, 2, 1, 2), (11, 0, 2, 1, 2), (10, 0, 0, 0, 2), (4, 1, 2, 0, 0), (2, 1, 2, 0, 0), (12, 0, 3, 1, 2), (11, 0, 3, 1, 2), (12, 1, 2, 0, 1), (11, 1, 2, 0, 1), (3, 1, 0, 1, 1)), ((4, 1, 1, 0, 3), (4, 1, 1, 0, 4), (8, 1, 1, 0, 3), (0, 0, 1, 0, 6), (8, 1, 0, 0, 3), (10, 1, 1, 0, 0), (10, 1, 1, 0, 2), (12, 0, 3, 1, 0), (11, 0, 3, 1, 0))),
    ("normed", (), (), ()),
    ("add", (0, 0, 0), (), ()),
    ("add", (1, 0, 0), (), ()),
    ("add", (0, 1, 1), ((12, 0, 1, 1, 6), (12, 0, 1, 1, 4)), ((12, 0, 3, 0, 4), (9, 0, 3, 0, 4), (12, 0, 1, 1, 6), (12, 0, 1, 1, 4))),
    ("add", (0, 1, 0), ((4, 0, 1, 0, 7), (4, 0, 1, 0, 6), (4, 0, 1, 0, 5)), ((4, 0, 1, 0, 7),)),
    ("add", (0, 2, 1), ((12, 0, 2, 1, 6), (12, 0, 2, 1, 4)), ((12, 0, 2, 1, 6), (12, 0, 2, 1, 4))),
    ("add", (0, 0, 1), ((3, 1, 2, 0, 0), (10, 1, 2, 0, 1), (4, 1, 3, 0, 0), (2, 1, 3, 0, 0), (3, 1, 3, 0, 0), (12, 0, 0, 1, 2), (12, 0, 0, 1, 6), (12, 0, 0, 1, 4)), ((10, 1, 2, 0, 1), (12, 1, 0, 1, 0), (11, 1, 0, 1, 0), (4, 2, 1, 0, 2), (12, 1, 0, 1, 2), (11, 1, 0, 1, 2), (2, 1, 2, 0, 0), (12, 1, 3, 0, 1), (9, 1, 3, 0, 1), (12, 1, 3, 0, 3), (9, 1, 3, 0, 3), (12, 1, 1, 0, 5), (0, 1, 1, 0, 5), (8, 1, 0, 0, 5), (12, 0, 0, 1, 6), (12, 0, 0, 1, 4))),
    ("add", (0, 2, 0), ((4, 0, 2, 0, 4), (4, 0, 2, 0, 7), (12, 0, 2, 0, 5)), ((4, 0, 2, 0, 7),)),
    ("add", (0, 3, 0), ((12, 0, 3, 0, 4), (12, 0, 3, 0, 6)), ((4, 0, 3, 0, 6), (4, 0, 3, 0, 7))),
    ("add", (0, 3, 1), ((12, 0, 3, 1, 6), (12, 0, 3, 1, 4)), ((12, 0, 3, 1, 6), (12, 0, 3, 1, 4))),
    ("keys", (), (), ()),
    ("weigh", (0, 2), (), ()),
    ("weigh", (2, 2), ((12, 1, 3, 0, 1), (2, 1, 3, 0, 2), (4, 1, 2, 1, 0), (12, 1, 2, 1, 1), (11, 1, 2, 1, 0), (2, 1, 3, 0, 1), (3, 1, 2, 1, 2), (12, 1, 3, 0, 3), (2, 1, 3, 0, 3)), ((10, 1, 3, 0, 0), (12, 1, 1, 1, 0), (11, 1, 1, 1, 0), (12, 1, 2, 0, 3), (9, 1, 2, 0, 3), (4, 2, 1, 0, 0), (10, 1, 2, 0, 3), (10, 1, 3, 0, 2), (0, 1, 1, 0, 6), (12, 1, 1, 1, 2), (11, 1, 1, 1, 2))),
    ("weigh", (4, 2), (), ()),
    ("weigh", (6, 2), (), ()),
    ("weigh", (8, 2), ((4, 1, 3, 1, 2), (3, 1, 3, 1, 2), (4, 1, 3, 1, 0), (4, 1, 3, 1, 1), (11, 1, 3, 1, 0), (12, 1, 2, 0, 3), (10, 1, 2, 0, 3), (2, 1, 3, 0, 4)), ((12, 1, 0, 1, 6), (12, 1, 0, 1, 4), (1, 3, 0, 0, 2), (4, 2, 1, 0, 1), (12, 1, 2, 1, 1), (11, 1, 2, 1, 1), (4, 1, 2, 1, 0), (3, 1, 2, 1, 0), (4, 1, 3, 0, 5), (10, 1, 3, 0, 4), (4, 1, 3, 0, 6), (9, 1, 3, 0, 5), (0, 1, 0, 0, 7), (4, 1, 1, 0, 7), (0, 1, 1, 0, 7), (1, 3, 0, 0, 0))),
    ("weigh", (10, 2), (), ()),
    ("weigh", (12, 2), (), ()),
    ("weigh", (14, 2), (), ((12, 1, 3, 1, 0), (11, 1, 3, 1, 0), (1, 3, 0, 0, 1), (4, 2, 1, 0, 3))),
    ("add", (1, 1, 1), (), ((12, 1, 1, 1, 6), (12, 1, 1, 1, 4))),
    ("add", (1, 2, 0), ((4, 1, 2, 0, 7), (12, 1, 2, 0, 5)), ((1, 3, 0, 0, 3), (12, 1, 2, 0, 5), (4, 1, 2, 0, 7))),
    ("add", (1, 1, 0), (), ()),
    ("add", (1, 0, 1), ((12, 1, 0, 1, 3), (4, 1, 0, 1, 7), (4, 1, 0, 1, 6), (4, 1, 0, 1, 5)), ()),
    ("add", (1, 2, 1), ((12, 1, 2, 1, 3), (12, 1, 2, 1, 6), (4, 1, 2, 1, 5)), ((12, 1, 2, 1, 3), (4, 1, 2, 1, 7), (12, 1, 2, 1, 5))),
    ("add", (1, 3, 0), ((4, 1, 3, 0, 7), (12, 1, 3, 0, 5)), ((4, 1, 3, 0, 7),)),
    ("add", (1, 3, 1), ((4, 1, 3, 1, 3), (12, 1, 3, 1, 6), (4, 1, 3, 1, 4), (4, 1, 3, 1, 5)), ((12, 1, 3, 1, 2), (12, 1, 3, 1, 6), (12, 1, 3, 1, 4))),
    ("", (), ((4, 3, 1, 0, 0), (4, 3, 1, 0, 1), (4, 3, 1, 0, 2), (4, 3, 1, 0, 3)), ()),
    ("", (), (), ()),
)


def paired(groups, shards):
    return groups == 2 and shards == 8


def rotary_tables(length):
    half = HEAD_DIM // 2
    exponent = -np.arange(half, dtype=np.float32) * np.float32(2.0) / np.float32(HEAD_DIM)
    frequency = np.power(np.float32(THETA), exponent, dtype=np.float32)
    angles = np.arange(length, dtype=np.float32)[:, None] * frequency[None, :]
    cosine, sine = np.cos(angles).astype(np.float32), np.sin(angles).astype(np.float32)
    return np.concatenate([cosine, cosine], 1), np.concatenate([-sine, sine], 1)


def kernel(
    groups, shards, doc_ref, normed_ref, queries_ref, key_ref, value_ref, cos_hbm, sin_hbm, out_ref,
    wbuf, xbuf, qbuf, obuf, pbuf, inverse, acc, kbuf, vbuf, bias, cos_ref, sin_ref,
    guest, share_out, share_in, load_sem, recv_sem, send_sem, guest_sem, share_sem, pair_send, pair_recv, out_sem, out_send, out_recv,
):
    twins = paired(groups, shards)
    ny = 2 if twins else 1
    nz = shards // ny
    parts = PARTS if twins else 1
    g, f, c = lax.axis_index("group"), lax.axis_index("fsdp"), lax.axis_index("ctx")
    z, y = f // ny, f % ny
    own_rows, depth = normed_ref.shape[1], key_ref.shape[0]
    length = 2 * own_rows
    piece_rows = depth // parts
    half_cols = queries_ref.shape[2] // 2
    pair = (g, f, 1 - c)
    up, down = (g, f + ny, c), (g, f - ny, c)
    if twins:
        y_dev, x_dev = (g, z * 2 + 1 - y, c), (1 - g, f, c)

    def shard(zs, ys):
        return zs * ny + ys

    def part(j, count=1):
        return g * (parts - count) + j * (1 - 2 * g) if twins else 0

    def copy(h, s, q, send_sem, device, count=1):
        ref = wbuf.at[h, s, pl.ds(pl.multiple_of(q * piece_rows, piece_rows), count * piece_rows), :]
        return pltpu.make_async_remote_copy(
            src_ref=ref, dst_ref=ref, send_sem=send_sem, recv_sem=recv_sem.at[h, s, q],
            device_id=device, device_id_type=MESH,
        )

    middle = (z + 1) // 2 % 2
    inward = 1 - 2 * (z // 2)

    def place(k, o):
        zs = z if k == 0 else z + inward * (k - middle * (2 if k == 1 else 1))
        return shard(zs, 1 - y if o else y)

    def wait_piece(h, s, j, count=1):
        q = part(j, count)
        copy(h, s, q, recv_sem.at[h, s, q], pair, count).wait_recv()

    chunk = own_rows // CHUNKS

    def remote(source, target, send_sem, recv_sem, device):
        return pltpu.make_async_remote_copy(
            src_ref=source, dst_ref=target, send_sem=send_sem, recv_sem=recv_sem, device_id=device, device_id_type=MESH,
        )

    def send(index, move):
        code, h, k, o, j = move
        link, count = code % DOUBLE, code // DOUBLE + 1
        near, far = (g, f + inward * ny, c), (g, f - inward * ny, c)
        device = near if link == 0 else far if link == 1 else y_dev if link == 2 else x_dev
        done = send_sem.at[index]
        if h == ROWS:
            start = pl.multiple_of((z + inward) * ny * depth, ny * depth)
            source = normed_ref.at[0, pl.ds(j * chunk, chunk), pl.ds(start, ny * depth)]
            return remote(source, guest.at[c, j], done, guest_sem.at[0, j], device)
        if h == SHARES:
            return remote(share_out.at[j], share_in.at[j], done, share_sem.at[j], device)
        return copy(h, place(k, o), part(j, count), done, device, count)

    def pass_guest(j):
        ref = guest.at[c, j]
        return remote(ref, ref, guest_sem.at[1, j], guest_sem.at[2, j], pair)

    def arrive(h, k, o, j, count):
        if h == ROWS:
            remote(guest.at[c, j], guest.at[c, j], guest_sem.at[1, j], guest_sem.at[0, j], pair).wait_recv()
            pass_guest(j).start()
        elif h == SHARES:
            remote(share_in.at[j], share_in.at[j], share_sem.at[j], share_sem.at[j], pair).wait_recv()
        else:
            wait_piece(h, place(k, o), j, count)

    def make_share(j):
        pass_guest(j).wait_recv()
        for side in range(2):
            total = jnp.zeros((chunk, 2 * HEAD_DIM), jnp.float32)
            for ys in range(ny):
                total += jnp.dot(
                    guest[side, j, :, ys * depth:(ys + 1) * depth], wbuf[1, shard(z, ys)],
                    preferred_element_type=jnp.float32,
                )
            share_out[j, side] = total.astype(SHARE_TYPE)

    def finish_values():
        vbuf[...] = acc[1].astype(jnp.bfloat16)

        if twins:
            @pl.when(middle == 0)
            def _():
                for j in range(CHUNKS):
                    for side in range(2):
                        rows = slice(side * own_rows + j * chunk, side * own_rows + (j + 1) * chunk)
                        vbuf[rows, :] = (acc[1, rows, :] + share_in[j, side].astype(jnp.float32)).astype(jnp.bfloat16)

    def z_copy(h, zs, way):
        return copy(h, zs, 0, send_sem.at[(h * nz + zs) * 2 + way], up if way == 0 else down)

    head_cols = pl.ds(pl.multiple_of(c * 2 * HEAD_DIM, 2 * HEAD_DIM), 2 * HEAD_DIM)
    weight_loads = [
        pltpu.make_async_copy(ref.at[:, head_cols], wbuf.at[h, f], load_sem.at[h])
        for h, ref in enumerate((key_ref, value_ref))
    ]
    own = pl.ds(pl.multiple_of(c * own_rows, own_rows), own_rows)
    other = pl.ds(pl.multiple_of((1 - c) * own_rows, own_rows), own_rows)
    my_cols = pl.ds(pl.multiple_of(c * half_cols, half_cols), half_cols)
    other_cols = pl.ds(pl.multiple_of((1 - c) * half_cols, half_cols), half_cols)
    other_loads = [
        pltpu.make_async_copy(normed_ref.at[0], xbuf.at[own, :], load_sem.at[2]),
        pltpu.make_async_copy(queries_ref.at[0, :, my_cols], qbuf.at[own, :], load_sem.at[3]),
        pltpu.make_async_copy(cos_hbm, cos_ref, load_sem.at[4]),
        pltpu.make_async_copy(sin_hbm, sin_ref, load_sem.at[5]),
    ]
    for load in weight_loads:
        load.start()

    barrier = pltpu.get_barrier_semaphore()
    pl.semaphore_signal(barrier, inc=1, device_id=pair, device_id_type=MESH)
    if twins:
        pl.semaphore_signal(barrier, inc=1, device_id=y_dev, device_id_type=MESH)
        pl.semaphore_signal(barrier, inc=1, device_id=x_dev, device_id_type=MESH)

    @pl.when(z < nz - 1)
    def _():
        pl.semaphore_signal(barrier, inc=1, device_id=up, device_id_type=MESH)

    @pl.when(z > 0)
    def _():
        pl.semaphore_signal(barrier, inc=1, device_id=down, device_id_type=MESH)

    line_peers = jnp.where(z > 0, 1, 0) + jnp.where(z < nz - 1, 1, 0)
    pl.semaphore_wait(barrier, (3 if twins else 1) + line_peers)

    def send_own(h):
        weight_loads[h].wait()

        @pl.when(z < nz - 1)
        def _():
            z_copy(h, z, 0).start()

        @pl.when(z > 0)
        def _():
            z_copy(h, z, 1).start()

    def each_way(d, action):
        @pl.when(z - d >= 0)
        def _():
            action(z - d, 0)

        @pl.when(z + d < nz)
        def _():
            action(z + d, 1)

    def passes_on(way):
        return z < nz - 1 if way == 0 else z > 0

    def forward_z(h, d):
        def one(zs, way):
            wait_piece(h, zs, 0)

            @pl.when(passes_on(way))
            def _():
                z_copy(h, zs, way).start()

        each_way(d, one)

    def drain_sends(h, d):
        def one(zs, way):
            @pl.when(passes_on(way))
            def _():
                z_copy(h, zs, way).wait_send()

        each_way(d, one)

    def drain_own(h):
        @pl.when(z < nz - 1)
        def _():
            z_copy(h, z, 0).wait_send()

        @pl.when(z > 0)
        def _():
            z_copy(h, z, 1).wait_send()

    def add_shard(h, s):
        columns = pl.ds(pl.multiple_of(s * depth, depth), depth)

        def tile(t, carry):
            rows = pl.ds(pl.multiple_of(t * 256, 256), 256)
            acc[h, rows, :] += jnp.dot(xbuf[rows, columns], wbuf[h, s], preferred_element_type=jnp.float32)
            return carry

        lax.fori_loop(0, length // 256, tile, 0)

    def add_same(h, d):
        each_way(d, lambda zs, way: add_shard(h, zs))

    def rotated(u, rows):
        return (u * cos_ref[rows, :] + pltpu.roll(u, HEAD_DIM // 2, 1) * sin_ref[rows, :]).astype(jnp.bfloat16)

    def wait_queries():
        for load in other_loads[1:]:
            load.wait()
        query_copy.wait_recv()

    def rotate_queries(first, count):
        def head(i, carry):
            cols = pl.ds(pl.multiple_of(i * HEAD_DIM, HEAD_DIM), HEAD_DIM)

            def tile(t, carry):
                rows = pl.ds(pl.multiple_of(t * 128, 128), 128)
                qbuf[rows, cols] = rotated(qbuf[rows, cols].astype(jnp.float32), rows)
                return carry

            return lax.fori_loop(0, length // 128, tile, carry)

        lax.fori_loop(first, first + count, head, 0)

    def make_bias():
        first = doc_ref[0]
        row = lax.broadcasted_iota(jnp.int32, (length, length), 0)
        col = lax.broadcasted_iota(jnp.int32, (length, length), 1)
        visible = (col <= row) & ((col >= first) | (row < first))
        bias[...] = jnp.where(visible, 0.0, MASKED)

    def finish_keys():
        def tile(t, carry):
            rows = pl.ds(pl.multiple_of(t * 128, 128), 128)
            for h in range(2):
                kbuf[h, rows, :] = rotated(acc[0, rows, h * HEAD_DIM:(h + 1) * HEAD_DIM], rows)
            return carry

        lax.fori_loop(0, length // 128, tile, 0)

    factor = HEAD_DIM ** -0.5 * 1.4426950408889634

    def weigh(first, count):
        h = first // GROUP

        def head(i, carry):
            cols = pl.ds(pl.multiple_of(i * HEAD_DIM, HEAD_DIM), HEAD_DIM)
            for block in range(2):
                rows = slice(block * own_rows, (block + 1) * own_rows)
                keys = (block + 1) * own_rows
                scores = lax.dot_general(
                    qbuf[rows, cols], kbuf[h, :keys, :], (((1,), (1,)), ((), ())),
                    preferred_element_type=jnp.float32,
                ) * factor + bias[rows, :keys]
                probs = jnp.exp2(scores - jnp.max(scores, axis=1, keepdims=True))
                total = jnp.sum(probs, axis=1, keepdims=True)
                pbuf[i, rows, :keys] = probs.astype(jnp.bfloat16)
                inverse[i, rows, :] = jnp.broadcast_to(1.0 / total, (own_rows, HEAD_DIM))
            return carry

        lax.fori_loop(first, first + count, head, 0)

    def mix(first, count):
        h = first // GROUP

        def head(i, carry):
            cols = pl.ds(pl.multiple_of(i * HEAD_DIM, HEAD_DIM), HEAD_DIM)
            for block in range(2):
                rows = slice(block * own_rows, (block + 1) * own_rows)
                keys = (block + 1) * own_rows
                mixed = jnp.dot(
                    pbuf[i, rows, :keys], vbuf[:keys, h * HEAD_DIM:(h + 1) * HEAD_DIM],
                    preferred_element_type=jnp.float32,
                )
                obuf[rows, cols] = (mixed * inverse[i, rows, :]).astype(jnp.bfloat16)
            return carry

        lax.fori_loop(first, first + count, head, 0, unroll=count)

    def out_copies(h):
        width = half_cols // OUT_GROUPS
        source = pl.ds(h * width, width)
        target = out_ref.at[0, :, pl.ds(pl.multiple_of(c * half_cols + h * width, width), width)]
        return (
            pltpu.make_async_copy(obuf.at[own, source], target, out_sem.at[h]),
            pltpu.make_async_remote_copy(
                src_ref=obuf.at[other, source], dst_ref=target, send_sem=out_send.at[h],
                recv_sem=out_recv.at[h], device_id=pair, device_id_type=MESH,
            ),
        )

    def send_out(h):
        for one in out_copies(h):
            one.start()

    query_copy = pltpu.make_async_remote_copy(
        src_ref=queries_ref.at[0, :, other_cols], dst_ref=qbuf.at[own, :], send_sem=pair_send.at[0],
        recv_sem=pair_recv.at[0], device_id=pair, device_id_type=MESH,
    )
    normed_copy = pltpu.make_async_remote_copy(
        src_ref=normed_ref.at[0], dst_ref=xbuf.at[own, :], send_sem=pair_send.at[1],
        recv_sem=pair_recv.at[1], device_id=pair, device_id_type=MESH,
    )

    def begin():
        for load in other_loads:
            load.start()
        query_copy.start()
        normed_copy.start()

    def clear():
        acc[...] = jnp.zeros_like(acc)
        make_bias()

    def wait_normed():
        other_loads[0].wait()
        normed_copy.wait_recv()

    def add_place(h, k, o):
        if h == 1 and k == 1:
            pl.when(middle == 1)(lambda: add_shard(h, place(k, o)))
        else:
            add_shard(h, place(k, o))

    if twins:
        steps = {
            "load": lambda h: weight_loads[h].wait(),
            "begin": begin,
            "clear": clear,
            "queries": wait_queries,
            "rotate": rotate_queries,
            "normed": wait_normed,
            "add": add_place,
            "keys": finish_keys,
            "weigh": weigh,
        }
        sent = [0, 0]
        for name, operands, *moves in SCHEDULE:
            for role in range(2):
                @pl.when(middle == role)
                def _(role=role):
                    for move in moves[role]:
                        code, h, k, o, j = move
                        if code % DOUBLE == WAIT:
                            arrive(h, k, o, j, code // DOUBLE + 1)
                        else:
                            if h == SHARES:
                                make_share(j)
                            send(sent[role], move).start()
                            sent[role] += 1
            if name:
                steps[name](*operands)
    else:
        send_own(0)
        begin()
        clear()
        wait_queries()
        rotate_queries(0, half_cols // HEAD_DIM)
        send_own(1)
        wait_normed()
        for h in range(PHASES):
            add_shard(h, f)

            def step(d, carry, h=h):
                forward_z(h, d)
                add_same(h, d)
                return carry

            lax.fori_loop(1, nz, step, 0)
            if h == 0:
                finish_keys()
                weigh(0, 8)
                weigh(8, 8)
    finish_values()
    heads = 2 * GROUP // OUT_GROUPS
    for group in range(OUT_GROUPS):
        mix(group * heads, heads)
        send_out(group)

    if twins:
        for role in range(2):
            @pl.when(middle == role)
            def _(role=role):
                moves = [move for step in SCHEDULE for move in step[2 + role] if move[0] % DOUBLE < WAIT]
                for index, move in enumerate(moves):
                    send(index, move).wait_send()
                if role == 1:
                    for j in range(CHUNKS):
                        pass_guest(j).wait_send()
    else:
        for h in range(PHASES):
            drain_own(h)

            def drain(d, carry, h=h):
                drain_sends(h, d)
                return carry

            lax.fori_loop(1, nz, drain, 0)
    query_copy.wait_send()
    normed_copy.wait_send()
    for group in range(OUT_GROUPS):
        local, remote = out_copies(group)
        local.wait()
        remote.wait()


def body(groups, shards, normed, queries, key_weight, value_weight, doc_start):
    _, rows, width = normed.shape
    depth = key_weight.shape[0]
    query_cols = queries.shape[2]
    length = 2 * rows
    twins = paired(groups, shards)
    parts = PARTS if twins else 1
    sends = max(sum(move[0] % DOUBLE < WAIT for step in SCHEDULE for move in step[role]) for role in (2, 3))
    cosine, sine = rotary_tables(length)
    dma = pltpu.SemaphoreType.DMA
    hbm = pl.BlockSpec(memory_space=pl.ANY)
    return pl.pallas_call(
        functools.partial(kernel, groups, shards),
        out_shape=jax.ShapeDtypeStruct((1, rows, query_cols), jnp.bfloat16),
        in_specs=[pl.BlockSpec(memory_space=pltpu.SMEM)] + [hbm] * 6,
        out_specs=hbm,
        scratch_shapes=[
            pltpu.VMEM((PHASES, shards, depth, 2 * HEAD_DIM), jnp.bfloat16),
            pltpu.VMEM((length, width), jnp.bfloat16),
            pltpu.VMEM((length, query_cols // 2), jnp.bfloat16),
            pltpu.VMEM((length, query_cols // 2), jnp.bfloat16),
            pltpu.VMEM((2 * GROUP, length, length), jnp.bfloat16),
            pltpu.VMEM((2 * GROUP, length, HEAD_DIM), jnp.float32),
            pltpu.VMEM((PHASES, length, 2 * HEAD_DIM), jnp.float32),
            pltpu.VMEM((2, length, HEAD_DIM), jnp.bfloat16),
            pltpu.VMEM((length, 2 * HEAD_DIM), jnp.bfloat16),
            pltpu.VMEM((length, length), jnp.float32),
            pltpu.VMEM((length, HEAD_DIM), jnp.float32),
            pltpu.VMEM((length, HEAD_DIM), jnp.float32),
            pltpu.VMEM((2, CHUNKS, rows // CHUNKS, 2 * depth if twins else HEAD_DIM), jnp.bfloat16),
            pltpu.VMEM((CHUNKS, 2, rows // CHUNKS, 2 * HEAD_DIM), SHARE_TYPE),
            pltpu.VMEM((CHUNKS, 2, rows // CHUNKS, 2 * HEAD_DIM), SHARE_TYPE),
            dma((6,)),
            dma((PHASES, shards, parts)),
            dma((sends if twins else PHASES * shards * 2,)),
            dma((3, CHUNKS)),
            dma((CHUNKS,)),
            dma((2,)),
            dma((2,)),
            dma((OUT_GROUPS,)),
            dma((OUT_GROUPS,)),
            dma((OUT_GROUPS,)),
        ],
        compiler_params=pltpu.CompilerParams(
            collective_id=0, has_side_effects=True, vmem_limit_bytes=56 * 1024 * 1024
        ),
    )(doc_start, normed, queries, key_weight, value_weight, jnp.asarray(cosine), jnp.asarray(sine))


def solution(mesh):
    placed = (
        P(("group", "fsdp"), "ctx", None),
        P(("group", "fsdp"), "ctx", None),
        P("fsdp", None),
        P("fsdp", None),
        P(("group", "fsdp")),
    )
    return jax.shard_map(
        functools.partial(body, mesh.shape["group"], mesh.shape["fsdp"]),
        mesh=mesh,
        in_specs=placed,
        out_specs=P(("group", "fsdp"), "ctx", None),
        check_vma=False,
    )
```

```python
import functools

import jax
import jax.numpy as jnp
import numpy as np
from jax import lax
from jax.experimental import pallas as pl
from jax.experimental.pallas import tpu as pltpu
from jax.sharding import PartitionSpec as P

HEAD_DIM = 128
GROUP = 8
THETA = 500000.0
MASKED = -1e30
MESH = pl.DeviceIdType.MESH
PHASES = 2
OUT_GROUPS = 4
PARTS = 8
WAIT = 4
DOUBLE = 8
CHUNKS = 4
ROWS, SHARES = 2, 3
SHARE_TYPE = jnp.bfloat16
SCHEDULE = (
    ("load", (0,), (), ()),
    ("begin", (), ((0, 0, 0, 0, 0), (10, 0, 0, 0, 0), (0, 0, 0, 0, 1), (8, 0, 0, 0, 2), (0, 0, 0, 0, 4)), ((8, 0, 0, 0, 0), (1, 0, 0, 0, 0), (10, 0, 0, 0, 0), (1, 0, 0, 0, 1), (2, 0, 0, 0, 2), (8, 0, 0, 0, 3), (9, 0, 0, 0, 3))),
    ("load", (1,), (), ()),
    ("clear", (), ((0, 1, 0, 0, 0), (10, 1, 0, 0, 0)), ()),
    ("queries", (), ((8, 0, 0, 0, 5), (0, 1, 0, 0, 4), (8, 1, 0, 0, 1), (4, 0, 1, 0, 0), (3, 0, 1, 0, 0), (2, 1, 0, 0, 2), (8, 1, 0, 0, 5), (12, 0, 0, 1, 0), (11, 0, 0, 1, 0), (4, 0, 1, 0, 1), (10, 0, 1, 0, 0), (3, 0, 1, 0, 1), (12, 0, 1, 0, 3), (2, 0, 1, 0, 3), (0, 1, 0, 0, 3), (12, 1, 0, 1, 0), (3, 1, 0, 1, 0), (4, 1, 0, 1, 2), (3, 1, 0, 1, 2), (12, 0, 2, 0, 0), (3, 0, 2, 0, 0), (10, 0, 2, 0, 0), (0, 1, 0, 0, 7), (12, 0, 1, 1, 0), (11, 0, 1, 1, 0), (4, 0, 1, 0, 2), (2, 0, 1, 0, 2), (10, 1, 0, 0, 3), (0, 2, 0, 0, 2), (12, 0, 3, 0, 0), (11, 0, 3, 0, 0), (12, 0, 2, 1, 0), (11, 0, 2, 1, 0), (0, 2, 0, 0, 0)), ((2, 0, 0, 0, 3), (4, 0, 1, 0, 0), (3, 0, 1, 0, 0), (4, 0, 1, 0, 1), (8, 0, 1, 0, 0), (0, 0, 0, 0, 2), (12, 0, 2, 0, 0), (3, 0, 2, 0, 0), (9, 0, 2, 0, 0), (10, 0, 2, 0, 0), (12, 0, 0, 1, 0), (11, 0, 0, 1, 0), (1, 0, 0, 0, 2), (4, 0, 0, 1, 2), (4, 0, 0, 1, 3), (11, 0, 0, 1, 2), (12, 0, 1, 0, 2), (8, 0, 1, 0, 2), (2, 0, 1, 0, 3), (10, 0, 1, 0, 1), (2, 0, 1, 0, 0), (12, 0, 2, 0, 3), (1, 0, 2, 0, 3), (12, 0, 2, 1, 0), (11, 0, 2, 1, 0), (12, 0, 3, 0, 0), (3, 0, 3, 0, 0), (8, 0, 0, 0, 5), (9, 0, 3, 0, 0), (4, 0, 2, 0, 2), (10, 0, 2, 0, 2), (1, 0, 2, 0, 4), (8, 1, 0, 0, 0), (4, 1, 1, 0, 0), (0, 1, 1, 0, 0), (12, 0, 3, 0, 2), (10, 0, 3, 0, 2), (10, 0, 3, 0, 0), (10, 1, 0, 0, 0), (0, 1, 0, 0, 2), (12, 0, 1, 1, 1), (4, 0, 1, 1, 3), (11, 0, 1, 1, 2), (1, 0, 2, 0, 2), (4, 0, 1, 0, 4), (12, 0, 1, 0, 5), (8, 0, 1, 0, 4), (9, 0, 3, 0, 2))),
    ("rotate", (0, 2), (), ()),
    ("rotate", (2, 2), ((2, 0, 3, 0, 1), (4, 0, 1, 1, 2), (4, 0, 1, 1, 3), (11, 0, 1, 1, 2), (2, 0, 3, 0, 0), (4, 0, 2, 0, 2), (4, 0, 2, 0, 3), (10, 0, 2, 0, 2), (0, 2, 0, 0, 1)), ((12, 0, 2, 1, 2), (11, 0, 2, 1, 2), (1, 0, 0, 0, 5))),
    ("rotate", (4, 2), (), ((10, 1, 0, 0, 2), (12, 1, 1, 0, 1), (8, 1, 1, 0, 1), (12, 1, 2, 0, 0), (1, 1, 2, 0, 0))),
    ("rotate", (6, 2), (), ()),
    ("rotate", (8, 2), ((0, 2, 0, 0, 3), (12, 0, 3, 0, 2), (10, 0, 3, 0, 2), (10, 0, 0, 0, 4), (4, 0, 3, 1, 0), (4, 0, 3, 1, 1), (11, 0, 3, 1, 0)), ((4, 0, 1, 1, 0), (11, 0, 1, 1, 0), (12, 0, 3, 1, 2), (11, 0, 3, 1, 2), (4, 1, 3, 0, 0), (1, 1, 3, 0, 0), (4, 1, 2, 0, 2), (9, 1, 2, 0, 1), (12, 0, 2, 0, 5), (9, 0, 2, 0, 5))),
    ("rotate", (10, 2), (), ()),
    ("rotate", (12, 2), (), ()),
    ("rotate", (14, 2), ((12, 0, 2, 1, 2), (11, 0, 2, 1, 2), (10, 0, 0, 0, 2), (4, 1, 2, 0, 0), (2, 1, 2, 0, 0), (12, 0, 3, 1, 2), (11, 0, 3, 1, 2), (12, 1, 2, 0, 1), (11, 1, 2, 0, 1), (3, 1, 0, 1, 1)), ((4, 1, 1, 0, 3), (4, 1, 1, 0, 4), (8, 1, 1, 0, 3), (0, 0, 1, 0, 6), (8, 1, 0, 0, 3), (10, 1, 1, 0, 0), (10, 1, 1, 0, 2), (12, 0, 3, 1, 0), (11, 0, 3, 1, 0))),
    ("normed", (), (), ()),
    ("add", (0, 0, 0), (), ()),
    ("add", (1, 0, 0), (), ()),
    ("add", (0, 1, 1), ((12, 0, 1, 1, 6), (12, 0, 1, 1, 4)), ((12, 0, 3, 0, 4), (9, 0, 3, 0, 4), (12, 0, 1, 1, 6), (12, 0, 1, 1, 4))),
    ("add", (0, 1, 0), ((4, 0, 1, 0, 7), (4, 0, 1, 0, 6), (4, 0, 1, 0, 5)), ((4, 0, 1, 0, 7),)),
    ("add", (0, 2, 1), ((12, 0, 2, 1, 6), (12, 0, 2, 1, 4)), ((12, 0, 2, 1, 6), (12, 0, 2, 1, 4))),
    ("add", (0, 0, 1), ((3, 1, 2, 0, 0), (10, 1, 2, 0, 1), (4, 1, 3, 0, 0), (2, 1, 3, 0, 0), (3, 1, 3, 0, 0), (12, 0, 0, 1, 2), (12, 0, 0, 1, 6), (12, 0, 0, 1, 4)), ((10, 1, 2, 0, 1), (12, 1, 0, 1, 0), (11, 1, 0, 1, 0), (4, 2, 1, 0, 2), (12, 1, 0, 1, 2), (11, 1, 0, 1, 2), (2, 1, 2, 0, 0), (12, 1, 3, 0, 1), (9, 1, 3, 0, 1), (12, 1, 3, 0, 3), (9, 1, 3, 0, 3), (12, 1, 1, 0, 5), (0, 1, 1, 0, 5), (8, 1, 0, 0, 5), (12, 0, 0, 1, 6), (12, 0, 0, 1, 4))),
    ("add", (0, 2, 0), ((4, 0, 2, 0, 4), (4, 0, 2, 0, 7), (12, 0, 2, 0, 5)), ((4, 0, 2, 0, 7),)),
    ("add", (0, 3, 0), ((12, 0, 3, 0, 4), (12, 0, 3, 0, 6)), ((4, 0, 3, 0, 6), (4, 0, 3, 0, 7))),
    ("add", (0, 3, 1), ((12, 0, 3, 1, 6), (12, 0, 3, 1, 4)), ((12, 0, 3, 1, 6), (12, 0, 3, 1, 4))),
    ("keys", (), (), ()),
    ("weigh", (0, 2), (), ()),
    ("weigh", (2, 2), ((12, 1, 3, 0, 1), (2, 1, 3, 0, 2), (4, 1, 2, 1, 0), (12, 1, 2, 1, 1), (11, 1, 2, 1, 0), (2, 1, 3, 0, 1), (3, 1, 2, 1, 2), (12, 1, 3, 0, 3), (2, 1, 3, 0, 3)), ((10, 1, 3, 0, 0), (12, 1, 1, 1, 0), (11, 1, 1, 1, 0), (12, 1, 2, 0, 3), (9, 1, 2, 0, 3), (4, 2, 1, 0, 0), (10, 1, 2, 0, 3), (10, 1, 3, 0, 2), (0, 1, 1, 0, 6), (12, 1, 1, 1, 2), (11, 1, 1, 1, 2))),
    ("weigh", (4, 2), (), ()),
    ("weigh", (6, 2), (), ()),
    ("weigh", (8, 2), ((4, 1, 3, 1, 2), (3, 1, 3, 1, 2), (4, 1, 3, 1, 0), (4, 1, 3, 1, 1), (11, 1, 3, 1, 0), (12, 1, 2, 0, 3), (10, 1, 2, 0, 3), (2, 1, 3, 0, 4)), ((12, 1, 0, 1, 6), (12, 1, 0, 1, 4), (1, 3, 0, 0, 2), (4, 2, 1, 0, 1), (12, 1, 2, 1, 1), (11, 1, 2, 1, 1), (4, 1, 2, 1, 0), (3, 1, 2, 1, 0), (4, 1, 3, 0, 5), (10, 1, 3, 0, 4), (4, 1, 3, 0, 6), (9, 1, 3, 0, 5), (0, 1, 0, 0, 7), (4, 1, 1, 0, 7), (0, 1, 1, 0, 7), (1, 3, 0, 0, 0))),
    ("weigh", (10, 2), (), ()),
    ("weigh", (12, 2), (), ()),
    ("weigh", (14, 2), (), ((12, 1, 3, 1, 0), (11, 1, 3, 1, 0), (1, 3, 0, 0, 1), (4, 2, 1, 0, 3))),
    ("add", (1, 1, 1), (), ((12, 1, 1, 1, 6), (12, 1, 1, 1, 4))),
    ("add", (1, 2, 0), ((4, 1, 2, 0, 7), (12, 1, 2, 0, 5)), ((1, 3, 0, 0, 3), (12, 1, 2, 0, 5), (4, 1, 2, 0, 7))),
    ("add", (1, 1, 0), (), ()),
    ("add", (1, 0, 1), ((12, 1, 0, 1, 3), (4, 1, 0, 1, 7), (4, 1, 0, 1, 6), (4, 1, 0, 1, 5)), ()),
    ("add", (1, 2, 1), ((12, 1, 2, 1, 3), (12, 1, 2, 1, 6), (4, 1, 2, 1, 5)), ((12, 1, 2, 1, 3), (4, 1, 2, 1, 7), (12, 1, 2, 1, 5))),
    ("add", (1, 3, 0), ((4, 1, 3, 0, 7), (12, 1, 3, 0, 5)), ((4, 1, 3, 0, 7),)),
    ("half", (1, 3, 1, 0), ((4, 1, 3, 1, 3),), ((12, 1, 3, 1, 2),)),
    ("half", (1, 3, 1, 1), ((12, 1, 3, 1, 6), (4, 1, 3, 1, 4), (4, 1, 3, 1, 5)), ((12, 1, 3, 1, 6), (12, 1, 3, 1, 4))),
    ("", (), ((4, 3, 1, 0, 0), (4, 3, 1, 0, 1), (4, 3, 1, 0, 2), (4, 3, 1, 0, 3)), ()),
    ("", (), (), ()),
)


def paired(groups, shards):
    return groups == 2 and shards == 8


def rotary_tables(length):
    half = HEAD_DIM // 2
    exponent = -np.arange(half, dtype=np.float32) * np.float32(2.0) / np.float32(HEAD_DIM)
    frequency = np.power(np.float32(THETA), exponent, dtype=np.float32)
    angles = np.arange(length, dtype=np.float32)[:, None] * frequency[None, :]
    cosine, sine = np.cos(angles).astype(np.float32), np.sin(angles).astype(np.float32)
    return np.concatenate([cosine, cosine], 1), np.concatenate([-sine, sine], 1)


def kernel(
    groups, shards, doc_ref, normed_ref, queries_ref, key_ref, value_ref, cos_hbm, sin_hbm, out_ref,
    wbuf, xbuf, qbuf, obuf, pbuf, inverse, acc, kbuf, vbuf, bias, cos_ref, sin_ref,
    guest, share_out, share_in, load_sem, recv_sem, send_sem, guest_sem, share_sem, pair_send, pair_recv, out_sem, out_send, out_recv,
):
    twins = paired(groups, shards)
    ny = 2 if twins else 1
    nz = shards // ny
    parts = PARTS if twins else 1
    g, f, c = lax.axis_index("group"), lax.axis_index("fsdp"), lax.axis_index("ctx")
    z, y = f // ny, f % ny
    own_rows, depth = normed_ref.shape[1], key_ref.shape[0]
    length = 2 * own_rows
    piece_rows = depth // parts
    half_cols = queries_ref.shape[2] // 2
    pair = (g, f, 1 - c)
    up, down = (g, f + ny, c), (g, f - ny, c)
    if twins:
        y_dev, x_dev = (g, z * 2 + 1 - y, c), (1 - g, f, c)

    def shard(zs, ys):
        return zs * ny + ys

    def part(j, count=1):
        return g * (parts - count) + j * (1 - 2 * g) if twins else 0

    def copy(h, s, q, send_sem, device, count=1):
        ref = wbuf.at[h, s, pl.ds(pl.multiple_of(q * piece_rows, piece_rows), count * piece_rows), :]
        return pltpu.make_async_remote_copy(
            src_ref=ref, dst_ref=ref, send_sem=send_sem, recv_sem=recv_sem.at[h, s, q],
            device_id=device, device_id_type=MESH,
        )

    middle = (z + 1) // 2 % 2
    inward = 1 - 2 * (z // 2)

    def place(k, o):
        zs = z if k == 0 else z + inward * (k - middle * (2 if k == 1 else 1))
        return shard(zs, 1 - y if o else y)

    def wait_piece(h, s, j, count=1):
        q = part(j, count)
        copy(h, s, q, recv_sem.at[h, s, q], pair, count).wait_recv()

    chunk = own_rows // CHUNKS

    def remote(source, target, send_sem, recv_sem, device):
        return pltpu.make_async_remote_copy(
            src_ref=source, dst_ref=target, send_sem=send_sem, recv_sem=recv_sem, device_id=device, device_id_type=MESH,
        )

    def send(index, move):
        code, h, k, o, j = move
        link, count = code % DOUBLE, code // DOUBLE + 1
        near, far = (g, f + inward * ny, c), (g, f - inward * ny, c)
        device = near if link == 0 else far if link == 1 else y_dev if link == 2 else x_dev
        done = send_sem.at[index]
        if h == ROWS:
            start = pl.multiple_of((z + inward) * ny * depth, ny * depth)
            source = normed_ref.at[0, pl.ds(j * chunk, chunk), pl.ds(start, ny * depth)]
            return remote(source, guest.at[c, j], done, guest_sem.at[0, j], device)
        if h == SHARES:
            return remote(share_out.at[j], share_in.at[j], done, share_sem.at[j], device)
        return copy(h, place(k, o), part(j, count), done, device, count)

    def pass_guest(j):
        ref = guest.at[c, j]
        return remote(ref, ref, guest_sem.at[1, j], guest_sem.at[2, j], pair)

    def arrive(h, k, o, j, count):
        if h == ROWS:
            remote(guest.at[c, j], guest.at[c, j], guest_sem.at[1, j], guest_sem.at[0, j], pair).wait_recv()
            pass_guest(j).start()
        elif h == SHARES:
            remote(share_in.at[j], share_in.at[j], share_sem.at[j], share_sem.at[j], pair).wait_recv()
        else:
            wait_piece(h, place(k, o), j, count)

    def make_share(j):
        pass_guest(j).wait_recv()
        for side in range(2):
            total = jnp.zeros((chunk, 2 * HEAD_DIM), jnp.float32)
            for ys in range(ny):
                total += jnp.dot(
                    guest[side, j, :, ys * depth:(ys + 1) * depth], wbuf[1, shard(z, ys)],
                    preferred_element_type=jnp.float32,
                )
            share_out[j, side] = total.astype(SHARE_TYPE)

    def finish_values():
        vbuf[...] = acc[1].astype(jnp.bfloat16)

        if twins:
            @pl.when(middle == 0)
            def _():
                for j in range(CHUNKS):
                    for side in range(2):
                        rows = slice(side * own_rows + j * chunk, side * own_rows + (j + 1) * chunk)
                        vbuf[rows, :] = (acc[1, rows, :] + share_in[j, side].astype(jnp.float32)).astype(jnp.bfloat16)

    def z_copy(h, zs, way):
        return copy(h, zs, 0, send_sem.at[(h * nz + zs) * 2 + way], up if way == 0 else down)

    head_cols = pl.ds(pl.multiple_of(c * 2 * HEAD_DIM, 2 * HEAD_DIM), 2 * HEAD_DIM)
    weight_loads = [
        pltpu.make_async_copy(ref.at[:, head_cols], wbuf.at[h, f], load_sem.at[h])
        for h, ref in enumerate((key_ref, value_ref))
    ]
    own = pl.ds(pl.multiple_of(c * own_rows, own_rows), own_rows)
    other = pl.ds(pl.multiple_of((1 - c) * own_rows, own_rows), own_rows)
    my_cols = pl.ds(pl.multiple_of(c * half_cols, half_cols), half_cols)
    other_cols = pl.ds(pl.multiple_of((1 - c) * half_cols, half_cols), half_cols)
    other_loads = [
        pltpu.make_async_copy(normed_ref.at[0], xbuf.at[own, :], load_sem.at[2]),
        pltpu.make_async_copy(queries_ref.at[0, :, my_cols], qbuf.at[own, :], load_sem.at[3]),
        pltpu.make_async_copy(cos_hbm, cos_ref, load_sem.at[4]),
        pltpu.make_async_copy(sin_hbm, sin_ref, load_sem.at[5]),
    ]
    for load in weight_loads:
        load.start()

    barrier = pltpu.get_barrier_semaphore()
    pl.semaphore_signal(barrier, inc=1, device_id=pair, device_id_type=MESH)
    if twins:
        pl.semaphore_signal(barrier, inc=1, device_id=y_dev, device_id_type=MESH)
        pl.semaphore_signal(barrier, inc=1, device_id=x_dev, device_id_type=MESH)

    @pl.when(z < nz - 1)
    def _():
        pl.semaphore_signal(barrier, inc=1, device_id=up, device_id_type=MESH)

    @pl.when(z > 0)
    def _():
        pl.semaphore_signal(barrier, inc=1, device_id=down, device_id_type=MESH)

    line_peers = jnp.where(z > 0, 1, 0) + jnp.where(z < nz - 1, 1, 0)
    pl.semaphore_wait(barrier, (3 if twins else 1) + line_peers)

    def send_own(h):
        weight_loads[h].wait()

        @pl.when(z < nz - 1)
        def _():
            z_copy(h, z, 0).start()

        @pl.when(z > 0)
        def _():
            z_copy(h, z, 1).start()

    def each_way(d, action):
        @pl.when(z - d >= 0)
        def _():
            action(z - d, 0)

        @pl.when(z + d < nz)
        def _():
            action(z + d, 1)

    def passes_on(way):
        return z < nz - 1 if way == 0 else z > 0

    def forward_z(h, d):
        def one(zs, way):
            wait_piece(h, zs, 0)

            @pl.when(passes_on(way))
            def _():
                z_copy(h, zs, way).start()

        each_way(d, one)

    def drain_sends(h, d):
        def one(zs, way):
            @pl.when(passes_on(way))
            def _():
                z_copy(h, zs, way).wait_send()

        each_way(d, one)

    def drain_own(h):
        @pl.when(z < nz - 1)
        def _():
            z_copy(h, z, 0).wait_send()

        @pl.when(z > 0)
        def _():
            z_copy(h, z, 1).wait_send()

    def add_shard(h, s):
        columns = pl.ds(pl.multiple_of(s * depth, depth), depth)

        def tile(t, carry):
            rows = pl.ds(pl.multiple_of(t * 256, 256), 256)
            acc[h, rows, :] += jnp.dot(xbuf[rows, columns], wbuf[h, s], preferred_element_type=jnp.float32)
            return carry

        lax.fori_loop(0, length // 256, tile, 0)

    def add_same(h, d):
        each_way(d, lambda zs, way: add_shard(h, zs))

    def rotated(u, rows):
        return (u * cos_ref[rows, :] + pltpu.roll(u, HEAD_DIM // 2, 1) * sin_ref[rows, :]).astype(jnp.bfloat16)

    def wait_queries():
        for load in other_loads[1:]:
            load.wait()
        query_copy.wait_recv()

    def rotate_queries(first, count):
        def head(i, carry):
            cols = pl.ds(pl.multiple_of(i * HEAD_DIM, HEAD_DIM), HEAD_DIM)

            def tile(t, carry):
                rows = pl.ds(pl.multiple_of(t * 128, 128), 128)
                qbuf[rows, cols] = rotated(qbuf[rows, cols].astype(jnp.float32), rows)
                return carry

            return lax.fori_loop(0, length // 128, tile, carry)

        lax.fori_loop(first, first + count, head, 0)

    def make_bias():
        first = doc_ref[0]
        row = lax.broadcasted_iota(jnp.int32, (length, length), 0)
        col = lax.broadcasted_iota(jnp.int32, (length, length), 1)
        visible = (col <= row) & ((col >= first) | (row < first))
        bias[...] = jnp.where(visible, 0.0, MASKED)

    def finish_keys():
        def tile(t, carry):
            rows = pl.ds(pl.multiple_of(t * 128, 128), 128)
            for h in range(2):
                kbuf[h, rows, :] = rotated(acc[0, rows, h * HEAD_DIM:(h + 1) * HEAD_DIM], rows)
            return carry

        lax.fori_loop(0, length // 128, tile, 0)

    factor = HEAD_DIM ** -0.5 * 1.4426950408889634

    def weigh(first, count):
        h = first // GROUP

        def head(i, carry):
            cols = pl.ds(pl.multiple_of(i * HEAD_DIM, HEAD_DIM), HEAD_DIM)
            for block in range(2):
                rows = slice(block * own_rows, (block + 1) * own_rows)
                keys = (block + 1) * own_rows
                scores = lax.dot_general(
                    qbuf[rows, cols], kbuf[h, :keys, :], (((1,), (1,)), ((), ())),
                    preferred_element_type=jnp.float32,
                ) * factor + bias[rows, :keys]
                probs = jnp.exp2(scores - jnp.max(scores, axis=1, keepdims=True))
                total = jnp.sum(probs, axis=1, keepdims=True)
                pbuf[i, rows, :keys] = probs.astype(jnp.bfloat16)
                inverse[i, rows, :] = jnp.broadcast_to(1.0 / total, (own_rows, HEAD_DIM))
            return carry

        lax.fori_loop(first, first + count, head, 0)

    def mix(first, count):
        h = first // GROUP

        def head(i, carry):
            cols = pl.ds(pl.multiple_of(i * HEAD_DIM, HEAD_DIM), HEAD_DIM)
            for block in range(2):
                rows = slice(block * own_rows, (block + 1) * own_rows)
                keys = (block + 1) * own_rows
                mixed = jnp.dot(
                    pbuf[i, rows, :keys], vbuf[:keys, h * HEAD_DIM:(h + 1) * HEAD_DIM],
                    preferred_element_type=jnp.float32,
                )
                obuf[rows, cols] = (mixed * inverse[i, rows, :]).astype(jnp.bfloat16)
            return carry

        lax.fori_loop(first, first + count, head, 0, unroll=count)

    def out_copies(h):
        width = half_cols // OUT_GROUPS
        source = pl.ds(h * width, width)
        target = out_ref.at[0, :, pl.ds(pl.multiple_of(c * half_cols + h * width, width), width)]
        return (
            pltpu.make_async_copy(obuf.at[own, source], target, out_sem.at[h]),
            pltpu.make_async_remote_copy(
                src_ref=obuf.at[other, source], dst_ref=target, send_sem=out_send.at[h],
                recv_sem=out_recv.at[h], device_id=pair, device_id_type=MESH,
            ),
        )

    def send_out(h):
        for one in out_copies(h):
            one.start()

    query_copy = pltpu.make_async_remote_copy(
        src_ref=queries_ref.at[0, :, other_cols], dst_ref=qbuf.at[own, :], send_sem=pair_send.at[0],
        recv_sem=pair_recv.at[0], device_id=pair, device_id_type=MESH,
    )
    normed_copy = pltpu.make_async_remote_copy(
        src_ref=normed_ref.at[0], dst_ref=xbuf.at[own, :], send_sem=pair_send.at[1],
        recv_sem=pair_recv.at[1], device_id=pair, device_id_type=MESH,
    )

    def begin():
        for load in other_loads:
            load.start()
        query_copy.start()
        normed_copy.start()

    def clear():
        acc[...] = jnp.zeros_like(acc)
        make_bias()

    def wait_normed():
        other_loads[0].wait()
        normed_copy.wait_recv()

    def add_half(h, k, o, side):
        s = place(k, o)
        base = pl.multiple_of(part(side * parts // 2, parts // 2) * piece_rows, depth // 2)
        columns = pl.ds(pl.multiple_of(s * depth + base, depth // 2), depth // 2)
        for t in range(length // 256):
            rows = slice(t * 256, (t + 1) * 256)
            acc[h, rows, :] += jnp.dot(
                xbuf[rows, columns], wbuf[h, s, pl.ds(base, depth // 2), :], preferred_element_type=jnp.float32
            )

    def add_place(h, k, o):
        if h == 1 and k == 1:
            pl.when(middle == 1)(lambda: add_shard(h, place(k, o)))
        else:
            add_shard(h, place(k, o))

    if twins:
        steps = {
            "load": lambda h: weight_loads[h].wait(),
            "begin": begin,
            "clear": clear,
            "queries": wait_queries,
            "rotate": rotate_queries,
            "normed": wait_normed,
            "add": add_place,
            "half": add_half,
            "keys": finish_keys,
            "weigh": weigh,
        }
        sent = [0, 0]
        for name, operands, *moves in SCHEDULE:
            for role in range(2):
                @pl.when(middle == role)
                def _(role=role):
                    for move in moves[role]:
                        code, h, k, o, j = move
                        if code % DOUBLE == WAIT:
                            arrive(h, k, o, j, code // DOUBLE + 1)
                        else:
                            if h == SHARES:
                                make_share(j)
                            send(sent[role], move).start()
                            sent[role] += 1
            if name:
                steps[name](*operands)
    else:
        send_own(0)
        begin()
        clear()
        wait_queries()
        rotate_queries(0, half_cols // HEAD_DIM)
        send_own(1)
        wait_normed()
        for h in range(PHASES):
            add_shard(h, f)

            def step(d, carry, h=h):
                forward_z(h, d)
                add_same(h, d)
                return carry

            lax.fori_loop(1, nz, step, 0)
            if h == 0:
                finish_keys()
                weigh(0, 8)
                weigh(8, 8)
    finish_values()
    heads = 2 * GROUP // OUT_GROUPS
    for group in range(OUT_GROUPS):
        mix(group * heads, heads)
        send_out(group)

    if twins:
        for role in range(2):
            @pl.when(middle == role)
            def _(role=role):
                moves = [move for step in SCHEDULE for move in step[2 + role] if move[0] % DOUBLE < WAIT]
                for index, move in enumerate(moves):
                    send(index, move).wait_send()
                if role == 1:
                    for j in range(CHUNKS):
                        pass_guest(j).wait_send()
    else:
        for h in range(PHASES):
            drain_own(h)

            def drain(d, carry, h=h):
                drain_sends(h, d)
                return carry

            lax.fori_loop(1, nz, drain, 0)
    query_copy.wait_send()
    normed_copy.wait_send()
    for group in range(OUT_GROUPS):
        local, remote = out_copies(group)
        local.wait()
        remote.wait()


def body(groups, shards, normed, queries, key_weight, value_weight, doc_start):
    _, rows, width = normed.shape
    depth = key_weight.shape[0]
    query_cols = queries.shape[2]
    length = 2 * rows
    twins = paired(groups, shards)
    parts = PARTS if twins else 1
    sends = max(sum(move[0] % DOUBLE < WAIT for step in SCHEDULE for move in step[role]) for role in (2, 3))
    cosine, sine = rotary_tables(length)
    dma = pltpu.SemaphoreType.DMA
    hbm = pl.BlockSpec(memory_space=pl.ANY)
    return pl.pallas_call(
        functools.partial(kernel, groups, shards),
        out_shape=jax.ShapeDtypeStruct((1, rows, query_cols), jnp.bfloat16),
        in_specs=[pl.BlockSpec(memory_space=pltpu.SMEM)] + [hbm] * 6,
        out_specs=hbm,
        scratch_shapes=[
            pltpu.VMEM((PHASES, shards, depth, 2 * HEAD_DIM), jnp.bfloat16),
            pltpu.VMEM((length, width), jnp.bfloat16),
            pltpu.VMEM((length, query_cols // 2), jnp.bfloat16),
            pltpu.VMEM((length, query_cols // 2), jnp.bfloat16),
            pltpu.VMEM((2 * GROUP, length, length), jnp.bfloat16),
            pltpu.VMEM((2 * GROUP, length, HEAD_DIM), jnp.float32),
            pltpu.VMEM((PHASES, length, 2 * HEAD_DIM), jnp.float32),
            pltpu.VMEM((2, length, HEAD_DIM), jnp.bfloat16),
            pltpu.VMEM((length, 2 * HEAD_DIM), jnp.bfloat16),
            pltpu.VMEM((length, length), jnp.float32),
            pltpu.VMEM((length, HEAD_DIM), jnp.float32),
            pltpu.VMEM((length, HEAD_DIM), jnp.float32),
            pltpu.VMEM((2, CHUNKS, rows // CHUNKS, 2 * depth if twins else HEAD_DIM), jnp.bfloat16),
            pltpu.VMEM((CHUNKS, 2, rows // CHUNKS, 2 * HEAD_DIM), SHARE_TYPE),
            pltpu.VMEM((CHUNKS, 2, rows // CHUNKS, 2 * HEAD_DIM), SHARE_TYPE),
            dma((6,)),
            dma((PHASES, shards, parts)),
            dma((sends if twins else PHASES * shards * 2,)),
            dma((3, CHUNKS)),
            dma((CHUNKS,)),
            dma((2,)),
            dma((2,)),
            dma((OUT_GROUPS,)),
            dma((OUT_GROUPS,)),
            dma((OUT_GROUPS,)),
        ],
        compiler_params=pltpu.CompilerParams(
            collective_id=0, has_side_effects=True, vmem_limit_bytes=56 * 1024 * 1024
        ),
    )(doc_start, normed, queries, key_weight, value_weight, jnp.asarray(cosine), jnp.asarray(sine))


def solution(mesh):
    placed = (
        P(("group", "fsdp"), "ctx", None),
        P(("group", "fsdp"), "ctx", None),
        P("fsdp", None),
        P("fsdp", None),
        P(("group", "fsdp")),
    )
    return jax.shard_map(
        functools.partial(body, mesh.shape["group"], mesh.shape["fsdp"]),
        mesh=mesh,
        in_specs=placed,
        out_specs=P(("group", "fsdp"), "ctx", None),
        check_vma=False,
    )
```
